32 devices in a mesh: dp: 16 (over z, y, x), tensor: 2 (over core).
Axes of the slice: x: 2, y: 2, z: 4, core: 2. Of those that a mesh axis runs over, the one named last changes fastest.
Arguments:
- tokens: bfloat16 [16384, 768], P(('dp', 'tensor')), may hold values from -6 to 6
- cotangent: bfloat16 [16384, 768], P(('dp', 'tensor')), may hold values from -6 to 6
- gain_attn: float32 [768], replicated, may hold values from 0.5 to 1.5
- gain_ffn: float32 [768], replicated, may hold values from 0.5 to 1.5
- route_query: float32 [768], replicated, may hold values from -0.21875 to 0.21875
- route_key: float32 [768], replicated, may hold values from -0.21875 to 0.21875
- route_ffn: float32 [768], replicated, may hold values from -0.21875 to 0.21875
- light_query: bfloat16 [768, 512], P(None, 'tensor'), may hold values from -0.21875 to 0.21875
- light_key: bfloat16 [768, 512], P(None, 'tensor'), may hold values from -0.21875 to 0.21875
- light_value: bfloat16 [768, 512], P(None, 'tensor'), may hold values from -0.21875 to 0.21875
- light_out: bfloat16 [512, 768], P('tensor'), may hold values from -1 to 1
- heavy_query: bfloat16 [768, 768], P(None, 'tensor'), may hold values from -0.21875 to 0.21875
- heavy_key: bfloat16 [768, 768], P(None, 'tensor'), may hold values from -0.21875 to 0.21875
- heavy_value: bfloat16 [768, 768], P(None, 'tensor'), may hold values from -0.21875 to 0.21875
- heavy_out: bfloat16 [768, 768], P('tensor'), may hold values from -1.25 to 1.25
- light_gate: bfloat16 [768, 1024], P(None, 'tensor'), may hold values from -0.21875 to 0.21875
- light_up: bfloat16 [768, 1024], P(None, 'tensor'), may hold values from -0.21875 to 0.21875
- light_down: bfloat16 [1024, 768], P('tensor'), may hold values from -0.25 to 0.25
- heavy_gate: bfloat16 [768, 4096], P(None, 'tensor'), may hold values from -0.21875 to 0.21875
- heavy_up: bfloat16 [768, 4096], P(None, 'tensor'), may hold values from -0.21875 to 0.21875
- heavy_down: bfloat16 [4096, 768], P('tensor'), may hold values from -0.1875 to 0.1875
- query_index: int32 [16, 128], P('dp'), may hold values from 0 to 1023, as said below
- key_index: int32 [16, 128], P('dp'), may hold values from 0 to 1023, as said below
- ffn_index: int32 [16, 128], P('dp'), may hold values from 0 to 1023, as said below
Outputs:
- block_out: bfloat16 [16384, 768], P(('dp', 'tensor'))
- input_grad: bfloat16 [16384, 768], P(('dp', 'tensor'))
- gain_attn_grad: float32 [768], replicated
- gain_ffn_grad: float32 [768], replicated
- route_query_grad: float32 [768], replicated
- route_key_grad: float32 [768], replicated
- route_ffn_grad: float32 [768], replicated
- light_query_grad: float32 [768, 512], P('dp', 'tensor')
- light_key_grad: float32 [768, 512], P('dp', 'tensor')
- light_value_grad: float32 [768, 512], P('dp', 'tensor')
- light_out_grad: float32 [512, 768], P('tensor', 'dp')
- heavy_query_grad: float32 [768, 768], P('dp', 'tensor')
- heavy_key_grad: float32 [768, 768], P('dp', 'tensor')
- heavy_value_grad: float32 [768, 768], P('dp', 'tensor')
- heavy_out_grad: float32 [768, 768], P('tensor', 'dp')
- light_gate_grad: float32 [768, 1024], P('dp', 'tensor')
- light_up_grad: float32 [768, 1024], P('dp', 'tensor')
- light_down_grad: float32 [1024, 768], P('tensor', 'dp')
- heavy_gate_grad: float32 [768, 4096], P('dp', 'tensor')
- heavy_up_grad: float32 [768, 4096], P('dp', 'tensor')
- heavy_down_grad: float32 [4096, 768], P('tensor', 'dp')
The draws below stay inside these ranges and needn't reach their ends.
Inputs may be any that keep to these rules, and one draw needn't show every extreme that they name: `query_index`: row s lists 128 different positions of sequence s. `key_index`: row s lists 128 different positions of sequence s. `ffn_index`: row s lists 128 different positions of sequence s.
All inputs are finite; a program needn't handle non-finite values.
Results may differ from the reference program's by a relative error of at most 0.018.
Values may be sent and summed in bfloat16 or wider, within the bound.
No kernel may reach another device: no remote copies, remote signals or barrier semaphores. Data moves between devices by JAX's collectives and lax.ppermute only.
A program may use at most 192 MiB of HBM per device.

```python
import jax
import jax.numpy as jnp
from jax import lax

D = 768
HEAD_DIM = 64
LIGHT_HEADS = 8
HEAVY_HEADS = 12
LIGHT_FF = 1024
HEAVY_FF = 4096
WINDOW = 128
SEQ_LEN = 1024
SEQS = 1
ROUTED = 128
TOKENS = 16384


def pick_positions(key):
    row_keys = jax.random.split(key, TOKENS // SEQ_LEN)

    def one_row(row_key):
        return jax.random.permutation(row_key, SEQ_LEN)[:ROUTED]
    return jax.vmap(one_row)(row_keys).astype(jnp.int32)


def draw_query_index(key, part):
    return pick_positions(jax.random.fold_in(key, 11))


def draw_key_index(key, part):
    return pick_positions(jax.random.fold_in(key, 23))


def draw_ffn_index(key, part):
    return pick_positions(jax.random.fold_in(key, 37))


def strengthened(entries, key, source, target, parts, factor):
    def block_of(axis_at):
        return (jnp.arange(entries.shape[axis_at]) // (entries.shape[axis_at] // parts)).reshape((-1,) + (1,) * (entries.ndim - 1 - axis_at))

    first = jax.random.permutation(key, parts)[block_of(target)]
    far = (block_of(target) + parts // 2) % parts
    return jnp.where((block_of(source) == first) | (block_of(source) == far), factor * entries, entries)


def steps_of(own_key, shape, shards, least, high):
    loudness = 1.0
    for dim, blocks in shards:
        draws = jax.random.uniform(jax.random.fold_in(jax.random.fold_in(own_key, 6), dim), (blocks,), jnp.float32, least / len(shards), high / len(shards))
        loudness = loudness * jnp.repeat(jnp.exp(draws), shape[dim] // blocks).reshape((-1,) + (1,) * (len(shape) - 1 - dim))
    return loudness


def normal_values(stream_key, shape, spread, most, cuts=(), kind=jnp.bfloat16):
    values = spread * jax.random.normal(stream_key, shape, jnp.float32)
    if cuts:
        values = values * steps_of(stream_key, shape, cuts, -0.22, 0.18)
    return jnp.clip(values, -most, most).astype(kind)


def heavy_noise(rng, extent, width, reach, cuts, heavy, kind=jnp.bfloat16):
    drawn = width * jax.random.normal(rng, extent, jnp.float32)
    if cuts:
        drawn = drawn * steps_of(rng, extent, cuts, -0.22, 0.18)
    return jnp.clip(strengthened(drawn, jax.random.fold_in(rng, 3), *heavy), -reach, reach).astype(kind)


def setup_inputs(seed: int = 0) -> dict:
    seeds = jax.random.split(jax.random.key(seed), 25)
    return {
        "tokens": normal_values(seeds[0], (TOKENS, D), 1.0, 6.0, ((0, 32),)),
        "cotangent": heavy_noise(seeds[1], (TOKENS, D), 1.0, 6.0, ((0, 32),), (0, 1, 32, 2.75)),
        "gain_attn": jnp.clip(1.0 + 0.1 * jax.random.normal(seeds[2], (D,), jnp.float32), 0.5, 1.5),
        "gain_ffn": jnp.clip(1.0 + 0.1 * jax.random.normal(seeds[3], (D,), jnp.float32), 0.5, 1.5),
        "route_query": normal_values(seeds[4], (D,), D ** -0.5, 0.21875, (), jnp.float32),
        "route_key": normal_values(seeds[5], (D,), D ** -0.5, 0.21875, (), jnp.float32),
        "route_ffn": normal_values(seeds[6], (D,), D ** -0.5, 0.21875, (), jnp.float32),
        "light_query": normal_values(seeds[7], (D, LIGHT_HEADS * HEAD_DIM), D ** -0.5, 0.21875, ((1, 2),)),
        "light_key": normal_values(seeds[8], (D, LIGHT_HEADS * HEAD_DIM), D ** -0.5, 0.21875, ((1, 2),)),
        "light_value": normal_values(seeds[9], (D, LIGHT_HEADS * HEAD_DIM), D ** -0.5, 0.21875, ((1, 2),)),
        "light_out": normal_values(seeds[10], (LIGHT_HEADS * HEAD_DIM, D), (LIGHT_HEADS * HEAD_DIM // 16) ** -0.5, 1.0, ((0, 2),)),
        "heavy_query": normal_values(seeds[11], (D, HEAVY_HEADS * HEAD_DIM), D ** -0.5, 0.21875, ((1, 2),)),
        "heavy_key": normal_values(seeds[12], (D, HEAVY_HEADS * HEAD_DIM), D ** -0.5, 0.21875, ((1, 2),)),
        "heavy_value": normal_values(seeds[13], (D, HEAVY_HEADS * HEAD_DIM), D ** -0.5, 0.21875, ((1, 2),)),
        "heavy_out": normal_values(seeds[14], (HEAVY_HEADS * HEAD_DIM, D), (HEAVY_HEADS * HEAD_DIM // 32) ** -0.5, 1.25, ((0, 2),)),
        "light_gate": normal_values(seeds[15], (D, LIGHT_FF), D ** -0.5, 0.21875, ((1, 2),)),
        "light_up": normal_values(seeds[16], (D, LIGHT_FF), D ** -0.5, 0.21875, ((1, 2),)),
        "light_down": normal_values(seeds[17], (LIGHT_FF, D), (LIGHT_FF // 2) ** -0.5, 0.25, ((0, 2),)),
        "heavy_gate": normal_values(seeds[18], (D, HEAVY_FF), D ** -0.5, 0.21875, ((1, 2),)),
        "heavy_up": normal_values(seeds[19], (D, HEAVY_FF), D ** -0.5, 0.21875, ((1, 2),)),
        "heavy_down": normal_values(seeds[20], (HEAVY_FF, D), (HEAVY_FF // 4) ** -0.5, 0.1875, ((0, 2),)),
        "query_index": draw_query_index(jax.random.fold_in(seeds[24], 71), 0),
        "key_index": draw_key_index(jax.random.fold_in(seeds[24], 71), 0),
        "ffn_index": draw_ffn_index(jax.random.fold_in(seeds[24], 71), 0),
    }


@jax.custom_vjp
def low(v):
    return lax.optimization_barrier(v.astype(jnp.bfloat16)).astype(jnp.float32)

@jax.custom_vjp
def low_back(v):
    return v

def low_keep(v):
    return (low(v), None)

def low_pass(kept, grad):
    return (grad,)

def back_keep(v):
    return (v, None)

def back_low(kept, grad):
    return (low(grad),)
low.defvjp(low_keep, low_pass)
low_back.defvjp(back_keep, back_low)

def precise_dot(left, right):
    return jnp.dot(left, right, precision=lax.Precision.HIGHEST, preferred_element_type=jnp.float32)

def rms_scale(values, gain):
    return values * lax.rsqrt(lax.optimization_barrier(jnp.mean(values * values, axis=-1, keepdims=True)) + 1e-06) * gain

def both_round(values):
    return low(low_back(values))

def geglu_mix(gate_part, up_part):
    return jax.nn.gelu(gate_part, approximate=False) * up_part

def local_attention(queries, key_rows, value_rows):
    length = queries.shape[0]
    block_rows = min(512, length)
    scaling = HEAD_DIM ** (-0.5)
    padded_keys = jnp.pad(key_rows, ((WINDOW, WINDOW), (0, 0), (0, 0)))
    padded_values = jnp.pad(value_rows, ((WINDOW, WINDOW), (0, 0), (0, 0)))

    def one_block(block_index):
        offset = (block_index * block_rows).astype(jnp.int32)
        query_block = lax.dynamic_slice_in_dim(queries, offset, block_rows, 0)
        key_block = lax.dynamic_slice_in_dim(padded_keys, offset, block_rows + 2 * WINDOW, 0)
        value_block = lax.dynamic_slice_in_dim(padded_values, offset, block_rows + 2 * WINDOW, 0)
        scores = low_back(jnp.einsum('qhd,khd->hqk', query_block, key_block, precision=lax.Precision.HIGHEST) * scaling)
        query_place = offset + jnp.arange(block_rows, dtype=jnp.int32)
        key_place = offset - WINDOW + jnp.arange(block_rows + 2 * WINDOW, dtype=jnp.int32)
        allowed = (jnp.abs(query_place[:, None] - key_place[None, :]) < WINDOW) & ((key_place >= 0) & (key_place < length))[None, :]
        scores = jnp.where(allowed[None], scores, -1e+30)
        weights = jax.nn.softmax(scores, axis=-1)
        return jnp.einsum('hqk,khd->qhd', low(weights), value_block, precision=lax.Precision.HIGHEST)
    blocks = lax.map(jax.checkpoint(one_block), jnp.arange(length // block_rows, dtype=jnp.int32))
    return blocks.reshape(queries.shape)

def sequence_forward(params, residual, query_index, key_index, ffn_index):
    gain_attn, gain_ffn, route_query, route_key, route_ffn, light_query, light_key, light_value, light_out, heavy_query, heavy_key, heavy_value, heavy_out, light_gate, light_up, light_down, heavy_gate, heavy_up, heavy_down = params
    length = residual.shape[0]
    scaling = HEAD_DIM ** (-0.5)
    positions = jnp.arange(length, dtype=jnp.int32)
    attn_input = low(rms_scale(residual, gain_attn))
    query_light = both_round(precise_dot(attn_input, light_query)).reshape(length, -1, HEAD_DIM)
    key_light = both_round(precise_dot(attn_input, light_key)).reshape(length, -1, HEAD_DIM)
    value_light = both_round(precise_dot(attn_input, light_value)).reshape(length, -1, HEAD_DIM)
    light_result = both_round(local_attention(query_light, key_light, value_light).reshape(length, -1))
    query_pick = (query_index[:, None] == positions[None, :]).astype(jnp.float32)
    key_pick = (key_index[:, None] == positions[None, :]).astype(jnp.float32)
    query_rows = precise_dot(query_pick, attn_input)
    key_raw = precise_dot(key_pick, attn_input)
    query_score = jax.nn.sigmoid(precise_dot(query_rows, route_query))
    key_score = jax.nn.sigmoid(precise_dot(key_raw, route_key))
    key_rows = low(key_score[:, None] * key_raw)
    routed = query_rows.shape[0]
    query_heavy = both_round(precise_dot(query_rows, heavy_query)).reshape(routed, -1, HEAD_DIM)
    key_heavy = both_round(precise_dot(key_rows, heavy_key)).reshape(routed, -1, HEAD_DIM)
    value_heavy = both_round(precise_dot(key_rows, heavy_value)).reshape(routed, -1, HEAD_DIM)
    heavy_scores = low_back(jnp.einsum('qhd,khd->hqk', query_heavy, key_heavy, precision=lax.Precision.HIGHEST) * scaling)
    heavy_probs = jax.nn.softmax(heavy_scores, axis=-1)
    heavy_raw = jnp.einsum('hqk,khd->qhd', low(heavy_probs), value_heavy, precision=lax.Precision.HIGHEST).reshape(routed, -1)
    heavy_result = both_round(query_score[:, None] * heavy_raw)
    attn_branch = precise_dot(light_result, light_out) + precise_dot(query_pick.T, precise_dot(heavy_result, heavy_out))
    middle = residual + low_back(attn_branch)
    ffn_input = low(rms_scale(middle, gain_ffn))
    gate_light = low_back(precise_dot(ffn_input, light_gate))
    up_light = low_back(precise_dot(ffn_input, light_up))
    act_light = low(geglu_mix(gate_light, up_light))
    ffn_pick = (ffn_index[:, None] == positions[None, :]).astype(jnp.float32)
    ffn_rows = precise_dot(ffn_pick, ffn_input)
    ffn_score = jax.nn.sigmoid(precise_dot(ffn_rows, route_ffn))
    gate_heavy = low_back(precise_dot(ffn_rows, heavy_gate))
    up_heavy = low_back(precise_dot(ffn_rows, heavy_up))
    act_heavy = low(ffn_score[:, None] * geglu_mix(gate_heavy, up_heavy))
    ffn_branch = precise_dot(act_light, light_down) + precise_dot(ffn_pick.T, precise_dot(act_heavy, heavy_down))
    return middle + low_back(ffn_branch)

def reference(tokens, cotangent, gain_attn, gain_ffn, route_query, route_key, route_ffn, light_query, light_key, light_value, light_out, heavy_query, heavy_key, heavy_value, heavy_out, light_gate, light_up, light_down, heavy_gate, heavy_up, heavy_down, query_index, key_index, ffn_index):
    params = tuple((item.astype(jnp.float32) for item in (gain_attn, gain_ffn, route_query, route_key, route_ffn, light_query, light_key, light_value, light_out, heavy_query, heavy_key, heavy_value, heavy_out, light_gate, light_up, light_down, heavy_gate, heavy_up, heavy_down)))
    groups = query_index.shape[0] // SEQS
    residual = tokens.astype(jnp.float32).reshape(groups, SEQS, SEQ_LEN, D)
    grads = cotangent.astype(jnp.float32).reshape(groups, SEQS, SEQ_LEN, D)
    query_groups = query_index.reshape(groups, SEQS, -1)
    key_groups = key_index.reshape(groups, SEQS, -1)
    ffn_groups = ffn_index.reshape(groups, SEQS, -1)

    def one_group(totals, item):
        resid_group, grad_group, query_part, key_part, ffn_part = item

        def group_forward(weights, values):
            return jax.vmap(sequence_forward, in_axes=(None, 0, 0, 0, 0))(weights, values, query_part, key_part, ffn_part)
        result, pull = jax.vjp(group_forward, params, resid_group)
        weight_grads, resid_grad = pull(grad_group)
        totals = tuple((first + second for first, second in zip(totals, weight_grads)))
        return (totals, (result, resid_grad))
    start_totals = tuple((jnp.zeros_like(item) for item in params))
    totals, (results, resid_grads) = lax.scan(one_group, start_totals, (residual, grads, query_groups, key_groups, ffn_groups))
    return (results.reshape(-1, D).astype(jnp.bfloat16), resid_grads.reshape(-1, D).astype(jnp.bfloat16), totals[0], totals[1], totals[2], totals[3], totals[4], totals[5], totals[6], totals[7], totals[8], totals[9], totals[10], totals[11], totals[12], totals[13], totals[14], totals[15], totals[16], totals[17], totals[18])
```

```python
import jax
import jax.numpy as jnp
from jax import lax
from jax.sharding import PartitionSpec as P

HEAD_DIM = 64
WINDOW = 128


def rms_scale(values, gain):
    return values * lax.rsqrt(jnp.mean(values * values, axis=-1, keepdims=True) + 1e-06) * gain


def geglu_mix(gate_part, up_part):
    return jax.nn.gelu(gate_part, approximate=False) * up_part


def matmul(left, right):
    return jnp.dot(left, right, preferred_element_type=jnp.float32)


def matmul_tn(left, right):
    return lax.dot_general(
        left, right, (((0,), (0,)), ((), ())), preferred_element_type=jnp.float32
    )


def matmul_nt(left, right):
    return lax.dot_general(
        left, right, (((1,), (1,)), ((), ())), preferred_element_type=jnp.float32
    )


def precise_vec(left, right):
    return jnp.dot(left, right, precision=lax.Precision.HIGHEST, preferred_element_type=jnp.float32)


def pick_matrix(index_rows, length):
    return (index_rows[:, :, None] == jnp.arange(length, dtype=jnp.int32)[None, None, :]).astype(
        jnp.bfloat16
    )


def pick_rows(picker, data, length):
    width = data.shape[1]
    picked = jnp.einsum(
        "gnq,gqm->gnm",
        picker,
        data.reshape(picker.shape[0], length, width),
        preferred_element_type=jnp.float32,
    )
    return picked.reshape(-1, width)


def spread_rows(places, values, row_total):
    return jnp.zeros((row_total, values.shape[1]), jnp.float32).at[places].add(values)


def window_allowed(block_rows, offset, length):
    query_place = offset + jnp.arange(block_rows, dtype=jnp.int32)
    key_place = offset - WINDOW + jnp.arange(block_rows + 2 * WINDOW, dtype=jnp.int32)
    near = jnp.abs(query_place[:, None] - key_place[None, :]) < WINDOW
    inside = (key_place >= 0) & (key_place < length)
    return near & inside[None, :]


def block_slices(queries, padded_keys, padded_values, sequence, offset, block_rows):
    head_count = queries.shape[2]
    window_rows = block_rows + 2 * WINDOW
    query_block = lax.dynamic_slice(
        queries, (sequence, offset, 0, 0), (1, block_rows, head_count, HEAD_DIM)
    )[0]
    key_block = lax.dynamic_slice(
        padded_keys, (sequence, offset, 0, 0), (1, window_rows, head_count, HEAD_DIM)
    )[0]
    value_block = lax.dynamic_slice(
        padded_values, (sequence, offset, 0, 0), (1, window_rows, head_count, HEAD_DIM)
    )[0]
    return (query_block, key_block, value_block)


def local_scores(query_block, key_block, offset, block_rows, length, scaling):
    scores = (
        jnp.einsum("qhd,khd->hqk", query_block, key_block, preferred_element_type=jnp.float32)
        * scaling
    )
    return jnp.where(window_allowed(block_rows, offset, length)[None], scores, -1e30)


def local_forward(queries, key_rows, value_rows, scaling):
    sequences = queries.shape[0]
    length = queries.shape[1]
    block_rows = min(512, length)
    per_sequence = length // block_rows
    padding = ((0, 0), (WINDOW, WINDOW), (0, 0), (0, 0))
    padded_keys = jnp.pad(key_rows, padding)
    padded_values = jnp.pad(value_rows, padding)

    def one_block(block_index):
        sequence = block_index // per_sequence
        offset = block_index % per_sequence * block_rows
        query_block, key_block, value_block = block_slices(
            queries, padded_keys, padded_values, sequence, offset, block_rows
        )
        scores = local_scores(query_block, key_block, offset, block_rows, length, scaling)
        maximum = jnp.max(scores, axis=-1, keepdims=True)
        exponent = jnp.exp(scores - maximum)
        totals = jnp.sum(exponent, axis=-1, keepdims=True)
        weights = (exponent / totals).astype(jnp.bfloat16)
        result = jnp.einsum(
            "hqk,khd->qhd", weights, value_block, preferred_element_type=jnp.float32
        )
        return (result.astype(jnp.bfloat16), (maximum + jnp.log(totals))[..., 0])

    results, log_totals = lax.map(one_block, jnp.arange(sequences * per_sequence, dtype=jnp.int32))
    return (results.reshape(queries.shape), log_totals)


def local_backward(queries, key_rows, value_rows, result_grad, log_totals, scaling):
    sequences = queries.shape[0]
    length = queries.shape[1]
    head_count = queries.shape[2]
    block_rows = min(512, length)
    per_sequence = length // block_rows
    window_rows = block_rows + 2 * WINDOW
    padding = ((0, 0), (WINDOW, WINDOW), (0, 0), (0, 0))
    padded_keys = jnp.pad(key_rows, padding)
    padded_values = jnp.pad(value_rows, padding)

    def one_block(carry, block_index):
        key_grad, value_grad = carry
        sequence = block_index // per_sequence
        offset = block_index % per_sequence * block_rows
        query_block, key_block, value_block = block_slices(
            queries, padded_keys, padded_values, sequence, offset, block_rows
        )
        scores = local_scores(query_block, key_block, offset, block_rows, length, scaling)
        grad_block = lax.dynamic_slice(
            result_grad, (sequence, offset, 0, 0), (1, block_rows, head_count, HEAD_DIM)
        )[0]
        weights_full = jnp.exp(scores - log_totals[block_index][..., None])
        weights = weights_full.astype(jnp.bfloat16)
        weight_grad = jnp.einsum(
            "qhd,khd->hqk", grad_block, value_block, preferred_element_type=jnp.float32
        )
        score_low = (
            weights_full
            * (weight_grad - jnp.sum(weights_full * weight_grad, axis=-1, keepdims=True))
        ).astype(jnp.bfloat16)
        query_grad = (
            jnp.einsum("hqk,khd->qhd", score_low, key_block, preferred_element_type=jnp.float32)
            * scaling
        )
        key_part = (
            jnp.einsum("hqk,qhd->khd", score_low, query_block, preferred_element_type=jnp.float32)
            * scaling
        )
        value_part = jnp.einsum(
            "hqk,qhd->khd", weights, grad_block, preferred_element_type=jnp.float32
        )
        place = (sequence, offset, 0, 0)
        window_shape = (1, window_rows, head_count, HEAD_DIM)
        key_grad = lax.dynamic_update_slice(
            key_grad, lax.dynamic_slice(key_grad, place, window_shape) + key_part[None], place
        )
        value_grad = lax.dynamic_update_slice(
            value_grad, lax.dynamic_slice(value_grad, place, window_shape) + value_part[None], place
        )
        return ((key_grad, value_grad), query_grad)

    zero_pad = jnp.zeros((sequences, length + 2 * WINDOW, head_count, HEAD_DIM), jnp.float32)
    (key_grad, value_grad), query_grad = lax.scan(
        one_block, (zero_pad, zero_pad), jnp.arange(sequences * per_sequence, dtype=jnp.int32)
    )
    return (
        query_grad.reshape(queries.shape),
        key_grad[:, WINDOW : WINDOW + length],
        value_grad[:, WINDOW : WINDOW + length],
    )


def routed_forward(queries, key_rows, value_rows, scaling):
    scores = (
        jnp.einsum("sqhd,skhd->shqk", queries, key_rows, preferred_element_type=jnp.float32)
        * scaling
    )
    weights = jax.nn.softmax(scores, axis=-1).astype(jnp.bfloat16)
    return jnp.einsum("shqk,skhd->sqhd", weights, value_rows, preferred_element_type=jnp.float32)


def routed_backward(queries, key_rows, value_rows, result_grad, scaling):
    scores = (
        jnp.einsum("sqhd,skhd->shqk", queries, key_rows, preferred_element_type=jnp.float32)
        * scaling
    )
    weights_full = jax.nn.softmax(scores, axis=-1)
    weights = weights_full.astype(jnp.bfloat16)
    weight_grad = jnp.einsum(
        "sqhd,skhd->shqk",
        result_grad,
        value_rows.astype(jnp.float32),
        precision=lax.Precision.HIGHEST,
    )
    score_low = (
        weights_full * (weight_grad - jnp.sum(weights_full * weight_grad, axis=-1, keepdims=True))
    ).astype(jnp.bfloat16)
    query_grad = (
        jnp.einsum("shqk,skhd->sqhd", score_low, key_rows, preferred_element_type=jnp.float32)
        * scaling
    )
    key_grad = (
        jnp.einsum("shqk,sqhd->skhd", score_low, queries, preferred_element_type=jnp.float32)
        * scaling
    )
    value_grad = jnp.einsum(
        "shqk,sqhd->skhd", weights.astype(jnp.float32), result_grad, precision=lax.Precision.HIGHEST
    )
    return (query_grad, key_grad, value_grad)


def pair_swap(values):
    return lax.ppermute(values, "tensor", [(0, 1), (1, 0)])


def pair_join(mine, other, side):
    return jnp.where(side == 0, jnp.concatenate([mine, other]), jnp.concatenate([other, mine]))


def pair_sum(partial_sum):
    mine = partial_sum.astype(jnp.bfloat16)
    return mine.astype(jnp.float32) + pair_swap(mine).astype(jnp.float32)


def pair_scatter(partial_sum, side):
    low = partial_sum.astype(jnp.bfloat16)
    half = low.shape[0] // 2
    keep = lax.dynamic_slice_in_dim(low, side * half, half, 0)
    send = lax.dynamic_slice_in_dim(low, (1 - side) * half, half, 0)
    return keep.astype(jnp.float32) + pair_swap(send).astype(jnp.float32)


def halving_sum(values, order):
    parts = lax.axis_size("dp")
    place = lax.axis_index("dp")
    bits = list(range(len(order) - 1, -1, -1))
    held = values.reshape((2,) * len(bits) + (values.shape[0] // parts, values.shape[1]))
    held = held.astype(jnp.bfloat16)
    for step, bit in enumerate(order):
        axis = bits.index(bit)
        bits.remove(bit)
        mine = (place >> bit) & 1
        keep = lax.dynamic_index_in_dim(held, mine, axis, keepdims=False)
        send = lax.dynamic_index_in_dim(held, 1 - mine, axis, keepdims=False)
        got = lax.ppermute(send, "dp", [(i, i ^ (1 << bit)) for i in range(parts)])
        held = keep.astype(jnp.float32) + got.astype(jnp.float32)
        if step < len(order) - 1:
            held = held.astype(jnp.bfloat16)
    return held


def butterfly_sum(values):
    parts = lax.axis_size("dp")
    values = values + pair_swap(values)
    for bit in range(parts.bit_length() - 1):
        values = values + lax.ppermute(values, "dp", [(i, i ^ (1 << bit)) for i in range(parts)])
    return values


def body(
    tokens,
    cotangent,
    gain_attn,
    gain_ffn,
    route_query,
    route_key,
    route_ffn,
    light_query,
    light_key,
    light_value,
    light_out,
    heavy_query,
    heavy_key,
    heavy_value,
    heavy_out,
    light_gate,
    light_up,
    light_down,
    heavy_gate,
    heavy_up,
    heavy_down,
    query_index,
    key_index,
    ffn_index,
):
    sequences = query_index.shape[0]
    local_rows = tokens.shape[0]
    row_total = local_rows * lax.axis_size("tensor")
    length = row_total // sequences
    scaling = HEAD_DIM ** (-0.5)
    light_heads = light_query.shape[1] // HEAD_DIM
    heavy_heads = heavy_query.shape[1] // HEAD_DIM
    seq_base = length * jnp.arange(sequences, dtype=jnp.int32)[:, None]
    query_places = (query_index + seq_base).reshape(-1)
    key_places = (key_index + seq_base).reshape(-1)
    ffn_places = (ffn_index + seq_base).reshape(-1)
    query_picker = pick_matrix(query_index, length)
    key_picker = pick_matrix(key_index, length)
    ffn_picker = pick_matrix(ffn_index, length)

    def head_view(values, head_count):
        return values.reshape(sequences, length, head_count, HEAD_DIM)

    def routed_view(values, head_count):
        return values.reshape(sequences, -1, head_count, HEAD_DIM)

    side = lax.axis_index("tensor")
    residual = pair_join(tokens, pair_swap(tokens), side).astype(jnp.float32)
    grad_rows = pair_join(cotangent, pair_swap(cotangent), side)
    attn_normed, attn_norm_pull = jax.vjp(rms_scale, residual, gain_attn)
    attn_input = attn_normed.astype(jnp.bfloat16)
    query_light = matmul(attn_input, light_query).astype(jnp.bfloat16)
    key_light = matmul(attn_input, light_key).astype(jnp.bfloat16)
    value_light = matmul(attn_input, light_value).astype(jnp.bfloat16)
    light_result, light_totals = local_forward(
        head_view(query_light, light_heads),
        head_view(key_light, light_heads),
        head_view(value_light, light_heads),
        scaling,
    )
    light_result = light_result.reshape(row_total, -1)
    query_rows = pick_rows(query_picker, attn_input, length).astype(jnp.bfloat16)
    key_raw = pick_rows(key_picker, attn_input, length)
    query_score = jax.nn.sigmoid(precise_vec(query_rows.astype(jnp.float32), route_query))
    key_score = jax.nn.sigmoid(precise_vec(key_raw, route_key))
    key_rows = (key_score[:, None] * key_raw).astype(jnp.bfloat16)
    query_heavy = matmul(query_rows, heavy_query).astype(jnp.bfloat16)
    key_heavy = matmul(key_rows, heavy_key).astype(jnp.bfloat16)
    value_heavy = matmul(key_rows, heavy_value).astype(jnp.bfloat16)
    heavy_raw = routed_forward(
        routed_view(query_heavy, heavy_heads),
        routed_view(key_heavy, heavy_heads),
        routed_view(value_heavy, heavy_heads),
        scaling,
    ).reshape(query_rows.shape[0], -1)
    heavy_result = (query_score[:, None] * heavy_raw).astype(jnp.bfloat16)
    heavy_branch = spread_rows(query_places, matmul(heavy_result, heavy_out), row_total)
    middle = residual + pair_sum(matmul(light_result, light_out) + heavy_branch)
    ffn_normed, ffn_norm_pull = jax.vjp(rms_scale, middle, gain_ffn)
    ffn_input = ffn_normed.astype(jnp.bfloat16)
    gate_light = matmul(ffn_input, light_gate)
    up_light = matmul(ffn_input, light_up)
    mixed_light, light_mix_pull = jax.vjp(geglu_mix, gate_light, up_light)
    act_light = mixed_light.astype(jnp.bfloat16)
    ffn_rows = pick_rows(ffn_picker, ffn_input, length).astype(jnp.bfloat16)
    ffn_score = jax.nn.sigmoid(precise_vec(ffn_rows.astype(jnp.float32), route_ffn))
    gate_heavy = matmul(ffn_rows, heavy_gate)
    up_heavy = matmul(ffn_rows, heavy_up)
    mixed_heavy, heavy_mix_pull = jax.vjp(geglu_mix, gate_heavy, up_heavy)
    act_heavy = (ffn_score[:, None] * mixed_heavy).astype(jnp.bfloat16)
    heavy_ffn = spread_rows(ffn_places, matmul(act_heavy, heavy_down), row_total)
    block_out = (
        lax.dynamic_slice_in_dim(middle, side * local_rows, local_rows, 0)
        + pair_scatter(matmul(act_light, light_down) + heavy_ffn, side)
    ).astype(jnp.bfloat16)
    light_down_grad = matmul_tn(grad_rows, act_light)
    gate_light_grad, up_light_grad = light_mix_pull(matmul_nt(grad_rows, light_down))
    gate_light_grad = gate_light_grad.astype(jnp.bfloat16)
    up_light_grad = up_light_grad.astype(jnp.bfloat16)
    light_gate_grad = matmul_tn(ffn_input, gate_light_grad)
    light_up_grad = matmul_tn(ffn_input, up_light_grad)
    cot_rows = pick_rows(ffn_picker, grad_rows, length).astype(jnp.bfloat16)
    heavy_down_grad = matmul_tn(cot_rows, act_heavy)
    act_heavy_grad = matmul_nt(cot_rows, heavy_down)
    ffn_score_grad = jnp.sum(act_heavy_grad * mixed_heavy, axis=-1)
    gate_heavy_grad, up_heavy_grad = heavy_mix_pull(ffn_score[:, None] * act_heavy_grad)
    gate_heavy_grad = gate_heavy_grad.astype(jnp.bfloat16)
    up_heavy_grad = up_heavy_grad.astype(jnp.bfloat16)
    heavy_gate_grad = matmul_tn(ffn_rows, gate_heavy_grad)
    heavy_up_grad = matmul_tn(ffn_rows, up_heavy_grad)
    ffn_logit_grad = ffn_score * (1.0 - ffn_score) * ffn_score_grad
    route_ffn_grad = precise_vec(ffn_logit_grad, ffn_rows.astype(jnp.float32))
    ffn_rows_grad = (
        matmul_nt(gate_heavy_grad, heavy_gate)
        + matmul_nt(up_heavy_grad, heavy_up)
        + ffn_logit_grad[:, None] * route_ffn
    )
    heavy_ffn_back = spread_rows(ffn_places, ffn_rows_grad, row_total)
    ffn_normed_grad = pair_sum(
        matmul_nt(gate_light_grad, light_gate)
        + matmul_nt(up_light_grad, light_up)
        + heavy_ffn_back
    )
    middle_part, gain_ffn_grad = ffn_norm_pull(ffn_normed_grad)
    gain_ffn_grad = 0.5 * gain_ffn_grad
    middle_grad = grad_rows.astype(jnp.float32) + middle_part
    middle_low = middle_grad.astype(jnp.bfloat16)
    light_out_grad = matmul_tn(middle_low, light_result)
    light_result_grad = matmul_nt(middle_low, light_out).astype(jnp.bfloat16)
    query_light_grad, key_light_grad, value_light_grad = local_backward(
        head_view(query_light, light_heads),
        head_view(key_light, light_heads),
        head_view(value_light, light_heads),
        head_view(light_result_grad, light_heads),
        light_totals,
        scaling,
    )
    query_light_grad = query_light_grad.reshape(row_total, -1).astype(jnp.bfloat16)
    key_light_grad = key_light_grad.reshape(row_total, -1).astype(jnp.bfloat16)
    value_light_grad = value_light_grad.reshape(row_total, -1).astype(jnp.bfloat16)
    light_query_grad = matmul_tn(attn_input, query_light_grad)
    light_key_grad = matmul_tn(attn_input, key_light_grad)
    light_value_grad = matmul_tn(attn_input, value_light_grad)
    mid_rows = pick_rows(query_picker, middle_low, length).astype(jnp.bfloat16)
    heavy_out_grad = matmul_tn(mid_rows, heavy_result)
    heavy_result_grad = matmul_nt(mid_rows, heavy_out).astype(jnp.bfloat16).astype(jnp.float32)
    query_score_grad = jnp.sum(heavy_result_grad * heavy_raw, axis=-1)
    heavy_raw_grad = query_score[:, None] * heavy_result_grad
    query_heavy_grad, key_heavy_grad, value_heavy_grad = routed_backward(
        routed_view(query_heavy, heavy_heads),
        routed_view(key_heavy, heavy_heads),
        routed_view(value_heavy, heavy_heads),
        routed_view(heavy_raw_grad, heavy_heads),
        scaling,
    )
    routed_rows = query_rows.shape[0]
    query_heavy_grad = query_heavy_grad.reshape(routed_rows, -1).astype(jnp.bfloat16)
    key_heavy_grad = key_heavy_grad.reshape(routed_rows, -1).astype(jnp.bfloat16)
    value_heavy_grad = value_heavy_grad.reshape(routed_rows, -1).astype(jnp.bfloat16)
    heavy_query_grad = matmul_tn(query_rows, query_heavy_grad)
    heavy_key_grad = matmul_tn(key_rows, key_heavy_grad)
    heavy_value_grad = matmul_tn(key_rows, value_heavy_grad)
    key_rows_grad = matmul_nt(key_heavy_grad, heavy_key) + matmul_nt(value_heavy_grad, heavy_value)
    key_logit_grad = key_score * (1.0 - key_score) * jnp.sum(key_rows_grad * key_raw, axis=-1)
    route_key_grad = precise_vec(key_logit_grad, key_raw)
    key_raw_grad = key_score[:, None] * key_rows_grad + key_logit_grad[:, None] * route_key
    query_logit_grad = query_score * (1.0 - query_score) * query_score_grad
    route_query_grad = precise_vec(query_logit_grad, query_rows.astype(jnp.float32))
    query_rows_grad = (
        matmul_nt(query_heavy_grad, heavy_query) + query_logit_grad[:, None] * route_query
    )
    heavy_attn_back = (
        spread_rows(query_places, query_rows_grad, row_total).at[key_places].add(key_raw_grad)
    )
    attn_partial = (
        matmul_nt(query_light_grad, light_query)
        + matmul_nt(key_light_grad, light_key)
        + matmul_nt(value_light_grad, light_value)
        + heavy_attn_back
    )
    row_factor = lax.rsqrt(jnp.mean(residual * residual, axis=-1, keepdims=True) + 1e-06)
    gain_attn_grad = jnp.sum(residual * row_factor * attn_partial, axis=0)
    attn_normed_grad = pair_scatter(attn_partial, side)
    own_tokens = tokens.astype(jnp.float32)
    _, own_pull = jax.vjp(rms_scale, own_tokens, gain_attn)
    resid_part, _ = own_pull(attn_normed_grad)
    own_middle_grad = lax.dynamic_slice_in_dim(middle_grad, side * local_rows, local_rows, 0)
    input_grad = (own_middle_grad + resid_part).astype(jnp.bfloat16)
    small = jnp.stack(
        [gain_attn_grad, gain_ffn_grad, route_query_grad, route_key_grad, route_ffn_grad]
    )
    small_summed = butterfly_sum(small)
    forward_order = list(range(lax.axis_size("dp").bit_length() - 1))
    other_order = [1, 0] + forward_order[2:]

    def group(pieces, order):
        widths = [piece.shape[1] for piece in pieces]
        total = halving_sum(
            jnp.concatenate([piece.astype(jnp.bfloat16) for piece in pieces], axis=1), order
        )
        out, start = [], 0
        for width in widths:
            out.append(total[:, start : start + width])
            start += width
        return out

    hg, hu, hd = group([heavy_gate_grad, heavy_up_grad, heavy_down_grad], forward_order)
    lg, lu, ld = group([light_gate_grad, light_up_grad, light_down_grad], other_order)
    ho, lo, hq, hk, hv = group(
        [heavy_out_grad, light_out_grad, heavy_query_grad, heavy_key_grad, heavy_value_grad],
        forward_order,
    )
    lq, lk, lv = group([light_query_grad, light_key_grad, light_value_grad], other_order)
    every_grad = (lq, lk, lv, lo.T, hq, hk, hv, ho.T, lg, lu, ld.T, hg, hu, hd.T)
    return (
        block_out,
        input_grad,
        small_summed[0],
        small_summed[1],
        small_summed[2],
        small_summed[3],
        small_summed[4],
        every_grad[0],
        every_grad[1],
        every_grad[2],
        every_grad[3],
        every_grad[4],
        every_grad[5],
        every_grad[6],
        every_grad[7],
        every_grad[8],
        every_grad[9],
        every_grad[10],
        every_grad[11],
        every_grad[12],
        every_grad[13],
    )


def solution(mesh):
    in_specs = (
        P(("dp", "tensor"), None),
        P(("dp", "tensor"), None),
        P(),
        P(),
        P(),
        P(),
        P(),
        P(None, "tensor"),
        P(None, "tensor"),
        P(None, "tensor"),
        P("tensor", None),
        P(None, "tensor"),
        P(None, "tensor"),
        P(None, "tensor"),
        P("tensor", None),
        P(None, "tensor"),
        P(None, "tensor"),
        P("tensor", None),
        P(None, "tensor"),
        P(None, "tensor"),
        P("tensor", None),
        P("dp", None),
        P("dp", None),
        P("dp", None),
    )
    out_specs = (
        P(("dp", "tensor"), None),
        P(("dp", "tensor"), None),
        P(),
        P(),
        P(),
        P(),
        P(),
        P("dp", "tensor"),
        P("dp", "tensor"),
        P("dp", "tensor"),
        P("tensor", "dp"),
        P("dp", "tensor"),
        P("dp", "tensor"),
        P("dp", "tensor"),
        P("tensor", "dp"),
        P("dp", "tensor"),
        P("dp", "tensor"),
        P("tensor", "dp"),
        P("dp", "tensor"),
        P("dp", "tensor"),
        P("tensor", "dp"),
    )
    return jax.shard_map(body, mesh=mesh, in_specs=in_specs, out_specs=out_specs, check_vma=False)
```

```python
import jax
import jax.numpy as jnp
from jax import lax
from jax.experimental import pallas as pl
from jax.experimental.pallas import tpu as pltpu
from jax.sharding import PartitionSpec as P

HEAD_DIM = 64
WINDOW = 128
EPS = 1e-06
VMEM_LIMIT = 60 * 1024 * 1024
f32 = jnp.float32
bf16 = jnp.bfloat16


def pair_swap(values):
    return lax.ppermute(values, "tensor", [(0, 1), (1, 0)])


def halving_sum(values, order):
    parts = lax.axis_size("dp")
    place = lax.axis_index("dp")
    bits = list(range(len(order) - 1, -1, -1))
    held = values.reshape((2,) * len(bits) + (values.shape[0] // parts, values.shape[1]))
    held = held.astype(jnp.bfloat16)
    for step, bit in enumerate(order):
        axis = bits.index(bit)
        bits.remove(bit)
        mine = (place >> bit) & 1
        keep = lax.dynamic_index_in_dim(held, mine, axis, keepdims=False)
        send = lax.dynamic_index_in_dim(held, 1 - mine, axis, keepdims=False)
        got = lax.ppermute(send, "dp", [(i, i ^ (1 << bit)) for i in range(parts)])
        held = keep.astype(jnp.float32) + got.astype(jnp.float32)
        if step < len(order) - 1:
            held = held.astype(jnp.bfloat16)
    return held


def butterfly_sum(values):
    parts = lax.axis_size("dp")
    values = values + pair_swap(values)
    for bit in range(parts.bit_length() - 1):
        values = values + lax.ppermute(values, "dp", [(i, i ^ (1 << bit)) for i in range(parts)])
    return values


def mm(left, right, left_dim=1, right_dim=0):
    return lax.dot_general(
        left, right, (((left_dim,), (right_dim,)), ((), ())), preferred_element_type=f32
    )


def split_low(values):
    high = values.astype(bf16)
    return high, (values - high.astype(f32)).astype(bf16)


def sigmoid(values):
    return 1.0 / (1.0 + jnp.exp(-values))


def row_factor(values):
    return lax.rsqrt(jnp.mean(values * values, axis=-1, keepdims=True) + EPS)


def picks(index_ref, length):
    rows = lax.broadcasted_iota(jnp.int32, (length, index_ref.shape[1]), 0)
    return jnp.where(rows == index_ref[...], 1.0, 0.0).astype(bf16)


def head_masks(width):
    lanes = lax.shift_right_logical(lax.broadcasted_iota(jnp.int32, (1, width), 1), 6)
    return [jnp.where(lanes == head, 1.0, 0.0).astype(f32) for head in range(width // HEAD_DIM)]


def stack_heads(values, masks):
    return jnp.concatenate([values * mask.astype(values.dtype) for mask in masks], axis=0)


def unstack_heads(values, masks):
    rows = values.shape[0] // len(masks)
    total = values[:rows] * masks[0]
    for head in range(1, len(masks)):
        total = total + values[head * rows : (head + 1) * rows] * masks[head]
    return total


def softmax_rows(scores, axis):
    exponent = jnp.exp(scores - jnp.max(scores, axis=axis, keepdims=True))
    return exponent * (1.0 / jnp.sum(exponent, axis=axis, keepdims=True))


def window_start(block, length):
    start = jnp.clip(block * WINDOW - WINDOW, 0, length - 3 * WINDOW)
    return pl.multiple_of(start, WINDOW)


def attn_forward_kernel(
    own_ref,
    other_ref,
    gain_ref,
    route_query_ref,
    route_key_ref,
    query_index_ref,
    key_index_ref,
    wq_ref,
    wk_ref,
    wv_ref,
    wo_ref,
    hq_ref,
    hk_ref,
    hv_ref,
    ho_ref,
    partial_ref,
    input_ref,
    q_ref,
    k_ref,
    v_ref,
    result_ref,
    query_rows_ref,
    key_raw_ref,
    key_rows_ref,
    qh_ref,
    kh_ref,
    vh_ref,
    raw_ref,
    heavy_result_ref,
    pick_ref,
):
    side = lax.axis_index("tensor")
    half = own_ref.shape[0]
    length = 2 * half
    tile = 256
    for ref, place in ((own_ref, side), (other_ref, 1 - side)):
        for start in range(0, half, tile):
            values = ref[start : start + tile, :].astype(f32)
            normed = values * row_factor(values) * gain_ref[...]
            rows = pl.ds(pl.multiple_of(place * half + start, tile), tile)
            input_ref[rows, :] = normed.astype(bf16)
    routed = query_index_ref.shape[1]
    pick_ref[:, :routed] = picks(query_index_ref, length)
    pick_ref[:, routed:] = picks(key_index_ref, length)
    picked = mm(pick_ref[...], input_ref[...], 0, 0)
    query_rows = picked[:routed]
    key_raw = picked[routed:]
    query_score = sigmoid(jnp.sum(query_rows * route_query_ref[...], axis=-1, keepdims=True))
    key_score = sigmoid(jnp.sum(key_raw * route_key_ref[...], axis=-1, keepdims=True))
    query_rows_ref[...] = query_rows.astype(bf16)
    key_raw_ref[...] = key_raw.astype(bf16)
    key_rows_ref[...] = (key_score * key_raw).astype(bf16)
    qh_ref[...] = mm(query_rows_ref[...], hq_ref[...]).astype(bf16)
    kh_ref[...] = mm(key_rows_ref[...], hk_ref[...]).astype(bf16)
    vh_ref[...] = mm(key_rows_ref[...], hv_ref[...]).astype(bf16)
    pair = 2 * HEAD_DIM
    pair_masks = head_masks(pair)
    for start in range(0, qh_ref.shape[1], pair):
        cols = slice(start, start + pair)
        stacked = stack_heads(qh_ref[:, cols] * (HEAD_DIM**-0.5), pair_masks)
        probs = softmax_rows(mm(stacked, kh_ref[:, cols], 1, 1), -1)
        raw_ref[:, cols] = unstack_heads(mm(probs.astype(bf16), vh_ref[:, cols]), pair_masks)
    heavy_result_ref[...] = (query_score * raw_ref[...]).astype(bf16)
    high, low = split_low(mm(heavy_result_ref[...], ho_ref[...]))

    for start in range(0, length, tile):
        rows = slice(start, start + tile)
        q_ref[rows, :] = mm(input_ref[rows, :], wq_ref[...]).astype(bf16)
        k_ref[rows, :] = mm(input_ref[rows, :], wk_ref[...]).astype(bf16)
        v_ref[rows, :] = mm(input_ref[rows, :], wv_ref[...]).astype(bf16)

    masks = head_masks(q_ref.shape[1])
    heads = len(masks)
    gap = lax.broadcasted_iota(jnp.int32, (WINDOW, 3 * WINDOW), 0) - lax.broadcasted_iota(
        jnp.int32, (WINDOW, 3 * WINDOW), 1
    )

    def one_block(block, carry):
        rows = pl.ds(pl.multiple_of(block * WINDOW, WINDOW), WINDOW)
        start = window_start(block, length)
        keys = pl.ds(start, 3 * WINDOW)
        stacked = stack_heads(q_ref[rows, :] * (HEAD_DIM**-0.5), masks)
        scores = mm(stacked, k_ref[keys, :], 1, 1)
        near = jnp.abs(gap + (block * WINDOW - start)) < WINDOW
        bias = jnp.where(near, 0.0, -1e30)
        probs = softmax_rows(scores + jnp.concatenate([bias] * heads, axis=0), -1)
        out = unstack_heads(mm(probs.astype(bf16), v_ref[keys, :]), masks)
        result_ref[rows, :] = out.astype(bf16)
        return carry

    lax.fori_loop(0, length // WINDOW, one_block, 0)
    for start in range(0, length, tile):
        rows = slice(start, start + tile)
        pick = pick_ref[rows, :routed]
        partial_ref[rows, :] = (
            mm(result_ref[rows, :], wo_ref[...]) + (mm(pick, high) + mm(pick, low))
        ).astype(bf16)


def gelu_parts(values):
    density = jnp.exp(-0.5 * values * values) * 0.3989422804014327
    below = 0.5 * (1.0 + lax.erf(values * 0.7071067811865476))
    return values * below, below + values * density


def ffn_kernel(
    own_ref,
    other_ref,
    mine_ref,
    got_ref,
    cot_own_ref,
    cot_other_ref,
    gain_ref,
    route_ref,
    index_ref,
    wg_ref,
    wu_ref,
    wd_ref,
    hg_ref,
    hu_ref,
    hd_ref,
    middle_ref,
    block_own_ref,
    block_send_ref,
    back_ref,
    light_grad_ref,
    rows_ref,
    cot_rows_ref,
    act_heavy_ref,
    mix_heavy_ref,
    route_grad_ref,
    input_ref,
    cot_ref,
    act_ref,
    mix_ref,
    pick_ref,
):
    side = lax.axis_index("tensor")
    half = own_ref.shape[0]
    length = 2 * half
    tile = 256
    for ref, cot, place in ((own_ref, cot_own_ref, side), (other_ref, cot_other_ref, 1 - side)):
        for start in range(0, half, tile):
            rows = pl.ds(pl.multiple_of(place * half + start, tile), tile)
            branch = mine_ref[rows, :].astype(f32) + got_ref[rows, :].astype(f32)
            middle = ref[start : start + tile, :].astype(f32) + branch
            middle_ref[rows, :] = middle
            input_ref[rows, :] = (middle * row_factor(middle) * gain_ref[...]).astype(bf16)
            cot_ref[rows, :] = cot[start : start + tile, :]
    pick_ref[...] = picks(index_ref, length)
    ffn_rows = mm(pick_ref[...], input_ref[...], 0, 0)
    rows_ref[...] = ffn_rows.astype(bf16)
    cot_rows_ref[...] = mm(pick_ref[...], cot_ref[...], 0, 0).astype(bf16)
    score = sigmoid(jnp.sum(ffn_rows * route_ref[...], axis=-1, keepdims=True))
    heavy_width = hg_ref.shape[1]
    chunk = 512
    score_grad = 0.0
    down = 0.0
    rows_grad = 0.0
    for start in range(0, heavy_width, chunk):
        cols = slice(start, start + chunk)
        up_cols = slice(heavy_width + start, heavy_width + start + chunk)
        gate = mm(rows_ref[...], hg_ref[:, cols])
        up = mm(rows_ref[...], hu_ref[:, cols])
        act_grad = mm(cot_rows_ref[...], hd_ref[cols, :], 1, 1)
        gelu, slope = gelu_parts(gate)
        mixed = gelu * up
        act_heavy_ref[:, cols] = (score * mixed).astype(bf16)
        score_grad = score_grad + jnp.sum(act_grad * mixed, axis=-1, keepdims=True)
        scaled = score * act_grad
        mix_heavy_ref[:, cols] = (scaled * up * slope).astype(bf16)
        mix_heavy_ref[:, up_cols] = (scaled * gelu).astype(bf16)
        down = down + mm(act_heavy_ref[:, cols], hd_ref[cols, :])
        rows_grad = rows_grad + mm(mix_heavy_ref[:, cols], hg_ref[:, cols], 1, 1)
        rows_grad = rows_grad + mm(mix_heavy_ref[:, up_cols], hu_ref[:, cols], 1, 1)
    logit_grad = score * (1.0 - score) * score_grad
    route_grad_ref[...] = jnp.sum(ffn_rows * logit_grad, axis=0, keepdims=True)
    rows_grad = rows_grad + logit_grad * route_ref[...]
    down_high, down_low = split_low(down)
    back_high, back_low = split_low(rows_grad)
    width = wg_ref.shape[1]
    for first in range(0, 2):
        place = side if first == 0 else 1 - side
        for start in range(0, half, tile):
            rows = pl.ds(pl.multiple_of(place * half + start, tile), tile)
            piece = slice(start, start + tile)
            gate = mm(input_ref[rows, :], wg_ref[...])
            up = mm(input_ref[rows, :], wu_ref[...])
            act_grad = mm(cot_ref[rows, :], wd_ref[...], 1, 1)
            gelu, slope = gelu_parts(gate)
            act_ref[rows, :] = (gelu * up).astype(bf16)
            mix_ref[rows, :width] = (act_grad * up * slope).astype(bf16)
            mix_ref[rows, width:] = (act_grad * gelu).astype(bf16)
            pick = pick_ref[rows, :]
            branch = mm(act_ref[rows, :], wd_ref[...]) + (mm(pick, down_high) + mm(pick, down_low))
            if first == 0:
                block_own_ref[piece, :] = middle_ref[rows, :] + branch
            else:
                block_send_ref[piece, :] = branch.astype(bf16)
            back_ref[rows, :] = (
                mm(mix_ref[rows, :width], wg_ref[...], 1, 1)
                + mm(mix_ref[rows, width:], wu_ref[...], 1, 1)
                + (mm(pick, back_high) + mm(pick, back_low))
            ).astype(bf16)
    light_grad_ref[:, : 2 * width] = mm(input_ref[...], mix_ref[...], 0, 0).astype(bf16)
    light_grad_ref[:, 2 * width :] = mm(cot_ref[...], act_ref[...], 0, 0).astype(bf16)


def attn_backward_kernel(
    own_ref,
    other_ref,
    cot_own_ref,
    cot_other_ref,
    middle_ref,
    mine_ref,
    got_ref,
    gain_attn_ref,
    gain_ffn_ref,
    route_query_ref,
    route_key_ref,
    query_index_ref,
    key_index_ref,
    wq_ref,
    wk_ref,
    wv_ref,
    wo_ref,
    hq_ref,
    hk_ref,
    hv_ref,
    ho_ref,
    input_ref,
    q_ref,
    k_ref,
    v_ref,
    result_ref,
    query_rows_ref,
    key_raw_ref,
    key_rows_ref,
    qh_ref,
    kh_ref,
    vh_ref,
    raw_ref,
    heavy_result_ref,
    own_middle_ref,
    own_back_ref,
    send_ref,
    light_grad_ref,
    out_grad_ref,
    heavy_grad_ref,
    small_ref,
    low_ref,
    out_ref,
    kt_ref,
    qt_grad_ref,
    k_grad_ref,
    v_grad_ref,
    grads_ref,
    pick_ref,
):
    side = lax.axis_index("tensor")
    half = own_ref.shape[0]
    length = 2 * half
    tile = 256
    scale = HEAD_DIM**-0.5
    gain_ffn_grad = 0.0
    for cot, place, owned in ((cot_own_ref, side, True), (cot_other_ref, 1 - side, False)):
        for start in range(0, half, tile):
            rows = pl.ds(pl.multiple_of(place * half + start, tile), tile)
            piece = slice(start, start + tile)
            normed_grad = mine_ref[rows, :].astype(f32) + got_ref[rows, :].astype(f32)
            middle = middle_ref[rows, :]
            factor = row_factor(middle)
            scaled = factor * middle
            gain_ffn_grad = gain_ffn_grad + jnp.sum(scaled * normed_grad, axis=0, keepdims=True)
            gained = gain_ffn_ref[...] * normed_grad
            inner = jnp.mean(scaled * gained, axis=-1, keepdims=True)
            grad = cot[piece, :].astype(f32) + factor * (gained - scaled * inner)
            if owned:
                own_middle_ref[piece, :] = grad
            low_ref[rows, :] = grad.astype(bf16)
    for start in range(0, length, tile):
        rows = slice(start, start + tile)
        out_ref[rows, :] = mm(low_ref[rows, :], wo_ref[...], 1, 1).astype(bf16)
    out_grad_ref[...] = mm(low_ref[...], result_ref[...], 0, 0).astype(bf16)

    routed = query_index_ref.shape[1]
    pick_ref[:, :routed] = picks(query_index_ref, length)
    pick_ref[:, routed:] = picks(key_index_ref, length)
    query_rows = query_rows_ref[...].astype(f32)
    key_raw = key_raw_ref[...].astype(f32)
    query_score = sigmoid(jnp.sum(query_rows * route_query_ref[...], axis=-1, keepdims=True))
    key_score = sigmoid(jnp.sum(key_raw * route_key_ref[...], axis=-1, keepdims=True))
    mid_rows = mm(pick_ref[:, :routed], low_ref[...], 0, 0).astype(bf16)
    heavy = qh_ref.shape[1]
    heavy_grad_ref[:, 3 * heavy :] = mm(mid_rows, heavy_result_ref[...], 0, 0).astype(bf16)
    heavy_out_grad = mm(mid_rows, ho_ref[...], 1, 1).astype(bf16)
    query_score_grad = jnp.sum(
        heavy_out_grad.astype(f32) * raw_ref[...], axis=-1, keepdims=True
    )
    raw_high, raw_low = split_low(query_score * heavy_out_grad.astype(f32))
    pair = 2 * HEAD_DIM
    pair_masks = head_masks(pair)
    stacked_score = jnp.concatenate([query_score] * 2, axis=0)
    q_parts, k_parts, v_parts = [], [], []
    for start in range(0, heavy, pair):
        cols = slice(start, start + pair)
        stacked = stack_heads(qh_ref[:, cols] * scale, pair_masks)
        probs = softmax_rows(mm(stacked, kh_ref[:, cols], 1, 1), -1)
        grad_stacked = stack_heads(heavy_out_grad[:, cols], pair_masks)
        probs_grad = stacked_score * mm(grad_stacked, vh_ref[:, cols], 1, 1)
        inner = jnp.sum(probs * probs_grad, axis=-1, keepdims=True)
        score_grad = (probs * (probs_grad - inner)).astype(bf16)
        probs_low = probs.astype(bf16)
        q_parts.append(unstack_heads(mm(score_grad, kh_ref[:, cols]) * scale, pair_masks))
        k_parts.append(mm(score_grad, stacked, 0, 0))
        v_parts.append(
            mm(probs_low, stack_heads(raw_high[:, cols], pair_masks), 0, 0)
            + mm(probs_low, stack_heads(raw_low[:, cols], pair_masks), 0, 0)
        )
    query_heavy_grad = jnp.concatenate(q_parts, axis=1).astype(bf16)
    key_heavy_grad = jnp.concatenate(k_parts, axis=1).astype(bf16)
    value_heavy_grad = jnp.concatenate(v_parts, axis=1).astype(bf16)
    heavy_grad_ref[:, :heavy] = mm(query_rows_ref[...], query_heavy_grad, 0, 0).astype(bf16)
    heavy_grad_ref[:, heavy : 2 * heavy] = mm(key_rows_ref[...], key_heavy_grad, 0, 0).astype(bf16)
    heavy_grad_ref[:, 2 * heavy : 3 * heavy] = mm(
        key_rows_ref[...], value_heavy_grad, 0, 0
    ).astype(bf16)
    key_rows_grad = mm(key_heavy_grad, hk_ref[...], 1, 1) + mm(
        value_heavy_grad, hv_ref[...], 1, 1
    )
    key_logit_grad = (
        key_score * (1.0 - key_score) * jnp.sum(key_rows_grad * key_raw, axis=-1, keepdims=True)
    )
    query_logit_grad = query_score * (1.0 - query_score) * query_score_grad
    key_raw_grad = key_score * key_rows_grad + key_logit_grad * route_key_ref[...]
    query_rows_grad = mm(query_heavy_grad, hq_ref[...], 1, 1)
    query_rows_grad = query_rows_grad + query_logit_grad * route_query_ref[...]
    small_ref[...] = jnp.zeros_like(small_ref)
    small_ref[1:2, :] = 0.5 * gain_ffn_grad
    small_ref[2:3, :] = jnp.sum(query_rows * query_logit_grad, axis=0, keepdims=True)
    small_ref[3:4, :] = jnp.sum(key_raw * key_logit_grad, axis=0, keepdims=True)
    back_high, back_low = split_low(jnp.concatenate([query_rows_grad, key_raw_grad], axis=0))

    kt_ref[...] = k_ref[...].T
    k_grad_ref[...] = jnp.zeros_like(k_grad_ref)
    v_grad_ref[...] = jnp.zeros_like(v_grad_ref)
    masks = head_masks(q_ref.shape[1])
    heads = len(masks)
    gap = lax.broadcasted_iota(jnp.int32, (3 * WINDOW, WINDOW), 1) - lax.broadcasted_iota(
        jnp.int32, (3 * WINDOW, WINDOW), 0
    )

    def one_block(block, carry):
        first = pl.multiple_of(block * WINDOW, WINDOW)
        rows = pl.ds(first, WINDOW)
        start = window_start(block, length)
        keys = pl.ds(start, 3 * WINDOW)
        stacked = stack_heads(q_ref[rows, :] * scale, masks)
        grad_stacked = stack_heads(out_ref[rows, :], masks)
        near = jnp.abs(gap + (block * WINDOW - start)) < WINDOW
        bias = jnp.where(near, 0.0, -1e30)
        scores = mm(k_ref[keys, :], stacked, 1, 1)
        probs = softmax_rows(scores + jnp.concatenate([bias] * heads, axis=1), 0)
        probs_grad = mm(v_ref[keys, :], grad_stacked, 1, 1)
        inner = jnp.sum(probs * probs_grad, axis=0, keepdims=True)
        score_grad = (probs * (probs_grad - inner)).astype(bf16)
        k_grad_ref[keys, :] += mm(score_grad, stacked)
        v_grad_ref[keys, :] += mm(probs.astype(bf16), grad_stacked)
        spread = mm(kt_ref[:, keys], score_grad) * scale
        for head in range(heads):
            lanes = slice(head * HEAD_DIM, (head + 1) * HEAD_DIM)
            qt_grad_ref[lanes, rows] = spread[lanes, head * WINDOW : (head + 1) * WINDOW]
        return carry

    lax.fori_loop(0, length // WINDOW, one_block, 0)
    light = q_ref.shape[1]
    grads_ref[:, :light] = qt_grad_ref[...].T.astype(bf16)
    grads_ref[:, light : 2 * light] = k_grad_ref[...].astype(bf16)
    grads_ref[:, 2 * light :] = v_grad_ref[...].astype(bf16)
    light_grad_ref[...] = mm(input_ref[...], grads_ref[...], 0, 0).astype(bf16)
    gain_attn_grad = 0.0
    for ref, place, owned in ((own_ref, side, True), (other_ref, 1 - side, False)):
        for start in range(0, half, tile):
            rows = pl.ds(pl.multiple_of(place * half + start, tile), tile)
            piece = slice(start, start + tile)
            pick = pick_ref[rows, :]
            back = (
                mm(grads_ref[rows, :light], wq_ref[...], 1, 1)
                + mm(grads_ref[rows, light : 2 * light], wk_ref[...], 1, 1)
                + mm(grads_ref[rows, 2 * light :], wv_ref[...], 1, 1)
                + (mm(pick, back_high) + mm(pick, back_low))
            )
            values = ref[piece, :].astype(f32)
            gain_attn_grad = gain_attn_grad + jnp.sum(
                values * row_factor(values) * back, axis=0, keepdims=True
            )
            if owned:
                own_back_ref[piece, :] = back
            else:
                send_ref[piece, :] = back.astype(bf16)
    small_ref[0:1, :] = gain_attn_grad


def whole(kernel, name, outs, scratch, *operands):
    return pl.pallas_call(
        kernel,
        name=name,
        out_shape=[jax.ShapeDtypeStruct(shape, dtype) for shape, dtype in outs],
        in_specs=[pl.BlockSpec(memory_space=pltpu.VMEM)] * len(operands),
        out_specs=[pl.BlockSpec(memory_space=pltpu.VMEM)] * len(outs),
        scratch_shapes=[pltpu.VMEM(shape, dtype) for shape, dtype in scratch],
        compiler_params=pltpu.CompilerParams(vmem_limit_bytes=VMEM_LIMIT),
    )(*operands)


def body(
    tokens,
    cotangent,
    gain_attn,
    gain_ffn,
    route_query,
    route_key,
    route_ffn,
    light_query,
    light_key,
    light_value,
    light_out,
    heavy_query,
    heavy_key,
    heavy_value,
    heavy_out,
    light_gate,
    light_up,
    light_down,
    heavy_gate,
    heavy_up,
    heavy_down,
    query_index,
    key_index,
    ffn_index,
):
    half, width = tokens.shape
    length = 2 * half
    routed = query_index.shape[1]
    light = light_query.shape[1]
    heavy = heavy_query.shape[1]
    light_ff = light_gate.shape[1]
    heavy_ff = heavy_gate.shape[1]
    gain_attn, gain_ffn, route_query, route_key, route_ffn = (
        item.reshape(1, -1) for item in (gain_attn, gain_ffn, route_query, route_key, route_ffn)
    )
    other_tokens = pair_swap(tokens)
    other_cotangent = pair_swap(cotangent)
    attn_weights = (
        light_query,
        light_key,
        light_value,
        light_out,
        heavy_query,
        heavy_key,
        heavy_value,
        heavy_out,
    )
    attn_partial, *saved = whole(
        attn_forward_kernel,
        "attn_forward",
        [((length, width), bf16)] * 2
        + [((length, light), bf16)] * 4
        + [((routed, width), bf16)] * 3
        + [((routed, heavy), bf16)] * 3
        + [((routed, heavy), f32), ((routed, heavy), bf16)],
        [((length, 2 * routed), bf16)],
        tokens,
        other_tokens,
        gain_attn,
        route_query,
        route_key,
        query_index,
        key_index,
        *attn_weights,
    )
    (
        middle,
        block_own,
        block_send,
        ffn_back,
        light_ffn_grad,
        ffn_rows,
        cot_rows,
        act_heavy,
        mix_heavy,
        route_ffn_grad,
    ) = whole(
        ffn_kernel,
        "ffn",
        [
            ((length, width), f32),
            ((half, width), f32),
            ((half, width), bf16),
            ((length, width), bf16),
            ((width, 3 * light_ff), bf16),
            ((routed, width), bf16),
            ((routed, width), bf16),
            ((routed, heavy_ff), bf16),
            ((routed, 2 * heavy_ff), bf16),
            ((1, width), f32),
        ],
        [
            ((length, width), bf16),
            ((length, width), bf16),
            ((length, light_ff), bf16),
            ((length, 2 * light_ff), bf16),
            ((length, routed), bf16),
        ],
        tokens,
        other_tokens,
        attn_partial,
        pair_swap(attn_partial),
        cotangent,
        other_cotangent,
        gain_ffn,
        route_ffn,
        ffn_index,
        light_gate,
        light_up,
        light_down,
        heavy_gate,
        heavy_up,
        heavy_down,
    )
    block_out = (block_own + pair_swap(block_send).astype(f32)).astype(bf16)
    own_middle, own_back, back_send, light_grad, out_grad, heavy_grad, small = whole(
        attn_backward_kernel,
        "attn_backward",
        [
            ((half, width), f32),
            ((half, width), f32),
            ((half, width), bf16),
            ((width, 3 * light), bf16),
            ((width, light), bf16),
            ((width, 4 * heavy), bf16),
            ((8, width), f32),
        ],
        [
            ((length, width), bf16),
            ((length, light), bf16),
            ((light, length), bf16),
            ((light, length), f32),
            ((length, light), f32),
            ((length, light), f32),
            ((length, 3 * light), bf16),
            ((length, 2 * routed), bf16),
        ],
        tokens,
        other_tokens,
        cotangent,
        other_cotangent,
        middle,
        ffn_back,
        pair_swap(ffn_back),
        gain_attn,
        gain_ffn,
        route_query,
        route_key,
        query_index,
        key_index,
        *attn_weights,
        *saved,
    )
    normed_grad = own_back + pair_swap(back_send).astype(f32)
    own_tokens = tokens.astype(f32)
    factor = row_factor(own_tokens)
    scaled = own_tokens * factor
    gained = gain_attn * normed_grad
    inner = jnp.mean(scaled * gained, axis=-1, keepdims=True)
    input_grad = (own_middle + factor * (gained - scaled * inner)).astype(bf16)
    small_summed = butterfly_sum(small + jnp.pad(route_ffn_grad, ((4, 3), (0, 0))))

    forward_order = list(range(lax.axis_size("dp").bit_length() - 1))
    other_order = [1, 0] + forward_order[2:]
    heavy_mix_grad = mm(ffn_rows, mix_heavy, 0, 0).astype(bf16)
    heavy_down_grad = mm(cot_rows, act_heavy, 0, 0).astype(bf16)
    mixed_sum = halving_sum(heavy_mix_grad, forward_order)
    down_sum = halving_sum(heavy_down_grad, other_order)
    light_ffn_sum = halving_sum(light_ffn_grad, other_order)
    heavy_sum = halving_sum(heavy_grad, forward_order)
    light_sum = halving_sum(light_grad, other_order)
    out_sum = halving_sum(out_grad, other_order)
    return (
        block_out,
        input_grad,
        small_summed[0],
        small_summed[1],
        small_summed[2],
        small_summed[3],
        small_summed[4],
        light_sum[:, :light],
        light_sum[:, light : 2 * light],
        light_sum[:, 2 * light :],
        out_sum.T,
        heavy_sum[:, :heavy],
        heavy_sum[:, heavy : 2 * heavy],
        heavy_sum[:, 2 * heavy : 3 * heavy],
        heavy_sum[:, 3 * heavy :].T,
        light_ffn_sum[:, :light_ff],
        light_ffn_sum[:, light_ff : 2 * light_ff],
        light_ffn_sum[:, 2 * light_ff :].T,
        mixed_sum[:, :heavy_ff],
        mixed_sum[:, heavy_ff:],
        down_sum.T,
    )


def solution(mesh):
    in_specs = (
        P(("dp", "tensor"), None),
        P(("dp", "tensor"), None),
        P(),
        P(),
        P(),
        P(),
        P(),
        P(None, "tensor"),
        P(None, "tensor"),
        P(None, "tensor"),
        P("tensor", None),
        P(None, "tensor"),
        P(None, "tensor"),
        P(None, "tensor"),
        P("tensor", None),
        P(None, "tensor"),
        P(None, "tensor"),
        P("tensor", None),
        P(None, "tensor"),
        P(None, "tensor"),
        P("tensor", None),
        P("dp", None),
        P("dp", None),
        P("dp", None),
    )
    out_specs = (
        P(("dp", "tensor"), None),
        P(("dp", "tensor"), None),
        P(),
        P(),
        P(),
        P(),
        P(),
        P("dp", "tensor"),
        P("dp", "tensor"),
        P("dp", "tensor"),
        P("tensor", "dp"),
        P("dp", "tensor"),
        P("dp", "tensor"),
        P("dp", "tensor"),
        P("tensor", "dp"),
        P("dp", "tensor"),
        P("dp", "tensor"),
        P("tensor", "dp"),
        P("dp", "tensor"),
        P("dp", "tensor"),
        P("tensor", "dp"),
    )
    return jax.shard_map(body, mesh=mesh, in_specs=in_specs, out_specs=out_specs, check_vma=False)
```

```python
import functools

import jax
import jax.numpy as jnp
from jax import lax
from jax.experimental import pallas as pl
from jax.experimental.pallas import tpu as pltpu
from jax.sharding import PartitionSpec as P

HEAD_DIM = 64
WINDOW = 128
EPS = 1e-06
VMEM_LIMIT = 60 * 1024 * 1024
f32 = jnp.float32
bf16 = jnp.bfloat16


def pair_swap(values):
    return lax.ppermute(values, "tensor", [(0, 1), (1, 0)])


def halving_sum(values, order):
    parts = lax.axis_size("dp")
    place = lax.axis_index("dp")
    bits = list(range(len(order) - 1, -1, -1))
    held = values.reshape((2,) * len(bits) + (values.shape[0] // parts, values.shape[1]))
    held = held.astype(jnp.bfloat16)
    for step, bit in enumerate(order):
        axis = bits.index(bit)
        bits.remove(bit)
        mine = (place >> bit) & 1
        keep = lax.dynamic_index_in_dim(held, mine, axis, keepdims=False)
        send = lax.dynamic_index_in_dim(held, 1 - mine, axis, keepdims=False)
        got = lax.ppermute(send, "dp", [(i, i ^ (1 << bit)) for i in range(parts)])
        held = keep.astype(jnp.float32) + got.astype(jnp.float32)
        if step < len(order) - 1:
            held = held.astype(jnp.bfloat16)
    return held


def butterfly_sum(values):
    parts = lax.axis_size("dp")
    values = values + pair_swap(values)
    for bit in range(parts.bit_length() - 1):
        values = values + lax.ppermute(values, "dp", [(i, i ^ (1 << bit)) for i in range(parts)])
    return values


PARTS = 16
LANES = ((0, 1, 2, 3), (1, 2, 0, 3), (2, 0, 1, 3))
RIDES = (1, 2, 0)


def insert(number, bit, value):
    low = number & ((1 << bit) - 1)
    return ((number - low) << 1) | (value << bit) | low


def after(token, values):
    return lax.optimization_barrier((values, token))[0]


def block_rows(index, block):
    return pl.ds(pl.multiple_of(index * block, 16), block)


def swap_bit(values, bit):
    parts = lax.axis_size("dp")
    return lax.ppermute(values, "dp", [(i, i ^ (1 << bit)) for i in range(parts)])


def my_bit(bit):
    return lax.shift_right_logical(lax.axis_index("dp"), bit) & 1


def mm(left, right, left_dim=1, right_dim=0):
    return lax.dot_general(
        left, right, (((left_dim,), (right_dim,)), ((), ())), preferred_element_type=f32
    )


def split_low(values):
    high = values.astype(bf16)
    return high, (values - high.astype(f32)).astype(bf16)


def sigmoid(values):
    return 1.0 / (1.0 + jnp.exp(-values))


def row_factor(values):
    return lax.rsqrt(jnp.mean(values * values, axis=-1, keepdims=True) + EPS)


def picks(index_ref, length):
    rows = lax.broadcasted_iota(jnp.int32, (length, index_ref.shape[1]), 0)
    return jnp.where(rows == index_ref[...], 1.0, 0.0).astype(bf16)


def head_masks(width):
    lanes = lax.shift_right_logical(lax.broadcasted_iota(jnp.int32, (1, width), 1), 6)
    return [jnp.where(lanes == head, 1.0, 0.0).astype(f32) for head in range(width // HEAD_DIM)]


def stack_heads(values, masks):
    return jnp.concatenate([values * mask.astype(values.dtype) for mask in masks], axis=0)


def unstack_heads(values, masks):
    rows = values.shape[0] // len(masks)
    total = values[:rows] * masks[0]
    for head in range(1, len(masks)):
        total = total + values[head * rows : (head + 1) * rows] * masks[head]
    return total


def softmax_rows(scores, axis):
    exponent = jnp.exp(scores - jnp.max(scores, axis=axis, keepdims=True))
    return exponent * (1.0 / jnp.sum(exponent, axis=axis, keepdims=True))


def window_start(block, length):
    start = jnp.clip(block * WINDOW - WINDOW, 0, length - 3 * WINDOW)
    return pl.multiple_of(start, WINDOW)


def attn_forward_kernel(
    own_ref,
    other_ref,
    gain_ref,
    route_query_ref,
    route_key_ref,
    query_index_ref,
    key_index_ref,
    wq_ref,
    wk_ref,
    wv_ref,
    wo_ref,
    hq_ref,
    hk_ref,
    hv_ref,
    ho_ref,
    partial_ref,
    input_ref,
    q_ref,
    k_ref,
    v_ref,
    result_ref,
    query_rows_ref,
    key_raw_ref,
    key_rows_ref,
    qh_ref,
    kh_ref,
    vh_ref,
    raw_ref,
    heavy_result_ref,
    pick_ref,
):
    side = lax.axis_index("tensor")
    half = own_ref.shape[0]
    length = 2 * half
    tile = 256
    for ref, place in ((own_ref, side), (other_ref, 1 - side)):
        for start in range(0, half, tile):
            values = ref[start : start + tile, :].astype(f32)
            normed = values * row_factor(values) * gain_ref[...]
            rows = pl.ds(pl.multiple_of(place * half + start, tile), tile)
            input_ref[rows, :] = normed.astype(bf16)
    routed = query_index_ref.shape[1]
    pick_ref[:, :routed] = picks(query_index_ref, length)
    pick_ref[:, routed:] = picks(key_index_ref, length)
    picked = mm(pick_ref[...], input_ref[...], 0, 0)
    query_rows = picked[:routed]
    key_raw = picked[routed:]
    query_score = sigmoid(jnp.sum(query_rows * route_query_ref[...], axis=-1, keepdims=True))
    key_score = sigmoid(jnp.sum(key_raw * route_key_ref[...], axis=-1, keepdims=True))
    query_rows_ref[...] = query_rows.astype(bf16)
    key_raw_ref[...] = key_raw.astype(bf16)
    key_rows_ref[...] = (key_score * key_raw).astype(bf16)
    qh_ref[...] = mm(query_rows_ref[...], hq_ref[...]).astype(bf16)
    kh_ref[...] = mm(key_rows_ref[...], hk_ref[...]).astype(bf16)
    vh_ref[...] = mm(key_rows_ref[...], hv_ref[...]).astype(bf16)
    pair = 2 * HEAD_DIM
    pair_masks = head_masks(pair)
    for start in range(0, qh_ref.shape[1], pair):
        cols = slice(start, start + pair)
        stacked = stack_heads(qh_ref[:, cols] * (HEAD_DIM**-0.5), pair_masks)
        probs = softmax_rows(mm(stacked, kh_ref[:, cols], 1, 1), -1)
        raw_ref[:, cols] = unstack_heads(mm(probs.astype(bf16), vh_ref[:, cols]), pair_masks)
    heavy_result_ref[...] = (query_score * raw_ref[...]).astype(bf16)
    high, low = split_low(mm(heavy_result_ref[...], ho_ref[...]))

    for start in range(0, length, tile):
        rows = slice(start, start + tile)
        q_ref[rows, :] = mm(input_ref[rows, :], wq_ref[...]).astype(bf16)
        k_ref[rows, :] = mm(input_ref[rows, :], wk_ref[...]).astype(bf16)
        v_ref[rows, :] = mm(input_ref[rows, :], wv_ref[...]).astype(bf16)

    masks = head_masks(q_ref.shape[1])
    heads = len(masks)
    gap = lax.broadcasted_iota(jnp.int32, (WINDOW, 3 * WINDOW), 0) - lax.broadcasted_iota(
        jnp.int32, (WINDOW, 3 * WINDOW), 1
    )

    def one_block(block, carry):
        rows = pl.ds(pl.multiple_of(block * WINDOW, WINDOW), WINDOW)
        start = window_start(block, length)
        keys = pl.ds(start, 3 * WINDOW)
        stacked = stack_heads(q_ref[rows, :] * (HEAD_DIM**-0.5), masks)
        scores = mm(stacked, k_ref[keys, :], 1, 1)
        near = jnp.abs(gap + (block * WINDOW - start)) < WINDOW
        bias = jnp.where(near, 0.0, -1e30)
        probs = softmax_rows(scores + jnp.concatenate([bias] * heads, axis=0), -1)
        out = unstack_heads(mm(probs.astype(bf16), v_ref[keys, :]), masks)
        result_ref[rows, :] = out.astype(bf16)
        return carry

    lax.fori_loop(0, length // WINDOW, one_block, 0)
    for start in range(0, length, tile):
        rows = slice(start, start + tile)
        pick = pick_ref[rows, :routed]
        partial_ref[rows, :] = (
            mm(result_ref[rows, :], wo_ref[...]) + (mm(pick, high) + mm(pick, low))
        ).astype(bf16)


def gelu_parts(values):
    density = jnp.exp(-0.5 * values * values) * 0.3989422804014327
    below = 0.5 * (1.0 + lax.erf(values * 0.7071067811865476))
    return values * below, below + values * density


def ffn_heavy_kernel(
    own_ref,
    other_ref,
    mine_ref,
    got_ref,
    cot_own_ref,
    cot_other_ref,
    gain_ref,
    route_ref,
    index_ref,
    hg_ref,
    hu_ref,
    hd_ref,
    send_x_ref,
    send_y_ref,
    send_z_ref,
    middle_ref,
    input_ref,
    cot_ref,
    pick_ref,
    down_ref,
    back_ref,
    route_grad_ref,
):
    side = lax.axis_index("tensor")
    half = own_ref.shape[0]
    length = 2 * half
    tile = 256
    for ref, cot, place in ((own_ref, cot_own_ref, side), (other_ref, cot_other_ref, 1 - side)):
        for start in range(0, half, tile):
            rows = pl.ds(pl.multiple_of(place * half + start, tile), tile)
            branch = mine_ref[rows, :].astype(f32) + got_ref[rows, :].astype(f32)
            middle = ref[start : start + tile, :].astype(f32) + branch
            middle_ref[rows, :] = middle
            input_ref[rows, :] = (middle * row_factor(middle) * gain_ref[...]).astype(bf16)
            cot_ref[rows, :] = cot[start : start + tile, :]
    pick_ref[...] = picks(index_ref, length)
    ffn_rows = mm(pick_ref[...], input_ref[...], 0, 0)
    rows_low = ffn_rows.astype(bf16)
    cot_rows = mm(pick_ref[...], cot_ref[...], 0, 0).astype(bf16)
    routed, model = rows_low.shape
    send_x_ref[:, :model] = rows_low
    send_y_ref[:, :model] = rows_low
    send_z_ref[:, :model] = cot_rows
    score = sigmoid(jnp.sum(ffn_rows * route_ref[...], axis=-1, keepdims=True))
    heavy_width = hg_ref.shape[1]
    chunk = 512
    score_grad = 0.0
    down = 0.0
    rows_grad = 0.0
    for start in range(0, heavy_width, chunk):
        cols = slice(start, start + chunk)
        out_cols = slice(model + start, model + start + chunk)
        gate = mm(rows_low, hg_ref[:, cols])
        up = mm(rows_low, hu_ref[:, cols])
        act_grad = mm(cot_rows, hd_ref[cols, :], 1, 1)
        gelu, slope = gelu_parts(gate)
        mixed = gelu * up
        score_grad = score_grad + jnp.sum(act_grad * mixed, axis=-1, keepdims=True)
        scaled = score * act_grad
        act = (score * mixed).astype(bf16)
        gate_grad = (scaled * up * slope).astype(bf16)
        up_grad = (scaled * gelu).astype(bf16)
        send_x_ref[:, out_cols] = gate_grad
        send_y_ref[:, out_cols] = up_grad
        send_z_ref[:, out_cols] = act
        down = down + mm(act, hd_ref[cols, :])
        rows_grad = rows_grad + mm(gate_grad, hg_ref[:, cols], 1, 1)
        rows_grad = rows_grad + mm(up_grad, hu_ref[:, cols], 1, 1)
    logit_grad = score * (1.0 - score) * score_grad
    route_grad_ref[...] = jnp.sum(ffn_rows * logit_grad, axis=0, keepdims=True)
    rows_grad = rows_grad + logit_grad * route_ref[...]
    down_ref[:routed, :], down_ref[routed:, :] = split_low(down)
    back_ref[:routed, :], back_ref[routed:, :] = split_low(rows_grad)


def ffn_light_kernel(
    middle_ref,
    input_ref,
    cot_ref,
    pick_ref,
    down_ref,
    rows_back_ref,
    wg_ref,
    wu_ref,
    wd_ref,
    back_ref,
    block_own_ref,
    block_send_ref,
    *rest,
):
    lane_refs = rest[:-3]
    light_grad_ref, act_ref, mix_ref = rest[-3:]
    side = lax.axis_index("tensor")
    half = block_own_ref.shape[0]
    tile = 256
    width = wg_ref.shape[1]
    for first in range(0, 2):
        place = side if first == 0 else 1 - side
        for start in range(0, half, tile):
            rows = pl.ds(pl.multiple_of(place * half + start, tile), tile)
            piece = slice(start, start + tile)
            gate = mm(input_ref[rows, :], wg_ref[...])
            up = mm(input_ref[rows, :], wu_ref[...])
            act_grad = mm(cot_ref[rows, :], wd_ref[...], 1, 1)
            gelu, slope = gelu_parts(gate)
            act_ref[rows, :] = (gelu * up).astype(bf16)
            mix_ref[rows, :width] = (act_grad * up * slope).astype(bf16)
            mix_ref[rows, width:] = (act_grad * gelu).astype(bf16)
            pick = jnp.concatenate([pick_ref[rows, :]] * 2, axis=1)
            branch = mm(act_ref[rows, :], wd_ref[...]) + mm(pick, down_ref[...])
            if first == 0:
                block_own_ref[piece, :] = middle_ref[rows, :] + branch
            else:
                block_send_ref[piece, :] = branch.astype(bf16)
            back_ref[rows, :] = (
                mm(mix_ref[rows, :width], wg_ref[...], 1, 1)
                + mm(mix_ref[rows, width:], wu_ref[...], 1, 1)
                + mm(pick, rows_back_ref[...])
            ).astype(bf16)
    light_grad_ref[:, : 2 * width] = mm(input_ref[...], mix_ref[...], 0, 0).astype(bf16)
    light_grad_ref[:, 2 * width :] = mm(cot_ref[...], act_ref[...], 0, 0).astype(bf16)
    for lane in range(len(lane_refs) // 2):
        lane_split(lane, lane_refs, 0, light_grad_ref, lane * width, (lane + 1) * width)


def lane_split(lane, lane_refs, left, grad_ref, first, last):
    bit = LANES[lane][0]
    mine = my_bit(bit)
    block = grad_ref.shape[0] // PARTS
    keep_ref, send_ref = lane_refs[lane], lane_refs[len(LANES) + lane]
    for p in range(PARTS // 2):
        rows = slice(p * block, (p + 1) * block)
        cols = slice(left, left + last - first)
        for ref, value in ((keep_ref, mine), (send_ref, 1 - mine)):
            ref[rows, cols] = grad_ref[block_rows(insert(p, bit, value), block), first:last]


def attn_backward_kernel(
    cot_own_ref,
    cot_other_ref,
    middle_ref,
    mine_ref,
    got_ref,
    gain_ffn_ref,
    route_query_ref,
    route_key_ref,
    query_index_ref,
    key_index_ref,
    wo_ref,
    hq_ref,
    hk_ref,
    hv_ref,
    ho_ref,
    result_ref,
    query_rows_ref,
    key_raw_ref,
    key_rows_ref,
    qh_ref,
    kh_ref,
    vh_ref,
    raw_ref,
    heavy_result_ref,
    own_middle_ref,
    out_ref,
    grad_ref,
    back_high_ref,
    back_low_ref,
    pick_ref,
    small_ref,
    low_ref,
):
    side = lax.axis_index("tensor")
    half = cot_own_ref.shape[0]
    length = 2 * half
    tile = 256
    scale = HEAD_DIM**-0.5
    heavy = qh_ref.shape[1]
    gain_ffn_grad = 0.0
    for cot, place, owned in ((cot_own_ref, side, True), (cot_other_ref, 1 - side, False)):
        for start in range(0, half, tile):
            rows = pl.ds(pl.multiple_of(place * half + start, tile), tile)
            piece = slice(start, start + tile)
            normed_grad = mine_ref[rows, :].astype(f32) + got_ref[rows, :].astype(f32)
            middle = middle_ref[rows, :]
            factor = row_factor(middle)
            scaled = factor * middle
            gain_ffn_grad = gain_ffn_grad + jnp.sum(scaled * normed_grad, axis=0, keepdims=True)
            gained = gain_ffn_ref[...] * normed_grad
            inner = jnp.mean(scaled * gained, axis=-1, keepdims=True)
            grad = cot[piece, :].astype(f32) + factor * (gained - scaled * inner)
            if owned:
                own_middle_ref[piece, :] = grad
            low_ref[rows, :] = grad.astype(bf16)
    for start in range(0, length, tile):
        rows = slice(start, start + tile)
        out_ref[rows, :] = mm(low_ref[rows, :], wo_ref[...], 1, 1).astype(bf16)
    grad_ref[:, 4 * heavy :] = mm(low_ref[...], result_ref[...], 0, 0).astype(bf16)

    routed = query_index_ref.shape[1]
    pick_ref[:, :routed] = picks(query_index_ref, length)
    pick_ref[:, routed:] = picks(key_index_ref, length)
    query_rows = query_rows_ref[...].astype(f32)
    key_raw = key_raw_ref[...].astype(f32)
    query_score = sigmoid(jnp.sum(query_rows * route_query_ref[...], axis=-1, keepdims=True))
    key_score = sigmoid(jnp.sum(key_raw * route_key_ref[...], axis=-1, keepdims=True))
    mid_rows = mm(pick_ref[:, :routed], low_ref[...], 0, 0).astype(bf16)
    grad_ref[:, 3 * heavy : 4 * heavy] = mm(mid_rows, heavy_result_ref[...], 0, 0).astype(bf16)
    heavy_out_grad = mm(mid_rows, ho_ref[...], 1, 1).astype(bf16)
    query_score_grad = jnp.sum(
        heavy_out_grad.astype(f32) * raw_ref[...], axis=-1, keepdims=True
    )
    raw_high, raw_low = split_low(query_score * heavy_out_grad.astype(f32))
    pair = 2 * HEAD_DIM
    pair_masks = head_masks(pair)
    stacked_score = jnp.concatenate([query_score] * 2, axis=0)
    q_parts, k_parts, v_parts = [], [], []
    for start in range(0, heavy, pair):
        cols = slice(start, start + pair)
        stacked = stack_heads(qh_ref[:, cols] * scale, pair_masks)
        probs = softmax_rows(mm(stacked, kh_ref[:, cols], 1, 1), -1)
        grad_stacked = stack_heads(heavy_out_grad[:, cols], pair_masks)
        probs_grad = stacked_score * mm(grad_stacked, vh_ref[:, cols], 1, 1)
        inner = jnp.sum(probs * probs_grad, axis=-1, keepdims=True)
        score_grad = (probs * (probs_grad - inner)).astype(bf16)
        probs_low = probs.astype(bf16)
        q_parts.append(unstack_heads(mm(score_grad, kh_ref[:, cols]) * scale, pair_masks))
        k_parts.append(mm(score_grad, stacked, 0, 0))
        v_parts.append(
            mm(probs_low, stack_heads(raw_high[:, cols], pair_masks), 0, 0)
            + mm(probs_low, stack_heads(raw_low[:, cols], pair_masks), 0, 0)
        )
    query_heavy_grad = jnp.concatenate(q_parts, axis=1).astype(bf16)
    key_heavy_grad = jnp.concatenate(k_parts, axis=1).astype(bf16)
    value_heavy_grad = jnp.concatenate(v_parts, axis=1).astype(bf16)
    grad_ref[:, :heavy] = mm(query_rows_ref[...], query_heavy_grad, 0, 0).astype(bf16)
    grad_ref[:, heavy : 2 * heavy] = mm(key_rows_ref[...], key_heavy_grad, 0, 0).astype(bf16)
    grad_ref[:, 2 * heavy : 3 * heavy] = mm(
        key_rows_ref[...], value_heavy_grad, 0, 0
    ).astype(bf16)
    key_rows_grad = mm(key_heavy_grad, hk_ref[...], 1, 1) + mm(
        value_heavy_grad, hv_ref[...], 1, 1
    )
    key_logit_grad = (
        key_score * (1.0 - key_score) * jnp.sum(key_rows_grad * key_raw, axis=-1, keepdims=True)
    )
    query_logit_grad = query_score * (1.0 - query_score) * query_score_grad
    key_raw_grad = key_score * key_rows_grad + key_logit_grad * route_key_ref[...]
    query_rows_grad = mm(query_heavy_grad, hq_ref[...], 1, 1)
    query_rows_grad = query_rows_grad + query_logit_grad * route_query_ref[...]
    small_ref[...] = jnp.zeros_like(small_ref)
    small_ref[1:2, :] = 0.5 * gain_ffn_grad
    small_ref[2:3, :] = jnp.sum(query_rows * query_logit_grad, axis=0, keepdims=True)
    small_ref[3:4, :] = jnp.sum(key_raw * key_logit_grad, axis=0, keepdims=True)
    high, low = split_low(jnp.concatenate([query_rows_grad, key_raw_grad], axis=0))
    back_high_ref[...] = high
    back_low_ref[...] = low


def heavy_split(cols, lane):
    tiles = cols // 128
    cuts = [0, (tiles + 2) // 3, 2 * ((tiles + 2) // 3), tiles]
    return cuts[lane] * 128, cuts[lane + 1] * 128


def light_backward_kernel(
    own_ref,
    other_ref,
    wq_ref,
    wk_ref,
    wv_ref,
    input_ref,
    q_ref,
    k_ref,
    v_ref,
    out_ref,
    heavy_grad_ref,
    back_high_ref,
    back_low_ref,
    pick_ref,
    own_back_ref,
    send_ref,
    small_ref,
    *rest,
):
    grad_refs = rest[:-6]
    light_grad_ref, kt_ref, qt_grad_ref, k_grad_ref, v_grad_ref, mixed_ref = rest[-6:]
    side = lax.axis_index("tensor")
    half = own_ref.shape[0]
    length = 2 * half
    tile = 256
    scale = HEAD_DIM**-0.5
    kt_ref[...] = k_ref[...].T
    k_grad_ref[...] = jnp.zeros_like(k_grad_ref)
    v_grad_ref[...] = jnp.zeros_like(v_grad_ref)
    masks = head_masks(q_ref.shape[1])
    heads = len(masks)
    gap = lax.broadcasted_iota(jnp.int32, (3 * WINDOW, WINDOW), 1) - lax.broadcasted_iota(
        jnp.int32, (3 * WINDOW, WINDOW), 0
    )

    def one_block(block, carry):
        first = pl.multiple_of(block * WINDOW, WINDOW)
        rows = pl.ds(first, WINDOW)
        start = window_start(block, length)
        keys = pl.ds(start, 3 * WINDOW)
        stacked = stack_heads(q_ref[rows, :] * scale, masks)
        grad_stacked = stack_heads(out_ref[rows, :], masks)
        near = jnp.abs(gap + (block * WINDOW - start)) < WINDOW
        bias = jnp.where(near, 0.0, -1e30)
        scores = mm(k_ref[keys, :], stacked, 1, 1)
        probs = softmax_rows(scores + jnp.concatenate([bias] * heads, axis=1), 0)
        probs_grad = mm(v_ref[keys, :], grad_stacked, 1, 1)
        inner = jnp.sum(probs * probs_grad, axis=0, keepdims=True)
        score_grad = (probs * (probs_grad - inner)).astype(bf16)
        k_grad_ref[keys, :] += mm(score_grad, stacked)
        v_grad_ref[keys, :] += mm(probs.astype(bf16), grad_stacked)
        spread = mm(kt_ref[:, keys], score_grad) * scale
        for head in range(heads):
            lanes = slice(head * HEAD_DIM, (head + 1) * HEAD_DIM)
            qt_grad_ref[lanes, rows] = spread[lanes, head * WINDOW : (head + 1) * WINDOW]
        return carry

    lax.fori_loop(0, length // WINDOW, one_block, 0)
    light = q_ref.shape[1]
    mixed_ref[:, :light] = qt_grad_ref[...].T.astype(bf16)
    mixed_ref[:, light : 2 * light] = k_grad_ref[...].astype(bf16)
    mixed_ref[:, 2 * light :] = v_grad_ref[...].astype(bf16)
    heavy_cols = heavy_grad_ref.shape[1]
    light_grad = mm(input_ref[...], mixed_ref[...], 0, 0).astype(bf16)
    gain_attn_grad = 0.0
    for ref, place, owned in ((own_ref, side, True), (other_ref, 1 - side, False)):
        for start in range(0, half, tile):
            rows = pl.ds(pl.multiple_of(place * half + start, tile), tile)
            piece = slice(start, start + tile)
            pick = pick_ref[rows, :]
            back = (
                mm(mixed_ref[rows, :light], wq_ref[...], 1, 1)
                + mm(mixed_ref[rows, light : 2 * light], wk_ref[...], 1, 1)
                + mm(mixed_ref[rows, 2 * light :], wv_ref[...], 1, 1)
                + (mm(pick, back_high_ref[...]) + mm(pick, back_low_ref[...]))
            )
            values = ref[piece, :].astype(f32)
            gain_attn_grad = gain_attn_grad + jnp.sum(
                values * row_factor(values) * back, axis=0, keepdims=True
            )
            if owned:
                own_back_ref[piece, :] = back
            else:
                send_ref[piece, :] = back.astype(bf16)
    small_ref[...] = gain_attn_grad
    if len(grad_refs) == 1:
        grad_refs[0][:, :heavy_cols] = heavy_grad_ref[...]
        grad_refs[0][:, heavy_cols:] = light_grad
        return
    light_grad_ref[...] = light_grad
    for lane in range(len(LANES)):
        left, right = heavy_split(heavy_cols, lane)
        lane_split(lane, grad_refs, 0, heavy_grad_ref, left, right)
        lane_split(lane, grad_refs, right - left, light_grad_ref, lane * light, (lane + 1) * light)


def join_kernel(lane, send_ref, got_ref, light_ref, next_keep_ref, next_send_ref, full_ref):
    model, heavy = full_ref.shape
    tall = next_send_ref.shape[0]
    light = light_ref.shape[1]
    for wrap in range(light_ref.shape[0] // tall):
        cols = slice(heavy + wrap * light, heavy + (wrap + 1) * light)
        next_send_ref[:, cols] = light_ref[wrap * tall : (wrap + 1) * tall, :]
    left = jnp.concatenate([send_ref[:, :model], got_ref[:, :model]], axis=0)
    right = jnp.concatenate([send_ref[:, model:], got_ref[:, model:]], axis=0)
    full_ref[...] = mm(left, right, 0, 0).astype(bf16)
    first, second = LANES[lane][:2]
    position = second - (1 if first < second else 0)
    mine, next_mine = my_bit(first), my_bit(second)
    block = model // PARTS
    for q in range(PARTS // 4):
        rows = slice(q * block, (q + 1) * block)
        for ref, value in ((next_keep_ref, next_mine), (next_send_ref, 1 - next_mine)):
            p = insert(q, position, value)
            ref[rows, :heavy] = full_ref[block_rows(insert(p, first, mine), block), :]


def fold_kernel(bit, position, block, *refs):
    next_keep_ref, next_send_ref, sum_ref = refs[-3:]
    left = 0
    for keep_ref, got_ref in zip(refs[:-3:2], refs[1:-3:2]):
        rows, width = keep_ref.shape
        tall = min(rows, got_ref.shape[0])
        skip = got_ref.shape[1] - width * (rows // tall) if tall < rows else 0
        for wrap in range(rows // tall):
            piece = slice(wrap * tall, (wrap + 1) * tall)
            got = got_ref[:, skip + wrap * width : skip + (wrap + 1) * width]
            both = keep_ref[piece, :].astype(f32) + got.astype(f32)
            sum_ref[piece, left : left + width] = both.astype(bf16)
        left += width
    mine = my_bit(bit)
    for q in range(next_keep_ref.shape[0] // block):
        rows = slice(q * block, (q + 1) * block)
        next_keep_ref[rows, :] = sum_ref[block_rows(insert(q, position, mine), block), :]
        next_send_ref[rows, :] = sum_ref[block_rows(insert(q, position, 1 - mine), block), :]


def last_fold_kernel(bit, *refs):
    lanes = (len(refs) - 3) // 2
    keep_ref, send_ref, sum_ref = refs[-3:]
    left = 0
    for lane in range(lanes):
        width = refs[lane].shape[1]
        both = refs[lane][...].astype(f32) + refs[lanes + lane][...].astype(f32)
        sum_ref[:, left : left + width] = both
        left += width
    mine = my_bit(bit)
    block = keep_ref.shape[0]
    keep_ref[...] = sum_ref[block_rows(mine, block), :]
    send_ref[...] = sum_ref[block_rows(1 - mine, block), :].astype(bf16)


def fold(bit, position, block, *pairs):
    rows = pairs[0].shape[0]
    width = sum(pair.shape[1] for pair in pairs[::2])
    return whole(
        functools.partial(fold_kernel, bit, position, block),
        "fold",
        2,
        [((rows // 2, width), bf16)] * 2,
        [((rows, width), bf16)],
        *pairs,
    )


def last_fold(bit, keeps, gots):
    rows = keeps[0].shape[0]
    width = sum(keep.shape[1] for keep in keeps)
    return whole(
        functools.partial(last_fold_kernel, bit),
        "last_fold",
        2,
        [((rows // 2, width), f32), ((rows // 2, width), bf16)],
        [((rows, width), f32)],
        *keeps,
        *gots,
    )


def whole(kernel, name, micros, outs, scratch, *operands):
    return pl.pallas_call(
        kernel,
        name=name,
        out_shape=[jax.ShapeDtypeStruct(shape, dtype) for shape, dtype in outs],
        in_specs=[pl.BlockSpec(memory_space=pltpu.VMEM)] * len(operands),
        out_specs=[pl.BlockSpec(memory_space=pltpu.VMEM)] * len(outs),
        scratch_shapes=[pltpu.VMEM(shape, dtype) for shape, dtype in scratch],
        compiler_params=pltpu.CompilerParams(vmem_limit_bytes=VMEM_LIMIT),
        cost_estimate=pl.CostEstimate(
            flops=micros * 10**9, transcendentals=0, bytes_accessed=micros * 10**6
        ),
    )(*operands)


def body(
    tokens,
    cotangent,
    gain_attn,
    gain_ffn,
    route_query,
    route_key,
    route_ffn,
    light_query,
    light_key,
    light_value,
    light_out,
    heavy_query,
    heavy_key,
    heavy_value,
    heavy_out,
    light_gate,
    light_up,
    light_down,
    heavy_gate,
    heavy_up,
    heavy_down,
    query_index,
    key_index,
    ffn_index,
):
    half, width = tokens.shape
    length = 2 * half
    routed = query_index.shape[1]
    light = light_query.shape[1]
    heavy = heavy_query.shape[1]
    light_ff = light_gate.shape[1]
    heavy_ff = heavy_gate.shape[1]
    gain_attn, gain_ffn, route_query, route_key, route_ffn = (
        item.reshape(1, -1) for item in (gain_attn, gain_ffn, route_query, route_key, route_ffn)
    )
    other_tokens = pair_swap(tokens)
    other_cotangent = pair_swap(cotangent)
    attn_weights = (
        light_query,
        light_key,
        light_value,
        light_out,
        heavy_query,
        heavy_key,
        heavy_value,
        heavy_out,
    )
    attn_partial, *saved = whole(
        attn_forward_kernel,
        "attn_forward",
        16,
        [((length, width), bf16)] * 2
        + [((length, light), bf16)] * 4
        + [((routed, width), bf16)] * 3
        + [((routed, heavy), bf16)] * 3
        + [((routed, heavy), f32), ((routed, heavy), bf16)],
        [((length, 2 * routed), bf16)],
        tokens,
        other_tokens,
        gain_attn,
        route_query,
        route_key,
        query_index,
        key_index,
        *attn_weights,
    )
    tuned = lax.axis_size("dp") == PARTS
    *sends, middle, ffn_input, cot_rows, ffn_pick, down, rows_back, route_ffn_grad = whole(
        ffn_heavy_kernel,
        "ffn_heavy",
        12,
        [((routed, width + heavy_ff), bf16)] * 3
        + [
            ((length, width), f32),
            ((length, width), bf16),
            ((length, width), bf16),
            ((length, routed), bf16),
            ((2 * routed, width), bf16),
            ((2 * routed, width), bf16),
            ((1, width), f32),
        ],
        [],
        tokens,
        other_tokens,
        attn_partial,
        pair_swap(attn_partial),
        cotangent,
        other_cotangent,
        gain_ffn,
        route_ffn,
        ffn_index,
        heavy_gate,
        heavy_up,
        heavy_down,
    )
    if tuned:
        gots = [swap_bit(send, order[0]) for send, order in zip(sends, LANES)]
    ffn_back, block_own, block_send, *light_parts = whole(
        ffn_light_kernel,
        "ffn_light",
        12,
        [((length, width), bf16), ((half, width), f32), ((half, width), bf16)]
        + ([((width // 2, light_ff), bf16)] * 6 if tuned else [((width, 3 * light_ff), bf16)]),
        ([((width, 3 * light_ff), bf16)] if tuned else [])
        + [((length, light_ff), bf16), ((length, 2 * light_ff), bf16)],
        middle,
        ffn_input,
        cot_rows,
        ffn_pick,
        down,
        rows_back,
        light_gate,
        light_up,
        light_down,
    )
    back_got = pair_swap(ffn_back)
    if tuned:
        light_keeps = light_parts[:3]
        light_sends = light_parts[3:]
        token = ffn_back
        ffn_keeps, ffn_sends = [], []
        for lane in range(3):
            keep, send = whole(
                functools.partial(join_kernel, lane),
                "join",
                3,
                [((width // 4, heavy_ff), bf16), ((width // 4, heavy_ff + 2 * light_ff), bf16)],
                [((width, heavy_ff), bf16)],
                after(token, sends[lane]),
                gots[lane],
                light_sends[RIDES[lane]],
            )
            token = keep
            ffn_keeps.append(keep)
            ffn_sends.append(send)
        ffn_gots = [swap_bit(send, order[1]) for send, order in zip(ffn_sends, LANES)]
        ffn_back = after(token, ffn_back)
    attn_input, q_light, k_light, v_light, *routed_saved = saved
    own_middle, out_back, heavy_grad, back_high, back_low, pick, small = whole(
        attn_backward_kernel,
        "attn_backward",
        10,
        [
            ((half, width), f32),
            ((length, light), bf16),
            ((width, 4 * heavy + light), bf16),
            ((2 * routed, width), bf16),
            ((2 * routed, width), bf16),
            ((length, 2 * routed), bf16),
            ((8, width), f32),
        ],
        [((length, width), bf16)],
        cotangent,
        other_cotangent,
        middle,
        ffn_back,
        back_got,
        gain_ffn,
        route_query,
        route_key,
        query_index,
        key_index,
        *attn_weights[3:],
        *routed_saved,
    )
    block = width // lax.axis_size("dp")
    own_back, back_send, gain_attn_grad, *attn_grads = whole(
        light_backward_kernel,
        "light_backward",
        16,
        [((half, width), f32), ((half, width), bf16), ((1, width), f32)]
        + (
            [
                ((width // 2, right - left + light), bf16)
                for left, right in [heavy_split(4 * heavy + light, lane) for lane in range(3)]
            ]
            * 2
            if tuned
            else [((width, 4 * heavy + 4 * light), bf16)]
        ),
        [
            ((width, 3 * light), bf16),
            ((light, length), bf16),
            ((light, length), f32),
            ((length, light), f32),
            ((length, light), f32),
            ((length, 3 * light), bf16),
        ],
        tokens,
        other_tokens,
        *attn_weights[:3],
        attn_input,
        q_light,
        k_light,
        v_light,
        out_back,
        heavy_grad,
        back_high,
        back_low,
        pick,
    )
    if tuned:
        attn_keeps = attn_grads[:3]
        attn_gots = [swap_bit(send, order[0]) for send, order in zip(attn_grads[3:], LANES)]
        token = gain_attn_grad

        def middle_stage(stage, token, keeps, *rest):
            next_keeps, next_gots = [], []
            for lane, order in enumerate(LANES):
                left = sorted(order[stage:])
                keep, send = fold(
                    order[stage],
                    left.index(order[stage]),
                    block,
                    after(token, keeps[lane]),
                    *(item[lane] for item in rest),
                )
                token = keep
                next_keeps.append(keep)
                next_gots.append(swap_bit(send, order[stage]))
            return token, next_keeps, next_gots

        token, ffn_keeps, ffn_gots_next = middle_stage(2, token, ffn_keeps, ffn_gots)
        token, attn_keeps, attn_gots = middle_stage(
            1, token, attn_keeps, attn_gots, light_keeps, [ffn_gots[RIDES.index(i)] for i in range(3)]
        )
        ffn_keep, ffn_send = last_fold(3, [after(token, ffn_keeps[0]), *ffn_keeps[1:]], ffn_gots_next)
        ffn_got = swap_bit(ffn_send, 3)
        small = after(ffn_keep, small)
    block_out = (block_own + pair_swap(block_send).astype(f32)).astype(bf16)
    normed_grad = own_back + pair_swap(back_send).astype(f32)
    own_tokens = tokens.astype(f32)
    factor = row_factor(own_tokens)
    scaled = own_tokens * factor
    gained = gain_attn * normed_grad
    inner = jnp.mean(scaled * gained, axis=-1, keepdims=True)
    input_grad = (own_middle + factor * (gained - scaled * inner)).astype(bf16)
    small = small + jnp.pad(route_ffn_grad, ((4, 3), (0, 0)))
    small_summed = butterfly_sum(small + jnp.pad(gain_attn_grad, ((0, 7), (0, 0))))

    if tuned:
        token, attn_keeps, attn_gots = middle_stage(2, small_summed, attn_keeps, attn_gots)
        attn_keep, attn_send = last_fold(3, [after(token, attn_keeps[0]), *attn_keeps[1:]], attn_gots)
        attn_got = swap_bit(attn_send, 3)
        ffn_sum = ffn_keep + ffn_got.astype(f32)
        attn_sum = attn_keep + attn_got.astype(f32)
        hg, hu, hd = jnp.split(ffn_sum, 3, axis=1)
        heavies, lights, ffn_lights, left = [], [], [], 0
        for lane in range(3):
            first, last = heavy_split(4 * heavy + light, lane)
            for pieces, size in ((heavies, last - first), (lights, light), (ffn_lights, light_ff)):
                pieces.append(attn_sum[:, left : left + size])
                left += size
        heavies = jnp.concatenate(heavies, axis=1)
        lq, lk, lv = lights
        lg, lu, ld = ffn_lights
    else:
        order = list(range(lax.axis_size("dp").bit_length() - 1))
        hg, hu, hd = (
            halving_sum(mm(send[:, :width], send[:, width:], 0, 0).astype(bf16), order)
            for send in sends
        )
        lg, lu, ld = jnp.split(halving_sum(light_parts[0], order), 3, axis=1)
        attn_sum = halving_sum(attn_grads[0], order)
        heavies = attn_sum[:, : 4 * heavy + light]
        lq, lk, lv = jnp.split(attn_sum[:, 4 * heavy + light :], 3, axis=1)
    return (
        block_out,
        input_grad,
        small_summed[0],
        small_summed[1],
        small_summed[2],
        small_summed[3],
        small_summed[4],
        lq,
        lk,
        lv,
        heavies[:, 4 * heavy :].T,
        heavies[:, :heavy],
        heavies[:, heavy : 2 * heavy],
        heavies[:, 2 * heavy : 3 * heavy],
        heavies[:, 3 * heavy : 4 * heavy].T,
        lg,
        lu,
        ld.T,
        hg,
        hu,
        hd.T,
    )


def solution(mesh):
    in_specs = (
        P(("dp", "tensor"), None),
        P(("dp", "tensor"), None),
        P(),
        P(),
        P(),
        P(),
        P(),
        P(None, "tensor"),
        P(None, "tensor"),
        P(None, "tensor"),
        P("tensor", None),
        P(None, "tensor"),
        P(None, "tensor"),
        P(None, "tensor"),
        P("tensor", None),
        P(None, "tensor"),
        P(None, "tensor"),
        P("tensor", None),
        P(None, "tensor"),
        P(None, "tensor"),
        P("tensor", None),
        P("dp", None),
        P("dp", None),
        P("dp", None),
    )
    out_specs = (
        P(("dp", "tensor"), None),
        P(("dp", "tensor"), None),
        P(),
        P(),
        P(),
        P(),
        P(),
        P("dp", "tensor"),
        P("dp", "tensor"),
        P("dp", "tensor"),
        P("tensor", "dp"),
        P("dp", "tensor"),
        P("dp", "tensor"),
        P("dp", "tensor"),
        P("tensor", "dp"),
        P("dp", "tensor"),
        P("dp", "tensor"),
        P("tensor", "dp"),
        P("dp", "tensor"),
        P("dp", "tensor"),
        P("tensor", "dp"),
    )
    return jax.shard_map(body, mesh=mesh, in_specs=in_specs, out_specs=out_specs, check_vma=False)
```

```python
import functools

import jax
import jax.numpy as jnp
from jax import lax
from jax.experimental import pallas as pl
from jax.experimental.pallas import tpu as pltpu
from jax.sharding import PartitionSpec as P

HEAD_DIM = 64
WINDOW = 128
EPS = 1e-06
VMEM_LIMIT = 24 * 1024 * 1024
f32 = jnp.float32
bf16 = jnp.bfloat16


def pair_swap(values):
    return lax.ppermute(values, "tensor", [(0, 1), (1, 0)])


def halving_sum(values, order):
    parts = lax.axis_size("dp")
    place = lax.axis_index("dp")
    bits = list(range(len(order) - 1, -1, -1))
    held = values.reshape((2,) * len(bits) + (values.shape[0] // parts, values.shape[1]))
    held = held.astype(jnp.bfloat16)
    for step, bit in enumerate(order):
        axis = bits.index(bit)
        bits.remove(bit)
        mine = (place >> bit) & 1
        keep = lax.dynamic_index_in_dim(held, mine, axis, keepdims=False)
        send = lax.dynamic_index_in_dim(held, 1 - mine, axis, keepdims=False)
        got = lax.ppermute(send, "dp", [(i, i ^ (1 << bit)) for i in range(parts)])
        held = keep.astype(jnp.float32) + got.astype(jnp.float32)
        if step < len(order) - 1:
            held = held.astype(jnp.bfloat16)
    return held


def butterfly_sum(values):
    parts = lax.axis_size("dp")
    values = values + pair_swap(values)
    for bit in range(parts.bit_length() - 1):
        values = values + lax.ppermute(values, "dp", [(i, i ^ (1 << bit)) for i in range(parts)])
    return values


PARTS = 16
LANES = ((0, 1, 2, 3), (1, 2, 0, 3), (2, 0, 1, 3))
RIDES = (1, 2, 0)


def insert(number, bit, value):
    low = number & ((1 << bit) - 1)
    return ((number - low) << 1) | (value << bit) | low


def row_of(ref):
    return ref[...].reshape(1, -1)


def input_rule(tokens, gain, own_middle, own_back, got):
    normed_grad = own_back + got.astype(f32)
    values = tokens.astype(f32)
    factor = row_factor(values)
    scaled = values * factor
    gained = gain * normed_grad
    inner = jnp.mean(scaled * gained, axis=-1, keepdims=True)
    return (own_middle + factor * (gained - scaled * inner)).astype(bf16)


def after(token, values):
    return lax.optimization_barrier((values, token))[0]


def block_rows(index, block):
    return pl.ds(pl.multiple_of(index * block, 16), block)


def swap_bit(values, bit):
    parts = lax.axis_size("dp")
    return lax.ppermute(values, "dp", [(i, i ^ (1 << bit)) for i in range(parts)])


def my_bit(bit):
    return lax.shift_right_logical(lax.axis_index("dp"), bit) & 1


def mm(left, right, left_dim=1, right_dim=0):
    return lax.dot_general(
        left, right, (((left_dim,), (right_dim,)), ((), ())), preferred_element_type=f32
    )


def split_low(values):
    high = values.astype(bf16)
    return high, (values - high.astype(f32)).astype(bf16)


def sigmoid(values):
    return 1.0 / (1.0 + jnp.exp(-values))


def row_factor(values):
    return lax.rsqrt(jnp.mean(values * values, axis=-1, keepdims=True) + EPS)


def picks(index_ref, length):
    rows = lax.broadcasted_iota(jnp.int32, (length, index_ref.shape[1]), 0)
    return jnp.where(rows == index_ref[...], 1.0, 0.0).astype(bf16)


def head_masks(width):
    lanes = lax.shift_right_logical(lax.broadcasted_iota(jnp.int32, (1, width), 1), 6)
    return [jnp.where(lanes == head, 1.0, 0.0).astype(f32) for head in range(width // HEAD_DIM)]


def stack_heads(values, masks):
    return jnp.concatenate([values * mask.astype(values.dtype) for mask in masks], axis=0)


def unstack_heads(values, masks):
    rows = values.shape[0] // len(masks)
    total = values[:rows] * masks[0]
    for head in range(1, len(masks)):
        total = total + values[head * rows : (head + 1) * rows] * masks[head]
    return total


def softmax_rows(scores, axis):
    exponent = jnp.exp(scores - jnp.max(scores, axis=axis, keepdims=True))
    return exponent * (1.0 / jnp.sum(exponent, axis=axis, keepdims=True))


def window_start(block, length):
    start = jnp.clip(block * WINDOW - WINDOW, 0, length - 3 * WINDOW)
    return pl.multiple_of(start, WINDOW)


def attn_forward_kernel(
    ready,
    other_ref,
    own_ref,
    gain_ref,
    route_query_ref,
    route_key_ref,
    query_index_ref,
    key_index_ref,
    hq_ref,
    hk_ref,
    hv_ref,
    ho_ref,
    wq_ref,
    wk_ref,
    wv_ref,
    wo_ref,
    partial_ref,
    input_ref,
    q_ref,
    k_ref,
    v_ref,
    result_ref,
    query_rows_ref,
    key_raw_ref,
    key_rows_ref,
    qh_ref,
    kh_ref,
    vh_ref,
    raw_ref,
    heavy_result_ref,
    pick_ref,
):
    ready(6)
    side = lax.axis_index("tensor")
    half = own_ref.shape[0]
    length = 2 * half
    tile = 256
    for ref, place in ((own_ref, side), (other_ref, 1 - side)):
        for start in range(0, half, tile):
            values = ref[start : start + tile, :].astype(f32)
            normed = values * row_factor(values) * row_of(gain_ref)
            rows = pl.ds(pl.multiple_of(place * half + start, tile), tile)
            input_ref[rows, :] = normed.astype(bf16)
    routed = query_index_ref.shape[1]
    pick_ref[:, :routed] = picks(query_index_ref, length)
    pick_ref[:, routed:] = picks(key_index_ref, length)
    picked = mm(pick_ref[...], input_ref[...], 0, 0)
    query_rows = picked[:routed]
    key_raw = picked[routed:]
    query_score = sigmoid(jnp.sum(query_rows * row_of(route_query_ref), axis=-1, keepdims=True))
    key_score = sigmoid(jnp.sum(key_raw * row_of(route_key_ref), axis=-1, keepdims=True))
    query_rows_ref[...] = query_rows.astype(bf16)
    key_raw_ref[...] = key_raw.astype(bf16)
    key_rows_ref[...] = (key_score * key_raw).astype(bf16)
    ready(10)
    qh_ref[...] = mm(query_rows_ref[...], hq_ref[...]).astype(bf16)
    kh_ref[...] = mm(key_rows_ref[...], hk_ref[...]).astype(bf16)
    vh_ref[...] = mm(key_rows_ref[...], hv_ref[...]).astype(bf16)
    pair = 2 * HEAD_DIM
    pair_masks = head_masks(pair)
    for start in range(0, qh_ref.shape[1], pair):
        cols = slice(start, start + pair)
        stacked = stack_heads(qh_ref[:, cols] * (HEAD_DIM**-0.5), pair_masks)
        probs = softmax_rows(mm(stacked, kh_ref[:, cols], 1, 1), -1)
        raw_ref[:, cols] = unstack_heads(mm(probs.astype(bf16), vh_ref[:, cols]), pair_masks)
    heavy_result_ref[...] = (query_score * raw_ref[...]).astype(bf16)
    high, low = split_low(mm(heavy_result_ref[...], ho_ref[...]))

    ready(14)
    for start in range(0, length, tile):
        rows = slice(start, start + tile)
        q_ref[rows, :] = mm(input_ref[rows, :], wq_ref[...]).astype(bf16)
        k_ref[rows, :] = mm(input_ref[rows, :], wk_ref[...]).astype(bf16)
        v_ref[rows, :] = mm(input_ref[rows, :], wv_ref[...]).astype(bf16)

    masks = head_masks(q_ref.shape[1])
    heads = len(masks)
    gap = lax.broadcasted_iota(jnp.int32, (WINDOW, 3 * WINDOW), 0) - lax.broadcasted_iota(
        jnp.int32, (WINDOW, 3 * WINDOW), 1
    )

    def one_block(block, carry):
        rows = pl.ds(pl.multiple_of(block * WINDOW, WINDOW), WINDOW)
        start = window_start(block, length)
        keys = pl.ds(start, 3 * WINDOW)
        stacked = stack_heads(q_ref[rows, :] * (HEAD_DIM**-0.5), masks)
        scores = mm(stacked, k_ref[keys, :], 1, 1)
        near = jnp.abs(gap + (block * WINDOW - start)) < WINDOW
        bias = jnp.where(near, 0.0, -1e30)
        probs = softmax_rows(scores + jnp.concatenate([bias] * heads, axis=0), -1)
        out = unstack_heads(mm(probs.astype(bf16), v_ref[keys, :]), masks)
        result_ref[rows, :] = out.astype(bf16)
        return carry

    lax.fori_loop(0, length // WINDOW, one_block, 0)
    for start in range(0, length, tile):
        rows = slice(start, start + tile)
        pick = pick_ref[rows, :routed]
        partial_ref[rows, :] = (
            mm(result_ref[rows, :], wo_ref[...]) + (mm(pick, high) + mm(pick, low))
        ).astype(bf16)


def gelu_parts(values):
    density = jnp.exp(-0.5 * values * values) * 0.3989422804014327
    below = 0.5 * (1.0 + lax.erf(values * 0.7071067811865476))
    return values * below, below + values * density


def ffn_heavy_kernel(
    ready,
    hg_ref,
    hu_ref,
    hd_ref,
    other_ref,
    mine_ref,
    got_ref,
    cot_other_ref,
    own_ref,
    cot_own_ref,
    gain_ref,
    route_ref,
    index_ref,
    send_x_ref,
    send_y_ref,
    send_z_ref,
    middle_ref,
    input_ref,
    cot_ref,
    pick_ref,
    down_ref,
    back_ref,
    route_grad_ref,
):
    ready(5)
    side = lax.axis_index("tensor")
    half = own_ref.shape[0]
    length = 2 * half
    tile = 256
    for ref, cot, place in ((own_ref, cot_own_ref, side), (other_ref, cot_other_ref, 1 - side)):
        for start in range(0, half, tile):
            rows = pl.ds(pl.multiple_of(place * half + start, tile), tile)
            branch = mine_ref[rows, :].astype(f32) + got_ref[rows, :].astype(f32)
            middle = ref[start : start + tile, :].astype(f32) + branch
            middle_ref[rows, :] = middle
            input_ref[rows, :] = (middle * row_factor(middle) * row_of(gain_ref)).astype(bf16)
            cot_ref[rows, :] = cot[start : start + tile, :]
    pick_ref[...] = picks(index_ref, length)
    ffn_rows = mm(pick_ref[...], input_ref[...], 0, 0)
    rows_low = ffn_rows.astype(bf16)
    cot_rows = mm(pick_ref[...], cot_ref[...], 0, 0).astype(bf16)
    routed, model = rows_low.shape
    send_x_ref[:, :model] = rows_low
    send_y_ref[:, :model] = rows_low
    send_z_ref[:, :model] = cot_rows
    score = sigmoid(jnp.sum(ffn_rows * row_of(route_ref), axis=-1, keepdims=True))
    heavy_width = hg_ref.shape[1]
    chunk = 512
    score_grad = 0.0
    down = 0.0
    rows_grad = 0.0
    for start in range(0, heavy_width, chunk):
        cols = slice(start, start + chunk)
        out_cols = slice(model + start, model + start + chunk)
        gate = mm(rows_low, hg_ref[:, cols])
        up = mm(rows_low, hu_ref[:, cols])
        act_grad = mm(cot_rows, hd_ref[cols, :], 1, 1)
        gelu, slope = gelu_parts(gate)
        mixed = gelu * up
        score_grad = score_grad + jnp.sum(act_grad * mixed, axis=-1, keepdims=True)
        scaled = score * act_grad
        act = (score * mixed).astype(bf16)
        gate_grad = (scaled * up * slope).astype(bf16)
        up_grad = (scaled * gelu).astype(bf16)
        send_x_ref[:, out_cols] = gate_grad
        send_y_ref[:, out_cols] = up_grad
        send_z_ref[:, out_cols] = act
        down = down + mm(act, hd_ref[cols, :])
        rows_grad = rows_grad + mm(gate_grad, hg_ref[:, cols], 1, 1)
        rows_grad = rows_grad + mm(up_grad, hu_ref[:, cols], 1, 1)
    logit_grad = score * (1.0 - score) * score_grad
    route_grad_ref[...] = jnp.sum(ffn_rows * logit_grad, axis=0, keepdims=True)
    rows_grad = rows_grad + logit_grad * row_of(route_ref)
    down_ref[:routed, :], down_ref[routed:, :] = split_low(down)
    back_ref[:routed, :], back_ref[routed:, :] = split_low(rows_grad)


def ffn_light_kernel(
    middle_ref,
    input_ref,
    cot_ref,
    pick_ref,
    down_ref,
    rows_back_ref,
    wg_ref,
    wu_ref,
    wd_ref,
    back_ref,
    block_own_ref,
    block_send_ref,
    *rest,
):
    lane_refs = rest[:-3]
    light_grad_ref, act_ref, mix_ref = rest[-3:]
    side = lax.axis_index("tensor")
    half = block_own_ref.shape[0]
    tile = 256
    width = wg_ref.shape[1]
    for first in range(0, 2):
        place = side if first == 0 else 1 - side
        for start in range(0, half, tile):
            rows = pl.ds(pl.multiple_of(place * half + start, tile), tile)
            piece = slice(start, start + tile)
            gate = mm(input_ref[rows, :], wg_ref[...])
            up = mm(input_ref[rows, :], wu_ref[...])
            act_grad = mm(cot_ref[rows, :], wd_ref[...], 1, 1)
            gelu, slope = gelu_parts(gate)
            act_ref[rows, :] = (gelu * up).astype(bf16)
            mix_ref[rows, :width] = (act_grad * up * slope).astype(bf16)
            mix_ref[rows, width:] = (act_grad * gelu).astype(bf16)
            pick = jnp.concatenate([pick_ref[rows, :]] * 2, axis=1)
            branch = mm(act_ref[rows, :], wd_ref[...]) + mm(pick, down_ref[...])
            if first == 0:
                block_own_ref[piece, :] = middle_ref[rows, :] + branch
            else:
                block_send_ref[piece, :] = branch.astype(bf16)
            back_ref[rows, :] = (
                mm(mix_ref[rows, :width], wg_ref[...], 1, 1)
                + mm(mix_ref[rows, width:], wu_ref[...], 1, 1)
                + mm(pick, rows_back_ref[...])
            ).astype(bf16)
    light_grad_ref[:, : 2 * width] = mm(input_ref[...], mix_ref[...], 0, 0).astype(bf16)
    light_grad_ref[:, 2 * width :] = mm(cot_ref[...], act_ref[...], 0, 0).astype(bf16)
    for lane in range(len(lane_refs) // 2):
        lane_split(lane, lane_refs, 0, light_grad_ref, lane * width, (lane + 1) * width)


def lane_split(lane, lane_refs, left, grad_ref, first, last):
    bit = LANES[lane][0]
    mine = my_bit(bit)
    block = grad_ref.shape[0] // PARTS
    keep_ref, send_ref = lane_refs[lane], lane_refs[len(LANES) + lane]
    for p in range(PARTS // 2):
        rows = slice(p * block, (p + 1) * block)
        cols = slice(left, left + last - first)
        for ref, value in ((keep_ref, mine), (send_ref, 1 - mine)):
            ref[rows, cols] = grad_ref[block_rows(insert(p, bit, value), block), first:last]


def attn_backward_kernel(
    ready,
    cot_other_ref,
    middle_ref,
    mine_ref,
    got_ref,
    result_ref,
    query_rows_ref,
    key_raw_ref,
    key_rows_ref,
    qh_ref,
    kh_ref,
    vh_ref,
    raw_ref,
    heavy_result_ref,
    cot_own_ref,
    gain_ffn_ref,
    route_query_ref,
    route_key_ref,
    query_index_ref,
    key_index_ref,
    wo_ref,
    ho_ref,
    hq_ref,
    hk_ref,
    hv_ref,
    own_middle_ref,
    out_ref,
    grad_ref,
    back_high_ref,
    back_low_ref,
    pick_ref,
    small_ref,
    low_ref,
):
    ready(6)
    side = lax.axis_index("tensor")
    half = cot_own_ref.shape[0]
    length = 2 * half
    tile = 256
    scale = HEAD_DIM**-0.5
    heavy = qh_ref.shape[1]
    light = result_ref.shape[1]
    gain_ffn_grad = 0.0
    for cot, place, owned in ((cot_own_ref, side, True), (cot_other_ref, 1 - side, False)):
        for start in range(0, half, tile):
            rows = pl.ds(pl.multiple_of(place * half + start, tile), tile)
            piece = slice(start, start + tile)
            normed_grad = mine_ref[rows, :].astype(f32) + got_ref[rows, :].astype(f32)
            middle = middle_ref[rows, :]
            factor = row_factor(middle)
            scaled = factor * middle
            gain_ffn_grad = gain_ffn_grad + jnp.sum(scaled * normed_grad, axis=0, keepdims=True)
            gained = row_of(gain_ffn_ref) * normed_grad
            inner = jnp.mean(scaled * gained, axis=-1, keepdims=True)
            grad = cot[piece, :].astype(f32) + factor * (gained - scaled * inner)
            if owned:
                own_middle_ref[piece, :] = grad
            low_ref[rows, :] = grad.astype(bf16)
    ready(11)
    for start in range(0, length, tile):
        rows = slice(start, start + tile)
        out_ref[rows, :] = mm(low_ref[rows, :], wo_ref[...], 1, 1).astype(bf16)
    grad_ref[:, heavy : heavy + light] = mm(low_ref[...], result_ref[...], 0, 0).astype(bf16)

    routed = query_index_ref.shape[1]
    pick_ref[:, :routed] = picks(query_index_ref, length)
    pick_ref[:, routed:] = picks(key_index_ref, length)
    query_rows = query_rows_ref[...].astype(f32)
    key_raw = key_raw_ref[...].astype(f32)
    query_score = sigmoid(jnp.sum(query_rows * row_of(route_query_ref), axis=-1, keepdims=True))
    key_score = sigmoid(jnp.sum(key_raw * row_of(route_key_ref), axis=-1, keepdims=True))
    mid_rows = mm(pick_ref[:, :routed], low_ref[...], 0, 0).astype(bf16)
    grad_ref[:, 3 * heavy + light :] = mm(mid_rows, heavy_result_ref[...], 0, 0).astype(bf16)
    heavy_out_grad = mm(mid_rows, ho_ref[...], 1, 1).astype(bf16)
    query_score_grad = jnp.sum(
        heavy_out_grad.astype(f32) * raw_ref[...], axis=-1, keepdims=True
    )
    raw_high, raw_low = split_low(query_score * heavy_out_grad.astype(f32))
    pair = 2 * HEAD_DIM
    pair_masks = head_masks(pair)
    stacked_score = jnp.concatenate([query_score] * 2, axis=0)
    q_parts, k_parts, v_parts = [], [], []
    for start in range(0, heavy, pair):
        cols = slice(start, start + pair)
        stacked = stack_heads(qh_ref[:, cols] * scale, pair_masks)
        probs = softmax_rows(mm(stacked, kh_ref[:, cols], 1, 1), -1)
        grad_stacked = stack_heads(heavy_out_grad[:, cols], pair_masks)
        probs_grad = stacked_score * mm(grad_stacked, vh_ref[:, cols], 1, 1)
        inner = jnp.sum(probs * probs_grad, axis=-1, keepdims=True)
        score_grad = (probs * (probs_grad - inner)).astype(bf16)
        probs_low = probs.astype(bf16)
        q_parts.append(unstack_heads(mm(score_grad, kh_ref[:, cols]) * scale, pair_masks))
        k_parts.append(mm(score_grad, stacked, 0, 0))
        v_parts.append(
            mm(probs_low, stack_heads(raw_high[:, cols], pair_masks), 0, 0)
            + mm(probs_low, stack_heads(raw_low[:, cols], pair_masks), 0, 0)
        )
    query_heavy_grad = jnp.concatenate(q_parts, axis=1).astype(bf16)
    key_heavy_grad = jnp.concatenate(k_parts, axis=1).astype(bf16)
    value_heavy_grad = jnp.concatenate(v_parts, axis=1).astype(bf16)
    grad_ref[:, :heavy] = mm(query_rows_ref[...], query_heavy_grad, 0, 0).astype(bf16)
    grad_ref[:, heavy + light : 2 * heavy + light] = mm(key_rows_ref[...], key_heavy_grad, 0, 0).astype(bf16)
    grad_ref[:, 2 * heavy + light : 3 * heavy + light] = mm(
        key_rows_ref[...], value_heavy_grad, 0, 0
    ).astype(bf16)
    key_rows_grad = mm(key_heavy_grad, hk_ref[...], 1, 1) + mm(
        value_heavy_grad, hv_ref[...], 1, 1
    )
    key_logit_grad = (
        key_score * (1.0 - key_score) * jnp.sum(key_rows_grad * key_raw, axis=-1, keepdims=True)
    )
    query_logit_grad = query_score * (1.0 - query_score) * query_score_grad
    key_raw_grad = key_score * key_rows_grad + key_logit_grad * row_of(route_key_ref)
    query_rows_grad = mm(query_heavy_grad, hq_ref[...], 1, 1)
    query_rows_grad = query_rows_grad + query_logit_grad * row_of(route_query_ref)
    small_ref[...] = jnp.zeros_like(small_ref)
    small_ref[1:2, :] = 0.5 * gain_ffn_grad
    small_ref[2:3, :] = jnp.sum(query_rows * query_logit_grad, axis=0, keepdims=True)
    small_ref[3:4, :] = jnp.sum(key_raw * key_logit_grad, axis=0, keepdims=True)
    high, low = split_low(jnp.concatenate([query_rows_grad, key_raw_grad], axis=0))
    back_high_ref[...] = high
    back_low_ref[...] = low


def lane_cuts(heavy, light):
    first = heavy + light
    second = first + 2 * heavy
    return (
        (0, first, 0, light),
        (first, second, light, light),
        (second, second + heavy, light, 3 * light),
    )


def light_backward_kernel(
    ready,
    other_ref,
    input_ref,
    q_ref,
    k_ref,
    v_ref,
    out_ref,
    heavy_grad_ref,
    back_high_ref,
    back_low_ref,
    pick_ref,
    own_ref,
    wq_ref,
    wk_ref,
    wv_ref,
    own_back_ref,
    send_ref,
    small_ref,
    *rest,
):
    grad_refs = rest[:-6]
    light_grad_ref, kt_ref, qt_grad_ref, k_grad_ref, v_grad_ref, mixed_ref = rest[-6:]
    side = lax.axis_index("tensor")
    half = own_ref.shape[0]
    length = 2 * half
    tile = 256
    scale = HEAD_DIM**-0.5
    kt_ref[...] = k_ref[...].T
    k_grad_ref[...] = jnp.zeros_like(k_grad_ref)
    v_grad_ref[...] = jnp.zeros_like(v_grad_ref)
    masks = head_masks(q_ref.shape[1])
    heads = len(masks)
    gap = lax.broadcasted_iota(jnp.int32, (3 * WINDOW, WINDOW), 1) - lax.broadcasted_iota(
        jnp.int32, (3 * WINDOW, WINDOW), 0
    )

    def one_block(block, carry):
        first = pl.multiple_of(block * WINDOW, WINDOW)
        rows = pl.ds(first, WINDOW)
        start = window_start(block, length)
        keys = pl.ds(start, 3 * WINDOW)
        stacked = stack_heads(q_ref[rows, :] * scale, masks)
        grad_stacked = stack_heads(out_ref[rows, :], masks)
        near = jnp.abs(gap + (block * WINDOW - start)) < WINDOW
        bias = jnp.where(near, 0.0, -1e30)
        scores = mm(k_ref[keys, :], stacked, 1, 1)
        probs = softmax_rows(scores + jnp.concatenate([bias] * heads, axis=1), 0)
        probs_grad = mm(v_ref[keys, :], grad_stacked, 1, 1)
        inner = jnp.sum(probs * probs_grad, axis=0, keepdims=True)
        score_grad = (probs * (probs_grad - inner)).astype(bf16)
        k_grad_ref[keys, :] += mm(score_grad, stacked)
        v_grad_ref[keys, :] += mm(probs.astype(bf16), grad_stacked)
        spread = mm(kt_ref[:, keys], score_grad) * scale
        for head in range(heads):
            lanes = slice(head * HEAD_DIM, (head + 1) * HEAD_DIM)
            qt_grad_ref[lanes, rows] = spread[lanes, head * WINDOW : (head + 1) * WINDOW]
        return carry

    lax.fori_loop(0, length // WINDOW, one_block, 0)
    light = q_ref.shape[1]
    mixed_ref[:, :light] = qt_grad_ref[...].T.astype(bf16)
    mixed_ref[:, light : 2 * light] = k_grad_ref[...].astype(bf16)
    mixed_ref[:, 2 * light :] = v_grad_ref[...].astype(bf16)
    heavy_cols = heavy_grad_ref.shape[1]
    heavy = (heavy_cols - light) // 4
    light_grad = mm(input_ref[...], mixed_ref[...], 0, 0).astype(bf16)
    ready(4)
    gain_attn_grad = 0.0
    for ref, place, owned in ((own_ref, side, True), (other_ref, 1 - side, False)):
        for start in range(0, half, tile):
            rows = pl.ds(pl.multiple_of(place * half + start, tile), tile)
            piece = slice(start, start + tile)
            pick = pick_ref[rows, :]
            back = (
                mm(mixed_ref[rows, :light], wq_ref[...], 1, 1)
                + mm(mixed_ref[rows, light : 2 * light], wk_ref[...], 1, 1)
                + mm(mixed_ref[rows, 2 * light :], wv_ref[...], 1, 1)
                + (mm(pick, back_high_ref[...]) + mm(pick, back_low_ref[...]))
            )
            values = ref[piece, :].astype(f32)
            gain_attn_grad = gain_attn_grad + jnp.sum(
                values * row_factor(values) * back, axis=0, keepdims=True
            )
            if owned:
                own_back_ref[piece, :] = back
            else:
                send_ref[piece, :] = back.astype(bf16)
    small_ref[...] = gain_attn_grad
    if len(grad_refs) == 1:
        grad_refs[0][:, :heavy_cols] = heavy_grad_ref[...]
        grad_refs[0][:, heavy_cols:] = light_grad
        return
    light_grad_ref[...] = light_grad
    for lane in range(len(LANES)):
        left, right, first, last = lane_cuts(heavy, light)[lane]
        lane_split(lane, grad_refs, 0, heavy_grad_ref, left, right)
        if last > first:
            lane_split(lane, grad_refs, right - left, light_grad_ref, first, last)


def join_kernel(lane, send_ref, got_ref, light_ref, next_keep_ref, next_send_ref, full_ref):
    model, heavy = full_ref.shape
    tall = next_send_ref.shape[0]
    light = light_ref.shape[1]
    for wrap in range(light_ref.shape[0] // tall):
        cols = slice(heavy + wrap * light, heavy + (wrap + 1) * light)
        next_send_ref[:, cols] = light_ref[wrap * tall : (wrap + 1) * tall, :]
    left = jnp.concatenate([send_ref[:, :model], got_ref[:, :model]], axis=0)
    right = jnp.concatenate([send_ref[:, model:], got_ref[:, model:]], axis=0)
    full_ref[...] = mm(left, right, 0, 0).astype(bf16)
    first, second = LANES[lane][:2]
    position = second - (1 if first < second else 0)
    mine, next_mine = my_bit(first), my_bit(second)
    block = model // PARTS
    for q in range(PARTS // 4):
        rows = slice(q * block, (q + 1) * block)
        for ref, value in ((next_keep_ref, next_mine), (next_send_ref, 1 - next_mine)):
            p = insert(q, position, value)
            ref[rows, :heavy] = full_ref[block_rows(insert(p, first, mine), block), :]


def pack_small(values, send_ref, left):
    high, low = split_low(values)
    both = jnp.concatenate([high.astype(f32), low.astype(f32)], axis=0).astype(bf16)
    wide = send_ref.shape[1] - left
    for i in range(both.shape[1] // wide):
        send_ref[16 * i : 16 * (i + 1), left:] = both[:, wide * i : wide * (i + 1)]


def unpack_small(got_ref, left, width):
    wide = got_ref.shape[1] - left
    both = jnp.concatenate(
        [got_ref[16 * i : 16 * (i + 1), left:] for i in range(width // wide)], axis=1
    ).astype(f32)
    return both[:8] + both[8:]


def fold_kernel(bit, position, block, pairs, *refs):
    next_keep_ref, next_send_ref = refs[2 * pairs :][-3:-1]
    sum_ref = refs[-1]
    extra = refs[2 * pairs : -3]
    left = 0
    for keep_ref, got_ref in zip(refs[: 2 * pairs : 2], refs[1 : 2 * pairs : 2]):
        rows, width = keep_ref.shape
        tall = min(rows, got_ref.shape[0])
        skip = got_ref.shape[1] - width * (rows // tall) if tall < rows else 0
        for wrap in range(rows // tall):
            piece = slice(wrap * tall, (wrap + 1) * tall)
            got = got_ref[:, skip + wrap * width : skip + (wrap + 1) * width]
            both = keep_ref[piece, :].astype(f32) + got.astype(f32)
            sum_ref[piece, left : left + width] = both.astype(bf16)
        left += width
    mine = my_bit(bit)
    for q in range(next_keep_ref.shape[0] // block):
        rows = slice(q * block, (q + 1) * block)
        next_keep_ref[rows, :] = sum_ref[block_rows(insert(q, position, mine), block), :]
        next_send_ref[rows, :left] = sum_ref[block_rows(insert(q, position, 1 - mine), block), :]
    if extra:
        *parts, small_ref = extra
        small = parts[0][...]
        if len(parts) == 2:
            small = small + parts[1][...]
        else:
            small = small + unpack_small(refs[1], refs[0].shape[1], small.shape[1])
        small_ref[...] = small
        pack_small(small, next_send_ref, left)


def last_fold_kernel(bit, lanes, *refs):
    extra = refs[2 * lanes : -3]
    keep_ref, send_ref, sum_ref = refs[-3:]
    left = 0
    for lane in range(lanes):
        width = refs[lane].shape[1]
        both = refs[lane][...].astype(f32) + refs[lanes + lane][:, :width].astype(f32)
        sum_ref[:, left : left + width] = both
        left += width
    mine = my_bit(bit)
    block = keep_ref.shape[0]
    keep_ref[...] = sum_ref[block_rows(mine, block), :]
    send_ref[:, :left] = sum_ref[block_rows(1 - mine, block), :].astype(bf16)
    if extra:
        small = extra[0][...]
        small = small + unpack_small(refs[lanes], refs[0].shape[1], small.shape[1])
        extra[1][...] = small
        pack_small(small, send_ref, left)


def final_kernel(widths, keep_ref, got_ref, *refs):
    left = 0
    outs = refs
    if len(refs) > len(widths):
        small_ref, *outs = refs
        total = keep_ref.shape[1]
        small = small_ref[...] + unpack_small(got_ref, total, small_ref.shape[1])
        for i, out_ref in enumerate(outs[len(widths) :]):
            out_ref[...] = small[i]
    for width, out_ref in zip(widths, outs):
        cols = slice(left, left + width)
        out_ref[...] = keep_ref[:, cols] + got_ref[:, cols].astype(f32)
        left += width


def fold(bit, position, block, *pairs, extra=()):
    rows = pairs[0].shape[0]
    width = sum(pair.shape[1] for pair in pairs[::2])
    ride = 128 if extra else 0
    return whole(
        functools.partial(fold_ride if extra else fold_kernel, bit, position, block, len(pairs) // 2),
        "fold",
        2,
        [((rows // 2, width), bf16), ((rows // 2, width + ride), bf16)]
        + [(item.shape, f32) for item in extra[:1]],
        [((rows, width), bf16)],
        *pairs,
        *extra,
    )


def fold_ride(bit, position, block, pairs, *refs):
    keep_ref, send_ref, small_ref, sum_ref = refs[-4:]
    fold_kernel(bit, position, block, pairs, *refs[:-4], small_ref, keep_ref, send_ref, sum_ref)


def last_fold(bit, keeps, gots, extra=()):
    rows = keeps[0].shape[0]
    width = sum(keep.shape[1] for keep in keeps)
    ride = 256 if extra else 0
    return whole(
        functools.partial(last_ride if extra else last_fold_kernel, bit, len(keeps)),
        "last_fold",
        2,
        [((rows // 2, width), f32), ((rows // 2, width + ride), bf16)]
        + [(item.shape, f32) for item in extra[:1]],
        [((rows, width), f32)],
        *keeps,
        *gots,
        *extra,
    )


def last_ride(bit, lanes, *refs):
    keep_ref, send_ref, small_ref, sum_ref = refs[-4:]
    last_fold_kernel(bit, lanes, *refs[:-4], small_ref, keep_ref, send_ref, sum_ref)


def final(widths, keep, got, extra=()):
    return whole(
        functools.partial(final_kernel, widths),
        "final",
        2,
        [((keep.shape[0], width), f32, 0) for width in widths]
        + [((item.shape[1],), f32, 0) for item in extra for _ in range(5)],
        [],
        keep,
        got,
        *extra,
    )


def whole(kernel, name, micros, outs, scratch, *operands, outside=0):
    inside = len(operands) - outside
    spaces = [pltpu.VMEM] * inside + [pltpu.HBM] * outside
    operands = [
        pltpu.with_memory_space_constraint(item, space) for item, space in zip(operands, spaces)
    ]
    shapes = [
        pltpu.VMEM(*out) if len(out) == 2 else jax.ShapeDtypeStruct(*out[:2]) for out in outs
    ]
    stage = [pltpu.VMEM(item.shape, item.dtype) for item in operands[inside:]]
    if outside:
        stage.append(pltpu.SemaphoreType.DMA((outside,)))

    def staged(*refs):
        if not outside:
            return kernel(*refs)
        sources, kept, sems = refs[inside : inside + outside], refs[-1 - outside : -1], refs[-1]
        copies = [
            pltpu.make_async_copy(source, target, sems.at[i])
            for i, (source, target) in enumerate(zip(sources, kept))
        ]
        for copy in copies:
            copy.start()
        waited = [False] * outside

        def ready(count):
            for i in range(count):
                if not waited[i]:
                    copies[i].wait()
                    waited[i] = True

        kernel(ready, *refs[:inside], *kept, *refs[inside + outside : -1 - outside])

    return pl.pallas_call(
        staged,
        name=name,
        out_shape=shapes,
        in_specs=[pl.BlockSpec(memory_space=space) for space in spaces],
        out_specs=[pl.BlockSpec(memory_space=pltpu.VMEM)] * len(outs),
        scratch_shapes=[pltpu.VMEM(shape, dtype) for shape, dtype in scratch] + stage,
        compiler_params=pltpu.CompilerParams(vmem_limit_bytes=VMEM_LIMIT),
        cost_estimate=pl.CostEstimate(
            flops=micros * 10**9, transcendentals=0, bytes_accessed=micros * 10**6
        ),
    )(*operands)


def body(
    tokens,
    cotangent,
    gain_attn,
    gain_ffn,
    route_query,
    route_key,
    route_ffn,
    light_query,
    light_key,
    light_value,
    light_out,
    heavy_query,
    heavy_key,
    heavy_value,
    heavy_out,
    light_gate,
    light_up,
    light_down,
    heavy_gate,
    heavy_up,
    heavy_down,
    query_index,
    key_index,
    ffn_index,
):
    half, width = tokens.shape
    length = 2 * half
    routed = query_index.shape[1]
    light = light_query.shape[1]
    heavy = heavy_query.shape[1]
    light_ff = light_gate.shape[1]
    heavy_ff = heavy_gate.shape[1]
    other_tokens = pair_swap(tokens)
    other_cotangent = pair_swap(cotangent)
    attn_weights = (
        heavy_query,
        heavy_key,
        heavy_value,
        heavy_out,
        light_query,
        light_key,
        light_value,
        light_out,
    )
    attn_partial, *saved = whole(
        attn_forward_kernel,
        "attn_forward",
        16,
        [((length, width), bf16)] * 2
        + [((length, light), bf16)] * 4
        + [((routed, width), bf16)] * 3
        + [((routed, heavy), bf16)] * 3
        + [((routed, heavy), f32), ((routed, heavy), bf16)],
        [((length, 2 * routed), bf16)],
        other_tokens,
        tokens,
        gain_attn,
        route_query,
        route_key,
        query_index,
        key_index,
        *attn_weights,
        outside=6 + len(attn_weights),
    )
    tuned = lax.axis_size("dp") == PARTS
    *sends, middle, ffn_input, cot_rows, ffn_pick, down, rows_back, route_ffn_grad = whole(
        ffn_heavy_kernel,
        "ffn_heavy",
        12,
        [((routed, width + heavy_ff), bf16)] * 3
        + [
            ((length, width), f32),
            ((length, width), bf16),
            ((length, width), bf16),
            ((length, routed), bf16),
            ((2 * routed, width), bf16),
            ((2 * routed, width), bf16),
            ((1, width), f32),
        ],
        [],
        heavy_gate,
        heavy_up,
        heavy_down,
        other_tokens,
        attn_partial,
        pair_swap(attn_partial),
        other_cotangent,
        tokens,
        cotangent,
        gain_ffn,
        route_ffn,
        ffn_index,
        outside=5,
    )
    if tuned:
        gots = [swap_bit(send, order[0]) for send, order in zip(sends, LANES)]
    ffn_back, block_own, block_send, *light_parts = whole(
        ffn_light_kernel,
        "ffn_light",
        12,
        [((length, width), bf16), ((half, width), f32), ((half, width), bf16)]
        + ([((width // 2, light_ff), bf16)] * 6 if tuned else [((width, 3 * light_ff), bf16)]),
        ([((width, 3 * light_ff), bf16)] if tuned else [])
        + [((length, light_ff), bf16), ((length, 2 * light_ff), bf16)],
        middle,
        ffn_input,
        cot_rows,
        ffn_pick,
        down,
        rows_back,
        light_gate,
        light_up,
        light_down,
    )
    if tuned:
        back_got = pair_swap(after(tuple(gots), ffn_back))
        light_keeps = light_parts[:3]
        light_sends = light_parts[3:]
        token = ffn_back
        ffn_keeps, ffn_sends = [], []
        for lane in range(3):
            keep, send = whole(
                functools.partial(join_kernel, lane),
                "join",
                3,
                [((width // 4, heavy_ff), bf16), ((width // 4, heavy_ff + 2 * light_ff), bf16)],
                [((width, heavy_ff), bf16)],
                after(token, sends[lane]),
                gots[lane],
                light_sends[RIDES[lane]],
            )
            token = keep
            ffn_keeps.append(keep)
            ffn_sends.append(send)
        ffn_gots = [swap_bit(send, order[1]) for send, order in zip(ffn_sends, LANES)]
        ffn_back = after(token, ffn_back)
    else:
        back_got = pair_swap(ffn_back)
    attn_input, q_light, k_light, v_light, *routed_saved = saved
    own_middle, out_back, heavy_grad, back_high, back_low, pick, small = whole(
        attn_backward_kernel,
        "attn_backward",
        10,
        [
            ((half, width), f32),
            ((length, light), bf16),
            ((width, 4 * heavy + light), bf16),
            ((2 * routed, width), bf16),
            ((2 * routed, width), bf16),
            ((length, 2 * routed), bf16),
            ((8, width), f32),
        ],
        [((length, width), bf16)],
        other_cotangent,
        middle,
        ffn_back,
        back_got,
        *routed_saved,
        cotangent,
        gain_ffn,
        route_query,
        route_key,
        query_index,
        key_index,
        light_out,
        heavy_out,
        heavy_query,
        heavy_key,
        heavy_value,
        outside=11,
    )
    block = width // lax.axis_size("dp")
    own_back, back_send, gain_attn_grad, *attn_grads = whole(
        light_backward_kernel,
        "light_backward",
        16,
        [((half, width), f32), ((half, width), bf16), ((1, width), f32)]
        + (
            [
                ((width // 2, right - left + last - first), bf16)
                for left, right, first, last in lane_cuts(heavy, light)
            ]
            * 2
            if tuned
            else [((width, 4 * heavy + 4 * light), bf16)]
        ),
        [
            ((width, 3 * light), bf16),
            ((light, length), bf16),
            ((light, length), f32),
            ((length, light), f32),
            ((length, light), f32),
            ((length, 3 * light), bf16),
        ],
        other_tokens,
        attn_input,
        q_light,
        k_light,
        v_light,
        out_back,
        heavy_grad,
        back_high,
        back_low,
        pick,
        tokens,
        light_query,
        light_key,
        light_value,
        outside=4,
    )
    small = small + jnp.pad(route_ffn_grad, ((4, 3), (0, 0)))
    small = small + jnp.pad(gain_attn_grad, ((0, 7), (0, 0)))
    if tuned:
        attn_keeps = attn_grads[:3]
        small = small + pair_swap(small)
        small_got = swap_bit(small, 0)
        attn_gots = [swap_bit(send, order[0]) for send, order in zip(attn_grads[3:], LANES)]

        def middle_stage(stage, token, keeps, *rest, extra=()):
            next_keeps, next_gots = [], []
            for lane, order in enumerate(LANES):
                left = sorted(order[stage:])
                keep, send, *small = fold(
                    order[stage],
                    left.index(order[stage]),
                    block,
                    after(token, keeps[lane]),
                    *(item[lane] for item in rest),
                    extra=extra if lane == 0 else (),
                )
                if lane == 0:
                    rider = small
                token = keep
                next_keeps.append(keep)
                next_gots.append(swap_bit(send, order[stage]))
            return token, next_keeps, next_gots, rider

        token, ffn_keeps, ffn_gots_next, _ = middle_stage(2, gain_attn_grad, ffn_keeps, ffn_gots)
        ffn_keep, ffn_send = last_fold(3, [after(token, ffn_keeps[0]), *ffn_keeps[1:]], ffn_gots_next)
        ffn_got = swap_bit(ffn_send, 3)
        token, attn_keeps, attn_gots, rider = middle_stage(
            1,
            ffn_keep,
            attn_keeps,
            attn_gots,
            light_keeps,
            [ffn_gots[RIDES.index(i)] for i in range(3)],
            extra=(small, small_got),
        )
        hg, hu, hd = final([heavy_ff] * 3, after(token, ffn_keep), ffn_got)
        token, attn_keeps, attn_gots, rider = middle_stage(
            2, hg, attn_keeps, attn_gots, extra=tuple(rider)
        )
        attn_keep, attn_send, rider = last_fold(
            3, [after(token, attn_keeps[0]), *attn_keeps[1:]], attn_gots, extra=tuple(rider)
        )
        attn_got = swap_bit(attn_send, 3)
        back_got = pair_swap(after(attn_keep, back_send))
        block_got = pair_swap(after(attn_keep, block_send))
        block_out = (block_own + block_got.astype(f32)).astype(bf16)
        input_grad = input_rule(tokens, gain_attn, own_middle, own_back, back_got)
        widths = [heavy, light, light, light_ff, heavy, heavy, light_ff, heavy, light, light, light_ff]
        pieces = final(widths, after((input_grad, block_out), attn_keep), attn_got, extra=(rider,))
        hq, lo, lq, lg, hk, hv, lu, ho, lk, lv, ld, *small_summed = pieces
    else:
        small_summed = butterfly_sum(small)
        block_out = (block_own + pair_swap(block_send).astype(f32)).astype(bf16)
        input_grad = input_rule(tokens, gain_attn, own_middle, own_back, pair_swap(back_send))
    if not tuned:
        order = list(range(lax.axis_size("dp").bit_length() - 1))
        hg, hu, hd = (
            halving_sum(mm(send[:, :width], send[:, width:], 0, 0).astype(bf16), order)
            for send in sends
        )
        lg, lu, ld = jnp.split(halving_sum(light_parts[0], order), 3, axis=1)
        attn_sum = halving_sum(attn_grads[0], order)
        cuts = [heavy, heavy + light, 2 * heavy + light, 3 * heavy + light, 4 * heavy + light]
        cuts += [4 * heavy + 2 * light, 4 * heavy + 3 * light]
        hq, lo, hk, hv, ho, lq, lk, lv = jnp.split(attn_sum, cuts, axis=1)
    return (
        block_out,
        input_grad,
        small_summed[0],
        small_summed[1],
        small_summed[2],
        small_summed[3],
        small_summed[4],
        lq,
        lk,
        lv,
        lo.T,
        hq,
        hk,
        hv,
        ho.T,
        lg,
        lu,
        ld.T,
        hg,
        hu,
        hd.T,
    )


def solution(mesh):
    in_specs = (
        P(("dp", "tensor"), None),
        P(("dp", "tensor"), None),
        P(),
        P(),
        P(),
        P(),
        P(),
        P(None, "tensor"),
        P(None, "tensor"),
        P(None, "tensor"),
        P("tensor", None),
        P(None, "tensor"),
        P(None, "tensor"),
        P(None, "tensor"),
        P("tensor", None),
        P(None, "tensor"),
        P(None, "tensor"),
        P("tensor", None),
        P(None, "tensor"),
        P(None, "tensor"),
        P("tensor", None),
        P("dp", None),
        P("dp", None),
        P("dp", None),
    )
    out_specs = (
        P(("dp", "tensor"), None),
        P(("dp", "tensor"), None),
        P(),
        P(),
        P(),
        P(),
        P(),
        P("dp", "tensor"),
        P("dp", "tensor"),
        P("dp", "tensor"),
        P("tensor", "dp"),
        P("dp", "tensor"),
        P("dp", "tensor"),
        P("dp", "tensor"),
        P("tensor", "dp"),
        P("dp", "tensor"),
        P("dp", "tensor"),
        P("tensor", "dp"),
        P("dp", "tensor"),
        P("dp", "tensor"),
        P("tensor", "dp"),
    )
    return jax.shard_map(body, mesh=mesh, in_specs=in_specs, out_specs=out_specs, check_vma=False)
```

```python
import functools

import jax
import jax.numpy as jnp
from jax import lax
from jax.experimental import pallas as pl
from jax.experimental.pallas import tpu as pltpu
from jax.sharding import PartitionSpec as P

HEAD_DIM = 64
WINDOW = 128
EPS = 1e-06
VMEM_LIMIT = 20 * 1024 * 1024
f32 = jnp.float32
bf16 = jnp.bfloat16


def pair_swap(values):
    return lax.ppermute(values, "tensor", [(0, 1), (1, 0)])


def halving_sum(values, order):
    parts = lax.axis_size("dp")
    place = lax.axis_index("dp")
    bits = list(range(len(order) - 1, -1, -1))
    held = values.reshape((2,) * len(bits) + (values.shape[0] // parts, values.shape[1]))
    held = held.astype(jnp.bfloat16)
    for step, bit in enumerate(order):
        axis = bits.index(bit)
        bits.remove(bit)
        mine = (place >> bit) & 1
        keep = lax.dynamic_index_in_dim(held, mine, axis, keepdims=False)
        send = lax.dynamic_index_in_dim(held, 1 - mine, axis, keepdims=False)
        got = lax.ppermute(send, "dp", [(i, i ^ (1 << bit)) for i in range(parts)])
        held = keep.astype(jnp.float32) + got.astype(jnp.float32)
        if step < len(order) - 1:
            held = held.astype(jnp.bfloat16)
    return held


def butterfly_sum(values):
    parts = lax.axis_size("dp")
    values = values + pair_swap(values)
    for bit in range(parts.bit_length() - 1):
        values = values + lax.ppermute(values, "dp", [(i, i ^ (1 << bit)) for i in range(parts)])
    return values


PARTS = 16
LANES = ((0, 1, 2, 3), (1, 2, 0, 3), (2, 0, 1, 3))
RIDES = (1, 2, 0)
ATTN_LANES = ((0, 1, 2, 3), (1, 2, 3, 0), (2, 0, 1, 3))


def insert(number, bit, value):
    low = number & ((1 << bit) - 1)
    return ((number - low) << 1) | (value << bit) | low


def row_of(ref):
    return ref[...].reshape(1, -1)


def input_rule(tokens, gain, own_middle, own_back, got):
    normed_grad = own_back + got.astype(f32)
    values = tokens.astype(f32)
    factor = row_factor(values)
    scaled = values * factor
    gained = gain * normed_grad
    inner = jnp.mean(scaled * gained, axis=-1, keepdims=True)
    return (own_middle + factor * (gained - scaled * inner)).astype(bf16)


def after(token, values):
    return lax.optimization_barrier((values, token))[0]


def block_rows(index, block):
    return pl.ds(pl.multiple_of(index * block, 16), block)


def swap_bit(values, bit):
    parts = lax.axis_size("dp")
    return lax.ppermute(values, "dp", [(i, i ^ (1 << bit)) for i in range(parts)])


def my_bit(bit):
    return lax.shift_right_logical(lax.axis_index("dp"), bit) & 1


def mm(left, right, left_dim=1, right_dim=0):
    return lax.dot_general(
        left, right, (((left_dim,), (right_dim,)), ((), ())), preferred_element_type=f32
    )


def split_low(values):
    high = values.astype(bf16)
    return high, (values - high.astype(f32)).astype(bf16)


def sigmoid(values):
    return 1.0 / (1.0 + jnp.exp(-values))


def row_factor(values):
    return lax.rsqrt(jnp.mean(values * values, axis=-1, keepdims=True) + EPS)


def picks(index_ref, length):
    rows = lax.broadcasted_iota(jnp.int32, (length, index_ref.shape[1]), 0)
    return jnp.where(rows == index_ref[...], 1.0, 0.0).astype(bf16)


def row_picks(columns_ref, length):
    rows = columns_ref.shape[0]
    cols = lax.broadcasted_iota(jnp.int32, (rows, length), 1)
    return jnp.where(cols == columns_ref[...], 1.0, 0.0).astype(bf16)


def head_masks(width):
    lanes = lax.shift_right_logical(lax.broadcasted_iota(jnp.int32, (1, width), 1), 6)
    return [jnp.where(lanes == head, 1.0, 0.0).astype(f32) for head in range(width // HEAD_DIM)]


def stack_heads(values, masks):
    return jnp.concatenate([values * mask.astype(values.dtype) for mask in masks], axis=0)


def unstack_heads(values, masks):
    rows = values.shape[0] // len(masks)
    total = values[:rows] * masks[0]
    for head in range(1, len(masks)):
        total = total + values[head * rows : (head + 1) * rows] * masks[head]
    return total


def softmax_rows(scores, axis):
    exponent = jnp.exp(scores - jnp.max(scores, axis=axis, keepdims=True))
    return exponent * (1.0 / jnp.sum(exponent, axis=axis, keepdims=True))


def window_start(block, length):
    start = jnp.clip(block * WINDOW - WINDOW, 0, length - 3 * WINDOW)
    return pl.multiple_of(start, WINDOW)


def attn_forward_kernel(
    ready,
    other_ref,
    columns_ref,
    gain_ref,
    route_query_ref,
    route_key_ref,
    query_index_ref,
    ffn_index_ref,
    own_ref,
    cot_ref,
    hq_ref,
    hk_ref,
    hv_ref,
    ho_ref,
    wq_ref,
    wk_ref,
    wv_ref,
    wo_ref,
    partial_ref,
    input_ref,
    q_ref,
    k_ref,
    v_ref,
    result_ref,
    query_rows_ref,
    key_raw_ref,
    key_rows_ref,
    qh_ref,
    kh_ref,
    vh_ref,
    raw_ref,
    heavy_result_ref,
    token_rows_ref,
    swap_rows_ref,
    ffn_pick_ref,
    pick_ref,
):
    ready(5)
    side = lax.axis_index("tensor")
    half = own_ref.shape[0]
    length = 2 * half
    tile = 256
    for ref, place in ((other_ref, 1 - side), (own_ref, side)):
        if ref is own_ref:
            ready(6)
        for start in range(0, half, tile):
            values = ref[start : start + tile, :].astype(f32)
            normed = values * row_factor(values) * row_of(gain_ref)
            rows = pl.ds(pl.multiple_of(place * half + start, tile), tile)
            input_ref[rows, :] = normed.astype(bf16)
    routed = query_index_ref.shape[1]
    pick_ref[...] = picks(query_index_ref, length)
    ffn_pick_ref[...] = picks(ffn_index_ref, length)
    picker = row_picks(columns_ref, length)
    picked = mm(picker[: 2 * routed], input_ref[...])
    own_pick = ffn_pick_ref[pl.ds(pl.multiple_of(side * half, half), half), :]
    other_pick = ffn_pick_ref[pl.ds(pl.multiple_of((1 - side) * half, half), half), :]
    token_rows = mm(own_pick, own_ref[...], 0, 0) + mm(other_pick, other_ref[...], 0, 0)
    token_rows_ref[...] = token_rows.astype(bf16)
    query_rows = picked[:routed]
    key_raw = picked[routed:]
    query_score = sigmoid(jnp.sum(query_rows * row_of(route_query_ref), axis=-1, keepdims=True))
    key_score = sigmoid(jnp.sum(key_raw * row_of(route_key_ref), axis=-1, keepdims=True))
    query_rows_ref[...] = query_rows.astype(bf16)
    key_raw_ref[...] = key_raw.astype(bf16)
    key_rows_ref[...] = (key_score * key_raw).astype(bf16)
    ready(11)
    swap_rows_ref[routed:, :] = mm(own_pick, cot_ref[...], 0, 0).astype(bf16)
    qh_ref[...] = mm(query_rows_ref[...], hq_ref[...]).astype(bf16)
    kh_ref[...] = mm(key_rows_ref[...], hk_ref[...]).astype(bf16)
    vh_ref[...] = mm(key_rows_ref[...], hv_ref[...]).astype(bf16)
    pair = 2 * HEAD_DIM
    pair_masks = head_masks(pair)
    for start in range(0, qh_ref.shape[1], pair):
        cols = slice(start, start + pair)
        stacked = stack_heads(qh_ref[:, cols] * (HEAD_DIM**-0.5), pair_masks)
        probs = softmax_rows(mm(stacked, kh_ref[:, cols], 1, 1), -1)
        raw_ref[:, cols] = unstack_heads(mm(probs.astype(bf16), vh_ref[:, cols]), pair_masks)
    heavy_result_ref[...] = (query_score * raw_ref[...]).astype(bf16)
    high, low = split_low(mm(heavy_result_ref[...], ho_ref[...]))

    ready(15)
    for start in range(0, length, tile):
        rows = slice(start, start + tile)
        q_ref[rows, :] = mm(input_ref[rows, :], wq_ref[...]).astype(bf16)
        k_ref[rows, :] = mm(input_ref[rows, :], wk_ref[...]).astype(bf16)
        v_ref[rows, :] = mm(input_ref[rows, :], wv_ref[...]).astype(bf16)

    masks = head_masks(q_ref.shape[1])
    heads = len(masks)
    gap = lax.broadcasted_iota(jnp.int32, (WINDOW, 3 * WINDOW), 0) - lax.broadcasted_iota(
        jnp.int32, (WINDOW, 3 * WINDOW), 1
    )

    def one_block(block, carry):
        rows = pl.ds(pl.multiple_of(block * WINDOW, WINDOW), WINDOW)
        start = window_start(block, length)
        keys = pl.ds(start, 3 * WINDOW)
        stacked = stack_heads(q_ref[rows, :] * (HEAD_DIM**-0.5), masks)
        scores = mm(stacked, k_ref[keys, :], 1, 1)
        near = jnp.abs(gap + (block * WINDOW - start)) < WINDOW
        bias = jnp.where(near, 0.0, -1e30)
        probs = softmax_rows(scores + jnp.concatenate([bias] * heads, axis=0), -1)
        out = unstack_heads(mm(probs.astype(bf16), v_ref[keys, :]), masks)
        result_ref[rows, :] = out.astype(bf16)
        return carry

    lax.fori_loop(0, length // WINDOW, one_block, 0, unroll=True)
    for start in range(0, length, tile):
        rows = slice(start, start + tile)
        pick = pick_ref[rows, :]
        partial_ref[rows, :] = (
            mm(result_ref[rows, :], wo_ref[...]) + (mm(pick, high) + mm(pick, low))
        ).astype(bf16)
    swap_rows_ref[:routed, :] = mm(picker[2 * routed :], partial_ref[...]).astype(bf16)


def gelu_parts(values):
    density = jnp.exp(-0.5 * values * values) * 0.3989422804014327
    below = 0.5 * (1.0 + lax.erf(values * 0.7071067811865476))
    return values * below, below + values * density


def ffn_heavy_kernel(
    ready,
    hg_ref,
    hu_ref,
    hd_ref,
    token_rows_ref,
    mine_ref,
    got_ref,
    gain_ref,
    route_ref,
    send_x_ref,
    send_y_ref,
    send_z_ref,
    rows_back_ref,
    route_grad_ref,
):
    routed, model = token_rows_ref.shape
    rows = slice(0, routed)
    middle = token_rows_ref[...].astype(f32) + (
        mine_ref[rows, :].astype(f32) + got_ref[rows, :].astype(f32)
    )
    cot_rows = mine_ref[routed:, :] + got_ref[routed:, :]
    ready(2)
    rows_low = (middle * row_factor(middle) * row_of(gain_ref)).astype(bf16)
    ffn_rows = rows_low.astype(f32)
    send_x_ref[:, :model] = rows_low
    send_y_ref[:, :model] = rows_low
    send_z_ref[:, :model] = cot_rows
    score = sigmoid(jnp.sum(ffn_rows * row_of(route_ref), axis=-1, keepdims=True))
    chunk = 512
    score_grad = 0.0
    for start in range(0, hg_ref.shape[1], chunk):
        cols = slice(start, start + chunk)
        out_cols = slice(model + start, model + start + chunk)
        gate = mm(rows_low, hg_ref[:, cols])
        up = mm(rows_low, hu_ref[:, cols])
        act_grad = mm(cot_rows, hd_ref[cols, :], 1, 1)
        gelu, slope = gelu_parts(gate)
        mixed = gelu * up
        score_grad = score_grad + jnp.sum(act_grad * mixed, axis=-1, keepdims=True)
        scaled = score * act_grad
        send_x_ref[:, out_cols] = (scaled * up * slope).astype(bf16)
        send_y_ref[:, out_cols] = (scaled * gelu).astype(bf16)
        send_z_ref[:, out_cols] = (score * mixed).astype(bf16)
    logit_grad = score * (1.0 - score) * score_grad
    route_grad_ref[...] = jnp.sum(ffn_rows * logit_grad, axis=0, keepdims=True)
    rows_back_ref[...] = logit_grad * row_of(route_ref)


def ffn_light_kernel(
    ready,
    other_ref,
    mine_ref,
    got_ref,
    cot_other_ref,
    pick_ref,
    rows_back_ref,
    gate_grad_ref,
    up_grad_ref,
    act_heavy_ref,
    hg_ref,
    hu_ref,
    hd_ref,
    wg_ref,
    wu_ref,
    wd_ref,
    gain_ref,
    own_ref,
    cot_own_ref,
    back_ref,
    block_own_ref,
    block_send_ref,
    middle_ref,
    *rest,
):
    lane_refs = rest[:-5]
    light_grad_ref, act_ref, mix_ref, input_ref, cot_ref = rest[-5:]
    side = lax.axis_index("tensor")
    half = block_own_ref.shape[0]
    tile = 256
    ready(1)
    for ref, cot, place in ((other_ref, cot_other_ref, 1 - side), (own_ref, cot_own_ref, side)):
        if ref is own_ref:
            ready(3)
        for start in range(0, half, tile):
            rows = pl.ds(pl.multiple_of(place * half + start, tile), tile)
            branch = mine_ref[rows, :].astype(f32) + got_ref[rows, :].astype(f32)
            middle = ref[start : start + tile, :].astype(f32) + branch
            middle_ref[rows, :] = middle
            input_ref[rows, :] = (middle * row_factor(middle) * row_of(gain_ref)).astype(bf16)
            cot_ref[rows, :] = cot[start : start + tile, :]
    model = input_ref.shape[1]
    down_high, down_low = split_low(mm(act_heavy_ref[:, model:], hd_ref[...]))
    down = jnp.concatenate([down_high, down_low], axis=0)
    rows_back = (
        rows_back_ref[...]
        + mm(gate_grad_ref[:, model:], hg_ref[...], 1, 1)
        + mm(up_grad_ref[:, model:], hu_ref[...], 1, 1)
    )
    rows_back = jnp.concatenate(split_low(rows_back), axis=0)
    width = wg_ref.shape[1]
    for first in range(0, 2):
        place = side if first == 0 else 1 - side
        for start in range(0, half, tile):
            rows = pl.ds(pl.multiple_of(place * half + start, tile), tile)
            piece = slice(start, start + tile)
            gate = mm(input_ref[rows, :], wg_ref[...])
            up = mm(input_ref[rows, :], wu_ref[...])
            act_grad = mm(cot_ref[rows, :], wd_ref[...], 1, 1)
            gelu, slope = gelu_parts(gate)
            act_ref[rows, :] = (gelu * up).astype(bf16)
            mix_ref[rows, :width] = (act_grad * up * slope).astype(bf16)
            mix_ref[rows, width:] = (act_grad * gelu).astype(bf16)
            pick = jnp.concatenate([pick_ref[rows, :]] * 2, axis=1)
            branch = mm(act_ref[rows, :], wd_ref[...]) + mm(pick, down)
            if first == 0:
                block_own_ref[piece, :] = middle_ref[rows, :] + branch
            else:
                block_send_ref[piece, :] = branch.astype(bf16)
            back_ref[rows, :] = (
                mm(mix_ref[rows, :width], wg_ref[...], 1, 1)
                + mm(mix_ref[rows, width:], wu_ref[...], 1, 1)
                + mm(pick, rows_back)
            ).astype(bf16)
    light_grad_ref[:, : 2 * width] = mm(input_ref[...], mix_ref[...], 0, 0).astype(bf16)
    light_grad_ref[:, 2 * width :] = mm(cot_ref[...], act_ref[...], 0, 0).astype(bf16)
    for lane in range(len(lane_refs) // 2):
        lane_split(lane, lane_refs, 0, light_grad_ref, lane * width, (lane + 1) * width)


def lane_split(lane, lane_refs, left, grad_ref, first, last):
    bit = LANES[lane][0]
    mine = my_bit(bit)
    block = grad_ref.shape[0] // PARTS
    keep_ref, send_ref = lane_refs[lane], lane_refs[len(lane_refs) // 2 + lane]
    for p in range(PARTS // 2):
        rows = slice(p * block, (p + 1) * block)
        cols = slice(left, left + last - first)
        for ref, value in ((keep_ref, mine), (send_ref, 1 - mine)):
            ref[rows, cols] = grad_ref[block_rows(insert(p, bit, value), block), first:last]


def attn_backward_kernel(
    ready,
    cot_other_ref,
    middle_ref,
    mine_ref,
    got_ref,
    result_ref,
    query_rows_ref,
    key_raw_ref,
    key_rows_ref,
    qh_ref,
    kh_ref,
    vh_ref,
    raw_ref,
    heavy_result_ref,
    gain_ffn_ref,
    route_query_ref,
    route_key_ref,
    query_index_ref,
    key_index_ref,
    cot_own_ref,
    wo_ref,
    ho_ref,
    hq_ref,
    hk_ref,
    hv_ref,
    own_middle_ref,
    out_ref,
    grad_ref,
    back_high_ref,
    back_low_ref,
    pick_ref,
    small_ref,
    low_ref,
):
    ready(5)
    side = lax.axis_index("tensor")
    half = cot_own_ref.shape[0]
    length = 2 * half
    tile = 256
    scale = HEAD_DIM**-0.5
    heavy = qh_ref.shape[1]
    light = result_ref.shape[1]
    gain_ffn_grad = 0.0
    for cot, place, owned in ((cot_other_ref, 1 - side, False), (cot_own_ref, side, True)):
        if owned:
            ready(6)
        for start in range(0, half, tile):
            rows = pl.ds(pl.multiple_of(place * half + start, tile), tile)
            piece = slice(start, start + tile)
            normed_grad = mine_ref[rows, :].astype(f32) + got_ref[rows, :].astype(f32)
            middle = middle_ref[rows, :]
            factor = row_factor(middle)
            scaled = factor * middle
            gain_ffn_grad = gain_ffn_grad + jnp.sum(scaled * normed_grad, axis=0, keepdims=True)
            gained = row_of(gain_ffn_ref) * normed_grad
            inner = jnp.mean(scaled * gained, axis=-1, keepdims=True)
            grad = cot[piece, :].astype(f32) + factor * (gained - scaled * inner)
            if owned:
                own_middle_ref[piece, :] = grad
            low_ref[rows, :] = grad.astype(bf16)
    ready(11)
    for start in range(0, length, tile):
        rows = slice(start, start + tile)
        out_ref[rows, :] = mm(low_ref[rows, :], wo_ref[...], 1, 1).astype(bf16)
    grad_ref[:, 4 * heavy :] = mm(low_ref[...], result_ref[...], 0, 0).astype(bf16)

    routed = query_index_ref.shape[1]
    pick_ref[:, :routed] = picks(query_index_ref, length)
    pick_ref[:, routed:] = picks(key_index_ref, length)
    query_rows = query_rows_ref[...].astype(f32)
    key_raw = key_raw_ref[...].astype(f32)
    query_score = sigmoid(jnp.sum(query_rows * row_of(route_query_ref), axis=-1, keepdims=True))
    key_score = sigmoid(jnp.sum(key_raw * row_of(route_key_ref), axis=-1, keepdims=True))
    mid_rows = mm(pick_ref[:, :routed], low_ref[...], 0, 0).astype(bf16)
    grad_ref[:, 3 * heavy : 4 * heavy] = mm(mid_rows, heavy_result_ref[...], 0, 0).astype(bf16)
    heavy_out_grad = mm(mid_rows, ho_ref[...], 1, 1).astype(bf16)
    query_score_grad = jnp.sum(
        heavy_out_grad.astype(f32) * raw_ref[...], axis=-1, keepdims=True
    )
    raw_high, raw_low = split_low(query_score * heavy_out_grad.astype(f32))
    pair = 2 * HEAD_DIM
    pair_masks = head_masks(pair)
    stacked_score = jnp.concatenate([query_score] * 2, axis=0)
    q_parts, k_parts, v_parts = [], [], []
    for start in range(0, heavy, pair):
        cols = slice(start, start + pair)
        stacked = stack_heads(qh_ref[:, cols] * scale, pair_masks)
        probs = softmax_rows(mm(stacked, kh_ref[:, cols], 1, 1), -1)
        grad_stacked = stack_heads(heavy_out_grad[:, cols], pair_masks)
        probs_grad = stacked_score * mm(grad_stacked, vh_ref[:, cols], 1, 1)
        inner = jnp.sum(probs * probs_grad, axis=-1, keepdims=True)
        score_grad = (probs * (probs_grad - inner)).astype(bf16)
        probs_low = probs.astype(bf16)
        q_parts.append(unstack_heads(mm(score_grad, kh_ref[:, cols]) * scale, pair_masks))
        k_parts.append(mm(score_grad, stacked, 0, 0))
        v_parts.append(
            mm(probs_low, stack_heads(raw_high[:, cols], pair_masks), 0, 0)
            + mm(probs_low, stack_heads(raw_low[:, cols], pair_masks), 0, 0)
        )
    query_heavy_grad = jnp.concatenate(q_parts, axis=1).astype(bf16)
    key_heavy_grad = jnp.concatenate(k_parts, axis=1).astype(bf16)
    value_heavy_grad = jnp.concatenate(v_parts, axis=1).astype(bf16)
    grad_ref[:, :heavy] = mm(query_rows_ref[...], query_heavy_grad, 0, 0).astype(bf16)
    grad_ref[:, heavy : 2 * heavy] = mm(key_rows_ref[...], key_heavy_grad, 0, 0).astype(bf16)
    grad_ref[:, 2 * heavy : 3 * heavy] = mm(
        key_rows_ref[...], value_heavy_grad, 0, 0
    ).astype(bf16)
    key_rows_grad = mm(key_heavy_grad, hk_ref[...], 1, 1) + mm(
        value_heavy_grad, hv_ref[...], 1, 1
    )
    key_logit_grad = (
        key_score * (1.0 - key_score) * jnp.sum(key_rows_grad * key_raw, axis=-1, keepdims=True)
    )
    query_logit_grad = query_score * (1.0 - query_score) * query_score_grad
    key_raw_grad = key_score * key_rows_grad + key_logit_grad * row_of(route_key_ref)
    query_rows_grad = mm(query_heavy_grad, hq_ref[...], 1, 1)
    query_rows_grad = query_rows_grad + query_logit_grad * row_of(route_query_ref)
    small_ref[...] = jnp.zeros_like(small_ref)
    small_ref[1:2, :] = 0.5 * gain_ffn_grad
    small_ref[2:3, :] = jnp.sum(query_rows * query_logit_grad, axis=0, keepdims=True)
    small_ref[3:4, :] = jnp.sum(key_raw * key_logit_grad, axis=0, keepdims=True)
    high, low = split_low(jnp.concatenate([query_rows_grad, key_raw_grad], axis=0))
    back_high_ref[...] = high
    back_low_ref[...] = low


def lane_cuts(heavy, light):
    return (
        (0, 2 * heavy, 0, light),
        (2 * heavy, 4 * heavy, 0, 0),
        (4 * heavy, 4 * heavy + light, light, 3 * light),
    )


def light_backward_kernel(
    ready,
    other_ref,
    input_ref,
    q_ref,
    k_ref,
    v_ref,
    out_ref,
    heavy_grad_ref,
    back_high_ref,
    back_low_ref,
    pick_ref,
    own_ref,
    wq_ref,
    wk_ref,
    wv_ref,
    own_back_ref,
    send_ref,
    small_ref,
    *rest,
):
    grad_refs = rest[:-6]
    light_grad_ref, kt_ref, qt_grad_ref, k_grad_ref, v_grad_ref, mixed_ref = rest[-6:]
    side = lax.axis_index("tensor")
    half = own_ref.shape[0]
    length = 2 * half
    tile = 256
    scale = HEAD_DIM**-0.5
    kt_ref[...] = k_ref[...].T
    k_grad_ref[...] = jnp.zeros_like(k_grad_ref)
    v_grad_ref[...] = jnp.zeros_like(v_grad_ref)
    masks = head_masks(q_ref.shape[1])
    heads = len(masks)
    gap = lax.broadcasted_iota(jnp.int32, (3 * WINDOW, WINDOW), 1) - lax.broadcasted_iota(
        jnp.int32, (3 * WINDOW, WINDOW), 0
    )

    def one_block(block, carry):
        first = pl.multiple_of(block * WINDOW, WINDOW)
        rows = pl.ds(first, WINDOW)
        start = window_start(block, length)
        keys = pl.ds(start, 3 * WINDOW)
        stacked = stack_heads(q_ref[rows, :] * scale, masks)
        grad_stacked = stack_heads(out_ref[rows, :], masks)
        near = jnp.abs(gap + (block * WINDOW - start)) < WINDOW
        bias = jnp.where(near, 0.0, -1e30)
        scores = mm(k_ref[keys, :], stacked, 1, 1)
        probs = softmax_rows(scores + jnp.concatenate([bias] * heads, axis=1), 0)
        probs_grad = mm(v_ref[keys, :], grad_stacked, 1, 1)
        inner = jnp.sum(probs * probs_grad, axis=0, keepdims=True)
        score_grad = (probs * (probs_grad - inner)).astype(bf16)
        k_grad_ref[keys, :] += mm(score_grad, stacked)
        v_grad_ref[keys, :] += mm(probs.astype(bf16), grad_stacked)
        spread = mm(kt_ref[:, keys], score_grad) * scale
        for head in range(heads):
            lanes = slice(head * HEAD_DIM, (head + 1) * HEAD_DIM)
            qt_grad_ref[lanes, rows] = spread[lanes, head * WINDOW : (head + 1) * WINDOW]
        return carry

    lax.fori_loop(0, length // WINDOW, one_block, 0, unroll=True)
    light = q_ref.shape[1]
    mixed_ref[:, :light] = qt_grad_ref[...].T.astype(bf16)
    mixed_ref[:, light : 2 * light] = k_grad_ref[...].astype(bf16)
    mixed_ref[:, 2 * light :] = v_grad_ref[...].astype(bf16)
    heavy_cols = heavy_grad_ref.shape[1]
    heavy = (heavy_cols - light) // 4
    light_grad = mm(input_ref[...], mixed_ref[...], 0, 0).astype(bf16)
    ready(4)
    gain_attn_grad = 0.0
    for ref, place, owned in ((own_ref, side, True), (other_ref, 1 - side, False)):
        for start in range(0, half, tile):
            rows = pl.ds(pl.multiple_of(place * half + start, tile), tile)
            piece = slice(start, start + tile)
            pick = pick_ref[rows, :]
            back = (
                mm(mixed_ref[rows, :light], wq_ref[...], 1, 1)
                + mm(mixed_ref[rows, light : 2 * light], wk_ref[...], 1, 1)
                + mm(mixed_ref[rows, 2 * light :], wv_ref[...], 1, 1)
                + (mm(pick, back_high_ref[...]) + mm(pick, back_low_ref[...]))
            )
            values = ref[piece, :].astype(f32)
            gain_attn_grad = gain_attn_grad + jnp.sum(
                values * row_factor(values) * back, axis=0, keepdims=True
            )
            if owned:
                own_back_ref[piece, :] = back
            else:
                send_ref[piece, :] = back.astype(bf16)
    small_ref[...] = gain_attn_grad
    if len(grad_refs) == 1:
        grad_refs[0][:, :heavy_cols] = heavy_grad_ref[...]
        grad_refs[0][:, heavy_cols:] = light_grad
        return
    light_grad_ref[...] = light_grad
    for lane, (left, right, first, last) in enumerate(lane_cuts(heavy, light)):
        if right > left:
            lane_split(lane, grad_refs, 0, heavy_grad_ref, left, right)
        if last > first:
            lane_split(lane, grad_refs, right - left, light_grad_ref, first, last)


def join_kernel(lane, send_ref, got_ref, light_ref, next_keep_ref, next_send_ref, full_ref):
    model, heavy = full_ref.shape
    tall = next_send_ref.shape[0]
    light = light_ref.shape[1]
    for wrap in range(light_ref.shape[0] // tall):
        cols = slice(heavy + wrap * light, heavy + (wrap + 1) * light)
        next_send_ref[:, cols] = light_ref[wrap * tall : (wrap + 1) * tall, :]
    left = jnp.concatenate([send_ref[:, :model], got_ref[:, :model]], axis=0)
    right = jnp.concatenate([send_ref[:, model:], got_ref[:, model:]], axis=0)
    full_ref[...] = mm(left, right, 0, 0).astype(bf16)
    first, second = LANES[lane][:2]
    position = second - (1 if first < second else 0)
    mine, next_mine = my_bit(first), my_bit(second)
    block = model // PARTS
    for q in range(PARTS // 4):
        rows = slice(q * block, (q + 1) * block)
        for ref, value in ((next_keep_ref, next_mine), (next_send_ref, 1 - next_mine)):
            p = insert(q, position, value)
            ref[rows, :heavy] = full_ref[block_rows(insert(p, first, mine), block), :]


def pack_small(values, send_ref, left):
    high, low = split_low(values)
    both = jnp.concatenate([high.astype(f32), low.astype(f32)], axis=0).astype(bf16)
    wide = send_ref.shape[1] - left
    for i in range(both.shape[1] // wide):
        send_ref[16 * i : 16 * (i + 1), left:] = both[:, wide * i : wide * (i + 1)]


def unpack_small(got_ref, left, width):
    wide = got_ref.shape[1] - left
    both = jnp.concatenate(
        [got_ref[16 * i : 16 * (i + 1), left:] for i in range(width // wide)], axis=1
    ).astype(f32)
    return both[:8] + both[8:]


def fold_kernel(bit, position, block, pairs, *refs):
    next_keep_ref, next_send_ref = refs[2 * pairs :][-3:-1]
    sum_ref = refs[-1]
    extra = refs[2 * pairs : -3]
    left = 0
    for keep_ref, got_ref in zip(refs[: 2 * pairs : 2], refs[1 : 2 * pairs : 2]):
        rows, width = keep_ref.shape
        tall = min(rows, got_ref.shape[0])
        skip = got_ref.shape[1] - width * (rows // tall) if tall < rows else 0
        for wrap in range(rows // tall):
            piece = slice(wrap * tall, (wrap + 1) * tall)
            got = got_ref[:, skip + wrap * width : skip + (wrap + 1) * width]
            both = keep_ref[piece, :].astype(f32) + got.astype(f32)
            sum_ref[piece, left : left + width] = both.astype(bf16)
        left += width
    mine = my_bit(bit)
    for q in range(next_keep_ref.shape[0] // block):
        rows = slice(q * block, (q + 1) * block)
        next_keep_ref[rows, :] = sum_ref[block_rows(insert(q, position, mine), block), :]
        next_send_ref[rows, :left] = sum_ref[block_rows(insert(q, position, 1 - mine), block), :]
    if extra:
        *parts, small_ref = extra
        small = parts[0][...]
        if len(parts) == 2 and parts[1].dtype == f32:
            small = small + parts[1][...]
        elif len(parts) == 2:
            small = small + unpack_small(parts[1], parts[1].shape[1] - 128, small.shape[1])
        else:
            small = small + unpack_small(refs[1], refs[0].shape[1], small.shape[1])
        small_ref[...] = small
        pack_small(small, next_send_ref, left)


def last_fold_kernel(bit, lanes, *refs):
    extra = refs[2 * lanes : -3]
    keep_ref, send_ref, sum_ref = refs[-3:]
    left = 0
    for lane in range(lanes):
        width = refs[lane].shape[1]
        both = refs[lane][...].astype(f32) + refs[lanes + lane][:, :width].astype(f32)
        sum_ref[:, left : left + width] = both
        left += width
    mine = my_bit(bit)
    block = keep_ref.shape[0]
    keep_ref[...] = sum_ref[block_rows(mine, block), :]
    send_ref[:, :left] = sum_ref[block_rows(1 - mine, block), :].astype(bf16)
    if extra:
        small = extra[0][...]
        small = small + unpack_small(refs[lanes], refs[0].shape[1], small.shape[1])
        extra[1][...] = small
        pack_small(small, send_ref, left)


def final_kernel(widths, keep_ref, got_ref, *refs):
    left = 0
    outs = refs
    if len(refs) > len(widths):
        small_ref, *outs = refs
        total = keep_ref.shape[1]
        small = small_ref[...] + unpack_small(got_ref, total, small_ref.shape[1])
        for i, out_ref in enumerate(outs[len(widths) :]):
            out_ref[...] = small[i]
    for width, out_ref in zip(widths, outs):
        cols = slice(left, left + width)
        out_ref[...] = keep_ref[:, cols] + got_ref[:, cols].astype(f32)
        left += width


def fold(bit, position, block, *pairs, extra=()):
    rows = pairs[0].shape[0]
    width = sum(pair.shape[1] for pair in pairs[::2])
    ride = 128 if extra else 0
    return whole(
        functools.partial(fold_ride if extra else fold_kernel, bit, position, block, len(pairs) // 2),
        "fold",
        2,
        [((rows // 2, width), bf16), ((rows // 2, width + ride), bf16)]
        + [(item.shape, f32) for item in extra[:1]],
        [((rows, width), bf16)],
        *pairs,
        *extra,
    )


def fold_ride(bit, position, block, pairs, *refs):
    keep_ref, send_ref, small_ref, sum_ref = refs[-4:]
    fold_kernel(bit, position, block, pairs, *refs[:-4], small_ref, keep_ref, send_ref, sum_ref)


def last_fold(bit, keeps, gots, extra=()):
    rows = keeps[0].shape[0]
    width = sum(keep.shape[1] for keep in keeps)
    ride = 256 if extra else 0
    return whole(
        functools.partial(last_ride if extra else last_fold_kernel, bit, len(keeps)),
        "last_fold",
        2,
        [((rows // 2, width), f32), ((rows // 2, width + ride), bf16)]
        + [(item.shape, f32) for item in extra[:1]],
        [((rows, width), f32)],
        *keeps,
        *gots,
        *extra,
    )


def last_ride(bit, lanes, *refs):
    keep_ref, send_ref, small_ref, sum_ref = refs[-4:]
    last_fold_kernel(bit, lanes, *refs[:-4], small_ref, keep_ref, send_ref, sum_ref)


def final(widths, keep, got, extra=()):
    return whole(
        functools.partial(final_kernel, widths),
        "final",
        2,
        [((keep.shape[0], width), f32, 0) for width in widths]
        + [((item.shape[1],), f32, 0) for item in extra for _ in range(5)],
        [],
        keep,
        got,
        *extra,
    )


def whole(kernel, name, micros, outs, scratch, *operands, outside=0):
    inside = len(operands) - outside
    spaces = [pltpu.VMEM] * inside + [pltpu.HBM] * outside
    operands = [
        pltpu.with_memory_space_constraint(item, space) for item, space in zip(operands, spaces)
    ]
    shapes = [
        pltpu.VMEM(*out) if len(out) == 2 else jax.ShapeDtypeStruct(*out[:2]) for out in outs
    ]
    stage = [pltpu.VMEM(item.shape, item.dtype) for item in operands[inside:]]
    if outside:
        stage.append(pltpu.SemaphoreType.DMA((outside,)))

    def staged(*refs):
        if not outside:
            return kernel(*refs)
        sources, kept, sems = refs[inside : inside + outside], refs[-1 - outside : -1], refs[-1]
        copies = [
            pltpu.make_async_copy(source, target, sems.at[i])
            for i, (source, target) in enumerate(zip(sources, kept))
        ]
        for copy in copies:
            copy.start()
        waited = [False] * outside

        def ready(count):
            for i in range(count):
                if not waited[i]:
                    copies[i].wait()
                    waited[i] = True

        kernel(ready, *refs[:inside], *kept, *refs[inside + outside : -1 - outside])

    return pl.pallas_call(
        staged,
        name=name,
        out_shape=shapes,
        in_specs=[pl.BlockSpec(memory_space=space) for space in spaces],
        out_specs=[pl.BlockSpec(memory_space=pltpu.VMEM)] * len(outs),
        scratch_shapes=[pltpu.VMEM(shape, dtype) for shape, dtype in scratch] + stage,
        compiler_params=pltpu.CompilerParams(vmem_limit_bytes=VMEM_LIMIT),
        cost_estimate=pl.CostEstimate(
            flops=micros * 10**9, transcendentals=0, bytes_accessed=micros * 10**6
        ),
    )(*operands)


def body(
    tokens,
    cotangent,
    gain_attn,
    gain_ffn,
    route_query,
    route_key,
    route_ffn,
    light_query,
    light_key,
    light_value,
    light_out,
    heavy_query,
    heavy_key,
    heavy_value,
    heavy_out,
    light_gate,
    light_up,
    light_down,
    heavy_gate,
    heavy_up,
    heavy_down,
    query_index,
    key_index,
    ffn_index,
):
    half, width = tokens.shape
    length = 2 * half
    routed = query_index.shape[1]
    light = light_query.shape[1]
    heavy = heavy_query.shape[1]
    light_ff = light_gate.shape[1]
    heavy_ff = heavy_gate.shape[1]
    other_tokens = pair_swap(tokens)
    attn_weights = (
        heavy_query,
        heavy_key,
        heavy_value,
        heavy_out,
        light_query,
        light_key,
        light_value,
        light_out,
    )
    columns = jnp.concatenate([query_index, key_index, ffn_index], axis=1).reshape(-1, 1)
    attn_partial, *saved, token_rows, swap_rows, ffn_pick = whole(
        attn_forward_kernel,
        "attn_forward",
        16,
        [((length, width), bf16)] * 2
        + [((length, light), bf16)] * 4
        + [((routed, width), bf16)] * 3
        + [((routed, heavy), bf16)] * 3
        + [((routed, heavy), f32), ((routed, heavy), bf16)]
        + [((routed, width), bf16), ((2 * routed, width), bf16), ((length, routed), bf16)],
        [((length, routed), bf16)],
        other_tokens,
        columns,
        gain_attn,
        route_query,
        route_key,
        query_index,
        ffn_index,
        tokens,
        cotangent,
        *attn_weights,
        outside=7 + len(attn_weights),
    )
    got_rows = pair_swap(swap_rows)
    other_cotangent = pair_swap(after(got_rows, cotangent))
    partial_got = pair_swap(after(got_rows, attn_partial))
    tuned = lax.axis_size("dp") == PARTS
    *sends, rows_back, route_ffn_grad = whole(
        ffn_heavy_kernel,
        "ffn_heavy",
        12,
        [((routed, width + heavy_ff), bf16)] * 3 + [((routed, width), f32), ((1, width), f32)],
        [],
        heavy_gate,
        heavy_up,
        heavy_down,
        token_rows,
        swap_rows,
        got_rows,
        gain_ffn,
        route_ffn,
        outside=2,
    )
    if tuned:
        gots = [swap_bit(send, order[0]) for send, order in zip(sends, LANES)]
    ffn_back, block_own, block_send, middle, *light_parts = whole(
        ffn_light_kernel,
        "ffn_light",
        12,
        [
            ((length, width), bf16),
            ((half, width), f32),
            ((half, width), bf16),
            ((length, width), f32),
        ]
        + ([((width // 2, light_ff), bf16)] * 6 if tuned else [((width, 3 * light_ff), bf16)]),
        ([((width, 3 * light_ff), bf16)] if tuned else [])
        + [
            ((length, light_ff), bf16),
            ((length, 2 * light_ff), bf16),
            ((length, width), bf16),
            ((length, width), bf16),
        ],
        other_tokens,
        attn_partial,
        partial_got,
        other_cotangent,
        ffn_pick,
        rows_back,
        *sends,
        heavy_gate,
        heavy_up,
        heavy_down,
        light_gate,
        light_up,
        light_down,
        gain_ffn,
        tokens,
        cotangent,
        outside=3,
    )
    if tuned:
        back_got = pair_swap(after(tuple(gots), ffn_back))
        light_keeps = light_parts[:3]
        light_sends = light_parts[3:]
        token = ffn_back
        ffn_keeps, ffn_sends = [], []
        for lane in range(3):
            keep, send = whole(
                functools.partial(join_kernel, lane),
                "join",
                3,
                [((width // 4, heavy_ff), bf16), ((width // 4, heavy_ff + 2 * light_ff), bf16)],
                [((width, heavy_ff), bf16)],
                after(token, sends[lane]),
                gots[lane],
                light_sends[RIDES[lane]],
            )
            token = keep
            ffn_keeps.append(keep)
            ffn_sends.append(send)
        ffn_gots = [swap_bit(send, order[1]) for send, order in zip(ffn_sends, LANES)]
        ffn_back = after(token, ffn_back)
    else:
        back_got = pair_swap(ffn_back)
    attn_input, q_light, k_light, v_light, *routed_saved = saved
    own_middle, out_back, heavy_grad, back_high, back_low, pick, small = whole(
        attn_backward_kernel,
        "attn_backward",
        10,
        [
            ((half, width), f32),
            ((length, light), bf16),
            ((width, 4 * heavy + light), bf16),
            ((2 * routed, width), bf16),
            ((2 * routed, width), bf16),
            ((length, 2 * routed), bf16),
            ((8, width), f32),
        ],
        [((length, width), bf16)],
        other_cotangent,
        middle,
        ffn_back,
        back_got,
        *routed_saved,
        gain_ffn,
        route_query,
        route_key,
        query_index,
        key_index,
        cotangent,
        light_out,
        heavy_out,
        heavy_query,
        heavy_key,
        heavy_value,
        outside=11,
    )
    block = width // lax.axis_size("dp")
    own_back, back_send, gain_attn_grad, *attn_grads = whole(
        light_backward_kernel,
        "light_backward",
        16,
        [((half, width), f32), ((half, width), bf16), ((1, width), f32)]
        + (
            [
                ((width // 2, right - left + last - first), bf16)
                for left, right, first, last in lane_cuts(heavy, light)
            ]
            * 2
            if tuned
            else [((width, 4 * heavy + 4 * light), bf16)]
        ),
        [
            ((width, 3 * light), bf16),
            ((light, length), bf16),
            ((light, length), f32),
            ((length, light), f32),
            ((length, light), f32),
            ((length, 3 * light), bf16),
        ],
        other_tokens,
        attn_input,
        q_light,
        k_light,
        v_light,
        out_back,
        heavy_grad,
        back_high,
        back_low,
        pick,
        tokens,
        light_query,
        light_key,
        light_value,
        outside=4,
    )
    small = small + jnp.pad(route_ffn_grad, ((4, 3), (0, 0)))
    small = small + jnp.pad(gain_attn_grad, ((0, 7), (0, 0)))
    if tuned:
        attn_keeps = attn_grads[:3]

        def middle_stage(orders, stage, token, pairs, extra, rider_lane):
            next_keeps, next_gots = [], []
            for lane, order in enumerate(orders):
                left = sorted(order[stage:])
                keep, send, *small = fold(
                    order[stage],
                    left.index(order[stage]),
                    block,
                    after(token, pairs[lane][0]),
                    *pairs[lane][1:],
                    extra=extra if lane == rider_lane else (),
                )
                if lane == rider_lane:
                    rider = small
                token = keep
                next_keeps.append(keep)
                next_gots.append(swap_bit(send, order[stage]))
            return token, next_keeps, next_gots, rider

        token, ffn_keeps, ffn_gots_next, rider = middle_stage(
            LANES, 2, gain_attn_grad, list(zip(ffn_keeps, ffn_gots)), (small, pair_swap(small)), 1
        )
        block_got = pair_swap(after(token, block_send))
        block_out = (block_own + block_got.astype(f32)).astype(bf16)
        back_got = pair_swap(after(token, back_send))
        input_grad = input_rule(tokens, gain_attn, own_middle, own_back, back_got)
        attn_gots = [
            swap_bit(after((*ffn_gots_next, block_out, input_grad), send), ATTN_LANES[lane][0])
            for lane, send in enumerate(attn_grads[3:])
        ]
        ffn_keep, ffn_send = last_fold(3, [after(token, ffn_keeps[0]), *ffn_keeps[1:]], ffn_gots_next)
        ffn_got = swap_bit(ffn_send, 3)
        token, attn_keeps, attn_gots, rider = middle_stage(
            ATTN_LANES,
            1,
            ffn_keep,
            [
                (attn_keeps[lane], attn_gots[lane], light_keeps[lane], got)
                for lane, got in enumerate(ffn_gots[RIDES.index(i)] for i in range(3))
            ],
            (*rider, ffn_gots_next[1]),
            0,
        )
        hg, hu, hd = final([heavy_ff] * 3, after(token, ffn_keep), ffn_got)
        token, attn_keeps, attn_gots, rider = middle_stage(
            ATTN_LANES, 2, hg, list(zip(attn_keeps, attn_gots)), tuple(rider), 0
        )
        attn_keep, attn_send, rider = last_fold(
            3, [after(token, attn_keeps[0]), attn_keeps[2]], attn_gots[::2], extra=tuple(rider)
        )
        attn_got = swap_bit(attn_send, 3)
        side_keep, side_send = last_fold(0, [after(attn_keep, attn_keeps[1])], attn_gots[1:2])
        side_got = swap_bit(side_send, 0)
        hv, ho, lu = final([heavy, heavy, light_ff], side_keep, side_got)
        widths = [heavy, heavy, light, light_ff, light, light, light, light_ff]
        pieces = final(widths, after(hv, attn_keep), attn_got, extra=(rider,))
        hq, hk, lq, lg, lo, lk, lv, ld, *small_summed = pieces
    else:
        small_summed = butterfly_sum(small)
        block_out = (block_own + pair_swap(block_send).astype(f32)).astype(bf16)
        input_grad = input_rule(tokens, gain_attn, own_middle, own_back, pair_swap(back_send))
    if not tuned:
        order = list(range(lax.axis_size("dp").bit_length() - 1))
        hg, hu, hd = (
            halving_sum(mm(send[:, :width], send[:, width:], 0, 0).astype(bf16), order)
            for send in sends
        )
        lg, lu, ld = jnp.split(halving_sum(light_parts[0], order), 3, axis=1)
        attn_sum = halving_sum(attn_grads[0], order)
        cuts = [heavy, 2 * heavy, 3 * heavy, 4 * heavy, 4 * heavy + light]
        cuts += [4 * heavy + 2 * light, 4 * heavy + 3 * light]
        hq, hk, hv, ho, lo, lq, lk, lv = jnp.split(attn_sum, cuts, axis=1)
    return (
        block_out,
        input_grad,
        small_summed[0],
        small_summed[1],
        small_summed[2],
        small_summed[3],
        small_summed[4],
        lq,
        lk,
        lv,
        lo.T,
        hq,
        hk,
        hv,
        ho.T,
        lg,
        lu,
        ld.T,
        hg,
        hu,
        hd.T,
    )


def solution(mesh):
    in_specs = (
        P(("dp", "tensor"), None),
        P(("dp", "tensor"), None),
        P(),
        P(),
        P(),
        P(),
        P(),
        P(None, "tensor"),
        P(None, "tensor"),
        P(None, "tensor"),
        P("tensor", None),
        P(None, "tensor"),
        P(None, "tensor"),
        P(None, "tensor"),
        P("tensor", None),
        P(None, "tensor"),
        P(None, "tensor"),
        P("tensor", None),
        P(None, "tensor"),
        P(None, "tensor"),
        P("tensor", None),
        P("dp", None),
        P("dp", None),
        P("dp", None),
    )
    out_specs = (
        P(("dp", "tensor"), None),
        P(("dp", "tensor"), None),
        P(),
        P(),
        P(),
        P(),
        P(),
        P("dp", "tensor"),
        P("dp", "tensor"),
        P("dp", "tensor"),
        P("tensor", "dp"),
        P("dp", "tensor"),
        P("dp", "tensor"),
        P("dp", "tensor"),
        P("tensor", "dp"),
        P("dp", "tensor"),
        P("dp", "tensor"),
        P("tensor", "dp"),
        P("dp", "tensor"),
        P("dp", "tensor"),
        P("tensor", "dp"),
    )
    return jax.shard_map(body, mesh=mesh, in_specs=in_specs, out_specs=out_specs, check_vma=False)
```

```python
import functools

import jax
import jax.numpy as jnp
from jax import lax
from jax.experimental import pallas as pl
from jax.experimental.pallas import tpu as pltpu
from jax.sharding import PartitionSpec as P

HEAD_DIM = 64
WINDOW = 128
EPS = 1e-06
VMEM_LIMIT = 20 * 1024 * 1024
f32 = jnp.float32
bf16 = jnp.bfloat16


def pair_swap(values):
    return lax.ppermute(values, "tensor", [(0, 1), (1, 0)])


def halving_sum(values, order):
    parts = lax.axis_size("dp")
    place = lax.axis_index("dp")
    bits = list(range(len(order) - 1, -1, -1))
    held = values.reshape((2,) * len(bits) + (values.shape[0] // parts, values.shape[1]))
    held = held.astype(jnp.bfloat16)
    for step, bit in enumerate(order):
        axis = bits.index(bit)
        bits.remove(bit)
        mine = (place >> bit) & 1
        keep = lax.dynamic_index_in_dim(held, mine, axis, keepdims=False)
        send = lax.dynamic_index_in_dim(held, 1 - mine, axis, keepdims=False)
        got = lax.ppermute(send, "dp", [(i, i ^ (1 << bit)) for i in range(parts)])
        held = keep.astype(jnp.float32) + got.astype(jnp.float32)
        if step < len(order) - 1:
            held = held.astype(jnp.bfloat16)
    return held


def butterfly_sum(values):
    parts = lax.axis_size("dp")
    values = values + pair_swap(values)
    for bit in range(parts.bit_length() - 1):
        values = values + lax.ppermute(values, "dp", [(i, i ^ (1 << bit)) for i in range(parts)])
    return values


PARTS = 16
LANES = ((0, 1, 2, 3), (1, 2, 0, 3), (2, 0, 1, 3))
RIDES = (1, 2, 0)
ATTN_LANES = ((0, 1, 2, 3), (1, 2, 3, 0), (2, 0, 1, 3))


def insert(number, bit, value):
    low = number & ((1 << bit) - 1)
    return ((number - low) << 1) | (value << bit) | low


def row_of(ref):
    return ref[...].reshape(1, -1)


def input_rule(tokens, gain, own_middle, own_back, got):
    normed_grad = own_back + got.astype(f32)
    values = tokens.astype(f32)
    factor = row_factor(values)
    scaled = values * factor
    gained = gain * normed_grad
    inner = jnp.mean(scaled * gained, axis=-1, keepdims=True)
    return (own_middle + factor * (gained - scaled * inner)).astype(bf16)


def after(token, values):
    return lax.optimization_barrier((values, token))[0]


def block_rows(index, block):
    return pl.ds(pl.multiple_of(index * block, 16), block)


def swap_bit(values, bit):
    parts = lax.axis_size("dp")
    return lax.ppermute(values, "dp", [(i, i ^ (1 << bit)) for i in range(parts)])


def my_bit(bit):
    return lax.shift_right_logical(lax.axis_index("dp"), bit) & 1


def mm(left, right, left_dim=1, right_dim=0):
    return lax.dot_general(
        left, right, (((left_dim,), (right_dim,)), ((), ())), preferred_element_type=f32
    )


def split_low(values):
    high = values.astype(bf16)
    return high, (values - high.astype(f32)).astype(bf16)


def sigmoid(values):
    return 1.0 / (1.0 + jnp.exp(-values))


def row_factor(values):
    return lax.rsqrt(jnp.mean(values * values, axis=-1, keepdims=True) + EPS)


def picks(index_ref, length):
    rows = lax.broadcasted_iota(jnp.int32, (length, index_ref.shape[1]), 0)
    return jnp.where(rows == index_ref[...], 1.0, 0.0).astype(bf16)


def row_picks(columns_ref, length):
    rows = columns_ref.shape[0]
    cols = lax.broadcasted_iota(jnp.int32, (rows, length), 1)
    return jnp.where(cols == columns_ref[...], 1.0, 0.0).astype(bf16)


def head_masks(width):
    lanes = lax.shift_right_logical(lax.broadcasted_iota(jnp.int32, (1, width), 1), 6)
    return [jnp.where(lanes == head, 1.0, 0.0).astype(f32) for head in range(width // HEAD_DIM)]


def stack_heads(values, masks):
    return jnp.concatenate([values * mask.astype(values.dtype) for mask in masks], axis=0)


def unstack_heads(values, masks):
    rows = values.shape[0] // len(masks)
    total = values[:rows] * masks[0]
    for head in range(1, len(masks)):
        total = total + values[head * rows : (head + 1) * rows] * masks[head]
    return total


def softmax_rows(scores, axis):
    exponent = jnp.exp(scores - jnp.max(scores, axis=axis, keepdims=True))
    return exponent * (1.0 / jnp.sum(exponent, axis=axis, keepdims=True))


def window_start(block, length):
    start = jnp.clip(block * WINDOW - WINDOW, 0, length - 3 * WINDOW)
    return pl.multiple_of(start, WINDOW)


def attn_forward_kernel(
    ready,
    other_ref,
    columns_ref,
    gain_ref,
    route_query_ref,
    route_key_ref,
    query_index_ref,
    ffn_index_ref,
    own_ref,
    cot_ref,
    hq_ref,
    hk_ref,
    hv_ref,
    ho_ref,
    wq_ref,
    wk_ref,
    wv_ref,
    wo_ref,
    partial_ref,
    input_ref,
    q_ref,
    k_ref,
    v_ref,
    result_ref,
    query_rows_ref,
    key_raw_ref,
    key_rows_ref,
    qh_ref,
    kh_ref,
    vh_ref,
    raw_ref,
    heavy_result_ref,
    token_rows_ref,
    swap_rows_ref,
    ffn_pick_ref,
    pick_ref,
):
    ready(5)
    side = lax.axis_index("tensor")
    half = own_ref.shape[0]
    length = 2 * half
    tile = 256
    for ref, place in ((other_ref, 1 - side), (own_ref, side)):
        if ref is own_ref:
            ready(6)
        for start in range(0, half, tile):
            values = ref[start : start + tile, :].astype(f32)
            normed = values * row_factor(values) * row_of(gain_ref)
            rows = pl.ds(pl.multiple_of(place * half + start, tile), tile)
            input_ref[rows, :] = normed.astype(bf16)
    routed = query_index_ref.shape[1]
    pick_ref[...] = picks(query_index_ref, length)
    ffn_pick_ref[...] = picks(ffn_index_ref, length)
    picker = row_picks(columns_ref, length)
    picked = mm(picker[: 2 * routed], input_ref[...])
    own_pick = ffn_pick_ref[pl.ds(pl.multiple_of(side * half, half), half), :]
    other_pick = ffn_pick_ref[pl.ds(pl.multiple_of((1 - side) * half, half), half), :]
    token_rows = mm(own_pick, own_ref[...], 0, 0) + mm(other_pick, other_ref[...], 0, 0)
    token_rows_ref[...] = token_rows.astype(bf16)
    query_rows = picked[:routed]
    key_raw = picked[routed:]
    query_score = sigmoid(jnp.sum(query_rows * row_of(route_query_ref), axis=-1, keepdims=True))
    key_score = sigmoid(jnp.sum(key_raw * row_of(route_key_ref), axis=-1, keepdims=True))
    query_rows_ref[...] = query_rows.astype(bf16)
    key_raw_ref[...] = key_raw.astype(bf16)
    key_rows_ref[...] = (key_score * key_raw).astype(bf16)
    ready(11)
    swap_rows_ref[routed:, :] = mm(own_pick, cot_ref[...], 0, 0).astype(bf16)
    qh_ref[...] = mm(query_rows_ref[...], hq_ref[...]).astype(bf16)
    kh_ref[...] = mm(key_rows_ref[...], hk_ref[...]).astype(bf16)
    vh_ref[...] = mm(key_rows_ref[...], hv_ref[...]).astype(bf16)
    pair = 2 * HEAD_DIM
    pair_masks = head_masks(pair)
    for start in range(0, qh_ref.shape[1], pair):
        cols = slice(start, start + pair)
        stacked = stack_heads(qh_ref[:, cols] * (HEAD_DIM**-0.5), pair_masks)
        probs = softmax_rows(mm(stacked, kh_ref[:, cols], 1, 1), -1)
        raw_ref[:, cols] = unstack_heads(mm(probs.astype(bf16), vh_ref[:, cols]), pair_masks)
    heavy_result_ref[...] = (query_score * raw_ref[...]).astype(bf16)
    high, low = split_low(mm(heavy_result_ref[...], ho_ref[...]))

    ready(15)
    for start in range(0, length, tile):
        rows = slice(start, start + tile)
        q_ref[rows, :] = mm(input_ref[rows, :], wq_ref[...]).astype(bf16)
        k_ref[rows, :] = mm(input_ref[rows, :], wk_ref[...]).astype(bf16)
        v_ref[rows, :] = mm(input_ref[rows, :], wv_ref[...]).astype(bf16)

    masks = head_masks(q_ref.shape[1])
    heads = len(masks)
    gap = lax.broadcasted_iota(jnp.int32, (WINDOW, 3 * WINDOW), 0) - lax.broadcasted_iota(
        jnp.int32, (WINDOW, 3 * WINDOW), 1
    )

    def one_block(block, carry):
        rows = pl.ds(pl.multiple_of(block * WINDOW, WINDOW), WINDOW)
        start = window_start(block, length)
        keys = pl.ds(start, 3 * WINDOW)
        stacked = stack_heads(q_ref[rows, :] * (HEAD_DIM**-0.5), masks)
        scores = mm(stacked, k_ref[keys, :], 1, 1)
        near = jnp.abs(gap + (block * WINDOW - start)) < WINDOW
        bias = jnp.where(near, 0.0, -1e30)
        probs = softmax_rows(scores + jnp.concatenate([bias] * heads, axis=0), -1)
        out = unstack_heads(mm(probs.astype(bf16), v_ref[keys, :]), masks)
        result_ref[rows, :] = out.astype(bf16)
        return carry

    lax.fori_loop(0, length // WINDOW, one_block, 0, unroll=True)
    for start in range(0, length, tile):
        rows = slice(start, start + tile)
        pick = pick_ref[rows, :]
        partial_ref[rows, :] = (
            mm(result_ref[rows, :], wo_ref[...]) + (mm(pick, high) + mm(pick, low))
        ).astype(bf16)
    swap_rows_ref[:routed, :] = mm(picker[2 * routed :], partial_ref[...]).astype(bf16)


def gelu_parts(values):
    density = jnp.exp(-0.5 * values * values) * 0.3989422804014327
    below = 0.5 * (1.0 + lax.erf(values * 0.7071067811865476))
    return values * below, below + values * density


def ffn_heavy_kernel(
    ready,
    hg_ref,
    hu_ref,
    hd_ref,
    token_rows_ref,
    mine_ref,
    got_ref,
    gain_ref,
    route_ref,
    send_x_ref,
    send_y_ref,
    send_z_ref,
    rows_back_ref,
    route_grad_ref,
):
    routed, model = token_rows_ref.shape
    rows = slice(0, routed)
    middle = token_rows_ref[...].astype(f32) + (
        mine_ref[rows, :].astype(f32) + got_ref[rows, :].astype(f32)
    )
    cot_rows = mine_ref[routed:, :] + got_ref[routed:, :]
    ready(2)
    rows_low = (middle * row_factor(middle) * row_of(gain_ref)).astype(bf16)
    ffn_rows = rows_low.astype(f32)
    send_x_ref[:, :model] = rows_low
    send_y_ref[:, :model] = rows_low
    send_z_ref[:, :model] = cot_rows
    score = sigmoid(jnp.sum(ffn_rows * row_of(route_ref), axis=-1, keepdims=True))
    chunk = 512
    score_grad = 0.0
    for start in range(0, hg_ref.shape[1], chunk):
        cols = slice(start, start + chunk)
        out_cols = slice(model + start, model + start + chunk)
        gate = mm(rows_low, hg_ref[:, cols])
        up = mm(rows_low, hu_ref[:, cols])
        act_grad = mm(cot_rows, hd_ref[cols, :], 1, 1)
        gelu, slope = gelu_parts(gate)
        mixed = gelu * up
        score_grad = score_grad + jnp.sum(act_grad * mixed, axis=-1, keepdims=True)
        scaled = score * act_grad
        send_x_ref[:, out_cols] = (scaled * up * slope).astype(bf16)
        send_y_ref[:, out_cols] = (scaled * gelu).astype(bf16)
        send_z_ref[:, out_cols] = (score * mixed).astype(bf16)
    logit_grad = score * (1.0 - score) * score_grad
    route_grad_ref[...] = jnp.sum(ffn_rows * logit_grad, axis=0, keepdims=True)
    rows_back_ref[...] = logit_grad * row_of(route_ref)


def ffn_light_kernel(
    ready,
    other_ref,
    mine_ref,
    got_ref,
    cot_other_ref,
    pick_ref,
    rows_back_ref,
    gate_grad_ref,
    up_grad_ref,
    act_heavy_ref,
    hg_ref,
    hu_ref,
    hd_ref,
    wg_ref,
    wu_ref,
    wd_ref,
    gain_ref,
    own_ref,
    cot_own_ref,
    back_ref,
    block_own_ref,
    block_send_ref,
    middle_ref,
    *rest,
):
    lane_refs = rest[:-5]
    light_grad_ref, act_ref, mix_ref, input_ref, cot_ref = rest[-5:]
    side = lax.axis_index("tensor")
    half = block_own_ref.shape[0]
    tile = 256
    ready(1)
    for ref, cot, place in ((other_ref, cot_other_ref, 1 - side), (own_ref, cot_own_ref, side)):
        if ref is own_ref:
            ready(3)

        def norm_tile(step, carry, ref=ref, cot=cot, place=place):
            start = pl.multiple_of(step * tile, tile)
            rows = pl.ds(pl.multiple_of(place * half + start, tile), tile)
            branch = mine_ref[rows, :].astype(f32) + got_ref[rows, :].astype(f32)
            middle = ref[pl.ds(start, tile), :].astype(f32) + branch
            middle_ref[rows, :] = middle
            input_ref[rows, :] = (middle * row_factor(middle) * row_of(gain_ref)).astype(bf16)
            cot_ref[rows, :] = cot[pl.ds(start, tile), :]
            return carry

        lax.fori_loop(0, half // tile, norm_tile, 0)
    model = input_ref.shape[1]
    down_high, down_low = split_low(mm(act_heavy_ref[:, model:], hd_ref[...]))
    down = jnp.concatenate([down_high, down_low], axis=0)
    rows_back = (
        rows_back_ref[...]
        + mm(gate_grad_ref[:, model:], hg_ref[...], 1, 1)
        + mm(up_grad_ref[:, model:], hu_ref[...], 1, 1)
    )
    rows_back = jnp.concatenate(split_low(rows_back), axis=0)
    width = wg_ref.shape[1]

    def one_tile(step, carry):
        rows = pl.ds(pl.multiple_of(step * tile, tile), tile)
        gate = mm(input_ref[rows, :], wg_ref[...])
        up = mm(input_ref[rows, :], wu_ref[...])
        act_grad = mm(cot_ref[rows, :], wd_ref[...], 1, 1)
        gelu, slope = gelu_parts(gate)
        act_ref[rows, :] = (gelu * up).astype(bf16)
        mix_ref[rows, :width] = (act_grad * up * slope).astype(bf16)
        mix_ref[rows, width:] = (act_grad * gelu).astype(bf16)
        pick = jnp.concatenate([pick_ref[rows, :]] * 2, axis=1)
        branch = mm(act_ref[rows, :], wd_ref[...]) + mm(pick, down)
        owned = step * tile >= half
        owned = jnp.where(side == 1, owned, jnp.logical_not(owned))
        piece = pl.ds(pl.multiple_of((step * tile) & (half - 1), tile), tile)

        @pl.when(owned)
        def _():
            block_own_ref[piece, :] = middle_ref[rows, :] + branch

        @pl.when(jnp.logical_not(owned))
        def _():
            block_send_ref[piece, :] = branch.astype(bf16)

        back_ref[rows, :] = (
            mm(mix_ref[rows, :width], wg_ref[...], 1, 1)
            + mm(mix_ref[rows, width:], wu_ref[...], 1, 1)
            + mm(pick, rows_back)
        ).astype(bf16)
        return carry

    lax.fori_loop(0, 2 * half // tile, one_tile, 0)
    light_grad_ref[:, : 2 * width] = mm(input_ref[...], mix_ref[...], 0, 0).astype(bf16)
    light_grad_ref[:, 2 * width :] = mm(cot_ref[...], act_ref[...], 0, 0).astype(bf16)
    for lane in range(len(lane_refs) // 2):
        lane_split(lane, lane_refs, 0, light_grad_ref, lane * width, (lane + 1) * width)


def lane_split(lane, lane_refs, left, grad_ref, first, last):
    bit = LANES[lane][0]
    mine = my_bit(bit)
    block = grad_ref.shape[0] // PARTS
    keep_ref, send_ref = lane_refs[lane], lane_refs[len(lane_refs) // 2 + lane]
    for p in range(PARTS // 2):
        rows = slice(p * block, (p + 1) * block)
        cols = slice(left, left + last - first)
        for ref, value in ((keep_ref, mine), (send_ref, 1 - mine)):
            ref[rows, cols] = grad_ref[block_rows(insert(p, bit, value), block), first:last]


def attn_backward_kernel(
    ready,
    cot_other_ref,
    middle_ref,
    mine_ref,
    got_ref,
    result_ref,
    query_rows_ref,
    key_raw_ref,
    key_rows_ref,
    qh_ref,
    kh_ref,
    vh_ref,
    raw_ref,
    heavy_result_ref,
    gain_ffn_ref,
    route_query_ref,
    route_key_ref,
    query_index_ref,
    key_index_ref,
    cot_own_ref,
    wo_ref,
    ho_ref,
    hq_ref,
    hk_ref,
    hv_ref,
    own_middle_ref,
    out_ref,
    grad_ref,
    back_high_ref,
    back_low_ref,
    pick_ref,
    small_ref,
    low_ref,
):
    ready(5)
    side = lax.axis_index("tensor")
    half = cot_own_ref.shape[0]
    length = 2 * half
    tile = 256
    scale = HEAD_DIM**-0.5
    heavy = qh_ref.shape[1]
    light = result_ref.shape[1]
    gain_ffn_grad = 0.0
    for cot, place, owned in ((cot_other_ref, 1 - side, False), (cot_own_ref, side, True)):
        if owned:
            ready(6)
        for start in range(0, half, tile):
            rows = pl.ds(pl.multiple_of(place * half + start, tile), tile)
            piece = slice(start, start + tile)
            normed_grad = mine_ref[rows, :].astype(f32) + got_ref[rows, :].astype(f32)
            middle = middle_ref[rows, :]
            factor = row_factor(middle)
            scaled = factor * middle
            gain_ffn_grad = gain_ffn_grad + jnp.sum(scaled * normed_grad, axis=0, keepdims=True)
            gained = row_of(gain_ffn_ref) * normed_grad
            inner = jnp.mean(scaled * gained, axis=-1, keepdims=True)
            grad = cot[piece, :].astype(f32) + factor * (gained - scaled * inner)
            if owned:
                own_middle_ref[piece, :] = grad
            low_ref[rows, :] = grad.astype(bf16)
    ready(11)
    for start in range(0, length, tile):
        rows = slice(start, start + tile)
        out_ref[rows, :] = mm(low_ref[rows, :], wo_ref[...], 1, 1).astype(bf16)
    grad_ref[:, 4 * heavy :] = mm(low_ref[...], result_ref[...], 0, 0).astype(bf16)

    routed = query_index_ref.shape[1]
    pick_ref[:, :routed] = picks(query_index_ref, length)
    pick_ref[:, routed:] = picks(key_index_ref, length)
    query_rows = query_rows_ref[...].astype(f32)
    key_raw = key_raw_ref[...].astype(f32)
    query_score = sigmoid(jnp.sum(query_rows * row_of(route_query_ref), axis=-1, keepdims=True))
    key_score = sigmoid(jnp.sum(key_raw * row_of(route_key_ref), axis=-1, keepdims=True))
    mid_rows = mm(pick_ref[:, :routed], low_ref[...], 0, 0).astype(bf16)
    grad_ref[:, 3 * heavy : 4 * heavy] = mm(mid_rows, heavy_result_ref[...], 0, 0).astype(bf16)
    heavy_out_grad = mm(mid_rows, ho_ref[...], 1, 1).astype(bf16)
    query_score_grad = jnp.sum(
        heavy_out_grad.astype(f32) * raw_ref[...], axis=-1, keepdims=True
    )
    raw_high, raw_low = split_low(query_score * heavy_out_grad.astype(f32))
    pair = 2 * HEAD_DIM
    pair_masks = head_masks(pair)
    stacked_score = jnp.concatenate([query_score] * 2, axis=0)
    q_parts, k_parts, v_parts = [], [], []
    for start in range(0, heavy, pair):
        cols = slice(start, start + pair)
        stacked = stack_heads(qh_ref[:, cols] * scale, pair_masks)
        probs = softmax_rows(mm(stacked, kh_ref[:, cols], 1, 1), -1)
        grad_stacked = stack_heads(heavy_out_grad[:, cols], pair_masks)
        probs_grad = stacked_score * mm(grad_stacked, vh_ref[:, cols], 1, 1)
        inner = jnp.sum(probs * probs_grad, axis=-1, keepdims=True)
        score_grad = (probs * (probs_grad - inner)).astype(bf16)
        probs_low = probs.astype(bf16)
        q_parts.append(unstack_heads(mm(score_grad, kh_ref[:, cols]) * scale, pair_masks))
        k_parts.append(mm(score_grad, stacked, 0, 0))
        v_parts.append(
            mm(probs_low, stack_heads(raw_high[:, cols], pair_masks), 0, 0)
            + mm(probs_low, stack_heads(raw_low[:, cols], pair_masks), 0, 0)
        )
    query_heavy_grad = jnp.concatenate(q_parts, axis=1).astype(bf16)
    key_heavy_grad = jnp.concatenate(k_parts, axis=1).astype(bf16)
    value_heavy_grad = jnp.concatenate(v_parts, axis=1).astype(bf16)
    grad_ref[:, :heavy] = mm(query_rows_ref[...], query_heavy_grad, 0, 0).astype(bf16)
    grad_ref[:, heavy : 2 * heavy] = mm(key_rows_ref[...], key_heavy_grad, 0, 0).astype(bf16)
    grad_ref[:, 2 * heavy : 3 * heavy] = mm(
        key_rows_ref[...], value_heavy_grad, 0, 0
    ).astype(bf16)
    key_rows_grad = mm(key_heavy_grad, hk_ref[...], 1, 1) + mm(
        value_heavy_grad, hv_ref[...], 1, 1
    )
    key_logit_grad = (
        key_score * (1.0 - key_score) * jnp.sum(key_rows_grad * key_raw, axis=-1, keepdims=True)
    )
    query_logit_grad = query_score * (1.0 - query_score) * query_score_grad
    key_raw_grad = key_score * key_rows_grad + key_logit_grad * row_of(route_key_ref)
    query_rows_grad = mm(query_heavy_grad, hq_ref[...], 1, 1)
    query_rows_grad = query_rows_grad + query_logit_grad * row_of(route_query_ref)
    small_ref[...] = jnp.zeros_like(small_ref)
    small_ref[1:2, :] = 0.5 * gain_ffn_grad
    small_ref[2:3, :] = jnp.sum(query_rows * query_logit_grad, axis=0, keepdims=True)
    small_ref[3:4, :] = jnp.sum(key_raw * key_logit_grad, axis=0, keepdims=True)
    high, low = split_low(jnp.concatenate([query_rows_grad, key_raw_grad], axis=0))
    back_high_ref[...] = high
    back_low_ref[...] = low


def lane_cuts(heavy, light):
    return (
        (0, 2 * heavy, 0, light),
        (2 * heavy, 4 * heavy, 0, 0),
        (4 * heavy, 4 * heavy + light, light, 3 * light),
    )


def light_backward_kernel(
    ready,
    other_ref,
    input_ref,
    q_ref,
    k_ref,
    v_ref,
    out_ref,
    heavy_grad_ref,
    back_high_ref,
    back_low_ref,
    pick_ref,
    own_ref,
    wq_ref,
    wk_ref,
    wv_ref,
    own_back_ref,
    send_ref,
    small_ref,
    *rest,
):
    grad_refs = rest[:-6]
    light_grad_ref, kt_ref, qt_grad_ref, k_grad_ref, v_grad_ref, mixed_ref = rest[-6:]
    side = lax.axis_index("tensor")
    half = own_ref.shape[0]
    length = 2 * half
    tile = 256
    scale = HEAD_DIM**-0.5
    kt_ref[...] = k_ref[...].T
    k_grad_ref[...] = jnp.zeros_like(k_grad_ref)
    v_grad_ref[...] = jnp.zeros_like(v_grad_ref)
    masks = head_masks(q_ref.shape[1])
    heads = len(masks)
    gap = lax.broadcasted_iota(jnp.int32, (3 * WINDOW, WINDOW), 1) - lax.broadcasted_iota(
        jnp.int32, (3 * WINDOW, WINDOW), 0
    )

    def one_block(block, carry):
        first = pl.multiple_of(block * WINDOW, WINDOW)
        rows = pl.ds(first, WINDOW)
        start = window_start(block, length)
        keys = pl.ds(start, 3 * WINDOW)
        stacked = stack_heads(q_ref[rows, :] * scale, masks)
        grad_stacked = stack_heads(out_ref[rows, :], masks)
        near = jnp.abs(gap + (block * WINDOW - start)) < WINDOW
        bias = jnp.where(near, 0.0, -1e30)
        scores = mm(k_ref[keys, :], stacked, 1, 1)
        probs = softmax_rows(scores + jnp.concatenate([bias] * heads, axis=1), 0)
        probs_grad = mm(v_ref[keys, :], grad_stacked, 1, 1)
        inner = jnp.sum(probs * probs_grad, axis=0, keepdims=True)
        score_grad = (probs * (probs_grad - inner)).astype(bf16)
        k_grad_ref[keys, :] += mm(score_grad, stacked)
        v_grad_ref[keys, :] += mm(probs.astype(bf16), grad_stacked)
        spread = mm(kt_ref[:, keys], score_grad) * scale
        for head in range(heads):
            lanes = slice(head * HEAD_DIM, (head + 1) * HEAD_DIM)
            qt_grad_ref[lanes, rows] = spread[lanes, head * WINDOW : (head + 1) * WINDOW]
        return carry

    lax.fori_loop(0, length // WINDOW, one_block, 0)
    light = q_ref.shape[1]
    mixed_ref[:, :light] = qt_grad_ref[...].T.astype(bf16)
    mixed_ref[:, light : 2 * light] = k_grad_ref[...].astype(bf16)
    mixed_ref[:, 2 * light :] = v_grad_ref[...].astype(bf16)
    heavy_cols = heavy_grad_ref.shape[1]
    heavy = (heavy_cols - light) // 4
    light_grad = mm(input_ref[...], mixed_ref[...], 0, 0).astype(bf16)
    ready(4)
    gain_attn_grad = 0.0
    for ref, place, owned in ((own_ref, side, True), (other_ref, 1 - side, False)):
        for start in range(0, half, tile):
            rows = pl.ds(pl.multiple_of(place * half + start, tile), tile)
            piece = slice(start, start + tile)
            pick = pick_ref[rows, :]
            back = (
                mm(mixed_ref[rows, :light], wq_ref[...], 1, 1)
                + mm(mixed_ref[rows, light : 2 * light], wk_ref[...], 1, 1)
                + mm(mixed_ref[rows, 2 * light :], wv_ref[...], 1, 1)
                + (mm(pick, back_high_ref[...]) + mm(pick, back_low_ref[...]))
            )
            values = ref[piece, :].astype(f32)
            gain_attn_grad = gain_attn_grad + jnp.sum(
                values * row_factor(values) * back, axis=0, keepdims=True
            )
            if owned:
                own_back_ref[piece, :] = back
            else:
                send_ref[piece, :] = back.astype(bf16)
    small_ref[...] = gain_attn_grad
    if len(grad_refs) == 1:
        grad_refs[0][:, :heavy_cols] = heavy_grad_ref[...]
        grad_refs[0][:, heavy_cols:] = light_grad
        return
    light_grad_ref[...] = light_grad
    for lane, (left, right, first, last) in enumerate(lane_cuts(heavy, light)):
        if right > left:
            lane_split(lane, grad_refs, 0, heavy_grad_ref, left, right)
        if last > first:
            lane_split(lane, grad_refs, right - left, light_grad_ref, first, last)


def join_kernel(lane, send_ref, got_ref, light_ref, next_keep_ref, next_send_ref, full_ref):
    model, heavy = full_ref.shape
    tall = next_send_ref.shape[0]
    light = light_ref.shape[1]
    for wrap in range(light_ref.shape[0] // tall):
        cols = slice(heavy + wrap * light, heavy + (wrap + 1) * light)
        next_send_ref[:, cols] = light_ref[wrap * tall : (wrap + 1) * tall, :]
    left = jnp.concatenate([send_ref[:, :model], got_ref[:, :model]], axis=0)
    right = jnp.concatenate([send_ref[:, model:], got_ref[:, model:]], axis=0)
    full_ref[...] = mm(left, right, 0, 0).astype(bf16)
    first, second = LANES[lane][:2]
    position = second - (1 if first < second else 0)
    mine, next_mine = my_bit(first), my_bit(second)
    block = model // PARTS
    for q in range(PARTS // 4):
        rows = slice(q * block, (q + 1) * block)
        for ref, value in ((next_keep_ref, next_mine), (next_send_ref, 1 - next_mine)):
            p = insert(q, position, value)
            ref[rows, :heavy] = full_ref[block_rows(insert(p, first, mine), block), :]


def pack_small(values, send_ref, left):
    high, low = split_low(values)
    both = jnp.concatenate([high.astype(f32), low.astype(f32)], axis=0).astype(bf16)
    wide = send_ref.shape[1] - left
    for i in range(both.shape[1] // wide):
        send_ref[16 * i : 16 * (i + 1), left:] = both[:, wide * i : wide * (i + 1)]


def unpack_small(got_ref, left, width):
    wide = got_ref.shape[1] - left
    both = jnp.concatenate(
        [got_ref[16 * i : 16 * (i + 1), left:] for i in range(width // wide)], axis=1
    ).astype(f32)
    return both[:8] + both[8:]


def fold_kernel(bit, position, block, pairs, *refs):
    next_keep_ref, next_send_ref = refs[2 * pairs :][-3:-1]
    sum_ref = refs[-1]
    extra = refs[2 * pairs : -3]
    left = 0
    for keep_ref, got_ref in zip(refs[: 2 * pairs : 2], refs[1 : 2 * pairs : 2]):
        rows, width = keep_ref.shape
        tall = min(rows, got_ref.shape[0])
        skip = got_ref.shape[1] - width * (rows // tall) if tall < rows else 0
        for wrap in range(rows // tall):
            piece = slice(wrap * tall, (wrap + 1) * tall)
            got = got_ref[:, skip + wrap * width : skip + (wrap + 1) * width]
            both = keep_ref[piece, :].astype(f32) + got.astype(f32)
            sum_ref[piece, left : left + width] = both.astype(bf16)
        left += width
    mine = my_bit(bit)
    for q in range(next_keep_ref.shape[0] // block):
        rows = slice(q * block, (q + 1) * block)
        next_keep_ref[rows, :] = sum_ref[block_rows(insert(q, position, mine), block), :]
        next_send_ref[rows, :left] = sum_ref[block_rows(insert(q, position, 1 - mine), block), :]
    if extra:
        *parts, small_ref = extra
        small = parts[0][...]
        if len(parts) == 2 and parts[1].dtype == f32:
            small = small + parts[1][...]
        elif len(parts) == 2:
            small = small + unpack_small(parts[1], parts[1].shape[1] - 128, small.shape[1])
        else:
            small = small + unpack_small(refs[1], refs[0].shape[1], small.shape[1])
        small_ref[...] = small
        pack_small(small, next_send_ref, left)


def last_fold_kernel(bit, lanes, *refs):
    extra = refs[2 * lanes : -3]
    keep_ref, send_ref, sum_ref = refs[-3:]
    left = 0
    for lane in range(lanes):
        width = refs[lane].shape[1]
        both = refs[lane][...].astype(f32) + refs[lanes + lane][:, :width].astype(f32)
        sum_ref[:, left : left + width] = both
        left += width
    mine = my_bit(bit)
    block = keep_ref.shape[0]
    keep_ref[...] = sum_ref[block_rows(mine, block), :]
    send_ref[:, :left] = sum_ref[block_rows(1 - mine, block), :].astype(bf16)
    if extra:
        small = extra[0][...]
        small = small + unpack_small(refs[lanes], refs[0].shape[1], small.shape[1])
        extra[1][...] = small
        pack_small(small, send_ref, left)


def final_kernel(widths, keep_ref, got_ref, *refs):
    left = 0
    outs = refs
    if len(refs) > len(widths):
        small_ref, *outs = refs
        total = keep_ref.shape[1]
        small = small_ref[...] + unpack_small(got_ref, total, small_ref.shape[1])
        for i, out_ref in enumerate(outs[len(widths) :]):
            out_ref[...] = small[i]
    for width, out_ref in zip(widths, outs):
        cols = slice(left, left + width)
        out_ref[...] = keep_ref[:, cols] + got_ref[:, cols].astype(f32)
        left += width


def fold(bit, position, block, *pairs, extra=()):
    rows = pairs[0].shape[0]
    width = sum(pair.shape[1] for pair in pairs[::2])
    ride = 128 if extra else 0
    return whole(
        functools.partial(fold_ride if extra else fold_kernel, bit, position, block, len(pairs) // 2),
        "fold",
        2,
        [((rows // 2, width), bf16), ((rows // 2, width + ride), bf16)]
        + [(item.shape, f32) for item in extra[:1]],
        [((rows, width), bf16)],
        *pairs,
        *extra,
    )


def fold_ride(bit, position, block, pairs, *refs):
    keep_ref, send_ref, small_ref, sum_ref = refs[-4:]
    fold_kernel(bit, position, block, pairs, *refs[:-4], small_ref, keep_ref, send_ref, sum_ref)


def last_fold(bit, keeps, gots, extra=()):
    rows = keeps[0].shape[0]
    width = sum(keep.shape[1] for keep in keeps)
    ride = 256 if extra else 0
    return whole(
        functools.partial(last_ride if extra else last_fold_kernel, bit, len(keeps)),
        "last_fold",
        2,
        [((rows // 2, width), f32), ((rows // 2, width + ride), bf16)]
        + [(item.shape, f32) for item in extra[:1]],
        [((rows, width), f32)],
        *keeps,
        *gots,
        *extra,
    )


def last_ride(bit, lanes, *refs):
    keep_ref, send_ref, small_ref, sum_ref = refs[-4:]
    last_fold_kernel(bit, lanes, *refs[:-4], small_ref, keep_ref, send_ref, sum_ref)


def final(widths, keep, got, extra=()):
    return whole(
        functools.partial(final_kernel, widths),
        "final",
        2,
        [((keep.shape[0], width), f32, 0) for width in widths]
        + [((item.shape[1],), f32, 0) for item in extra for _ in range(5)],
        [],
        keep,
        got,
        *extra,
    )


def whole(kernel, name, micros, outs, scratch, *operands, outside=0):
    inside = len(operands) - outside
    spaces = [pltpu.VMEM] * inside + [pltpu.HBM] * outside
    operands = [
        pltpu.with_memory_space_constraint(item, space) for item, space in zip(operands, spaces)
    ]
    shapes = [
        pltpu.VMEM(*out) if len(out) == 2 else jax.ShapeDtypeStruct(*out[:2]) for out in outs
    ]
    stage = [pltpu.VMEM(item.shape, item.dtype) for item in operands[inside:]]
    if outside:
        stage.append(pltpu.SemaphoreType.DMA((outside,)))

    def staged(*refs):
        if not outside:
            return kernel(*refs)
        sources, kept, sems = refs[inside : inside + outside], refs[-1 - outside : -1], refs[-1]
        copies = [
            pltpu.make_async_copy(source, target, sems.at[i])
            for i, (source, target) in enumerate(zip(sources, kept))
        ]
        for copy in copies:
            copy.start()
        waited = [False] * outside

        def ready(count):
            for i in range(count):
                if not waited[i]:
                    copies[i].wait()
                    waited[i] = True

        kernel(ready, *refs[:inside], *kept, *refs[inside + outside : -1 - outside])

    return pl.pallas_call(
        staged,
        name=name,
        out_shape=shapes,
        in_specs=[pl.BlockSpec(memory_space=space) for space in spaces],
        out_specs=[pl.BlockSpec(memory_space=pltpu.VMEM)] * len(outs),
        scratch_shapes=[pltpu.VMEM(shape, dtype) for shape, dtype in scratch] + stage,
        compiler_params=pltpu.CompilerParams(vmem_limit_bytes=VMEM_LIMIT),
        cost_estimate=pl.CostEstimate(
            flops=micros * 10**9, transcendentals=0, bytes_accessed=micros * 10**6
        ),
    )(*operands)


def body(
    tokens,
    cotangent,
    gain_attn,
    gain_ffn,
    route_query,
    route_key,
    route_ffn,
    light_query,
    light_key,
    light_value,
    light_out,
    heavy_query,
    heavy_key,
    heavy_value,
    heavy_out,
    light_gate,
    light_up,
    light_down,
    heavy_gate,
    heavy_up,
    heavy_down,
    query_index,
    key_index,
    ffn_index,
):
    half, width = tokens.shape
    length = 2 * half
    routed = query_index.shape[1]
    light = light_query.shape[1]
    heavy = heavy_query.shape[1]
    light_ff = light_gate.shape[1]
    heavy_ff = heavy_gate.shape[1]
    other_tokens = pair_swap(tokens)
    attn_weights = (
        heavy_query,
        heavy_key,
        heavy_value,
        heavy_out,
        light_query,
        light_key,
        light_value,
        light_out,
    )
    columns = jnp.concatenate([query_index, key_index, ffn_index], axis=1).reshape(-1, 1)
    attn_partial, *saved, token_rows, swap_rows, ffn_pick = whole(
        attn_forward_kernel,
        "attn_forward",
        16,
        [((length, width), bf16)] * 2
        + [((length, light), bf16)] * 4
        + [((routed, width), bf16)] * 3
        + [((routed, heavy), bf16)] * 3
        + [((routed, heavy), f32), ((routed, heavy), bf16)]
        + [((routed, width), bf16), ((2 * routed, width), bf16), ((length, routed), bf16)],
        [((length, routed), bf16)],
        other_tokens,
        columns,
        gain_attn,
        route_query,
        route_key,
        query_index,
        ffn_index,
        tokens,
        cotangent,
        *attn_weights,
        outside=7 + len(attn_weights),
    )
    got_rows = pair_swap(swap_rows)
    other_cotangent = pair_swap(after(got_rows, cotangent))
    partial_got = pair_swap(after(got_rows, attn_partial))
    tuned = lax.axis_size("dp") == PARTS
    *sends, rows_back, route_ffn_grad = whole(
        ffn_heavy_kernel,
        "ffn_heavy",
        12,
        [((routed, width + heavy_ff), bf16)] * 3 + [((routed, width), f32), ((1, width), f32)],
        [],
        heavy_gate,
        heavy_up,
        heavy_down,
        token_rows,
        swap_rows,
        got_rows,
        gain_ffn,
        route_ffn,
        outside=2,
    )
    if tuned:
        gots = [swap_bit(send, order[0]) for send, order in zip(sends, LANES)]
    ffn_back, block_own, block_send, middle, *light_parts = whole(
        ffn_light_kernel,
        "ffn_light",
        12,
        [
            ((length, width), bf16),
            ((half, width), f32),
            ((half, width), bf16),
            ((length, width), f32),
        ]
        + ([((width // 2, light_ff), bf16)] * 6 if tuned else [((width, 3 * light_ff), bf16)]),
        ([((width, 3 * light_ff), bf16)] if tuned else [])
        + [
            ((length, light_ff), bf16),
            ((length, 2 * light_ff), bf16),
            ((length, width), bf16),
            ((length, width), bf16),
        ],
        other_tokens,
        attn_partial,
        partial_got,
        other_cotangent,
        ffn_pick,
        rows_back,
        *sends,
        heavy_gate,
        heavy_up,
        heavy_down,
        light_gate,
        light_up,
        light_down,
        gain_ffn,
        tokens,
        cotangent,
        outside=3,
    )
    if tuned:
        back_got = pair_swap(after(tuple(gots), ffn_back))
        light_keeps = light_parts[:3]
        light_sends = light_parts[3:]
        token = ffn_back
        ffn_keeps, ffn_sends = [], []
        for lane in range(3):
            keep, send = whole(
                functools.partial(join_kernel, lane),
                "join",
                3,
                [((width // 4, heavy_ff), bf16), ((width // 4, heavy_ff + 2 * light_ff), bf16)],
                [((width, heavy_ff), bf16)],
                after(token, sends[lane]),
                gots[lane],
                light_sends[RIDES[lane]],
            )
            token = keep
            ffn_keeps.append(keep)
            ffn_sends.append(send)
        ffn_gots = [swap_bit(send, order[1]) for send, order in zip(ffn_sends, LANES)]
        ffn_back = after(token, ffn_back)
    else:
        back_got = pair_swap(ffn_back)
    attn_input, q_light, k_light, v_light, *routed_saved = saved
    own_middle, out_back, heavy_grad, back_high, back_low, pick, small = whole(
        attn_backward_kernel,
        "attn_backward",
        10,
        [
            ((half, width), f32),
            ((length, light), bf16),
            ((width, 4 * heavy + light), bf16),
            ((2 * routed, width), bf16),
            ((2 * routed, width), bf16),
            ((length, 2 * routed), bf16),
            ((8, width), f32),
        ],
        [((length, width), bf16)],
        other_cotangent,
        middle,
        ffn_back,
        back_got,
        *routed_saved,
        gain_ffn,
        route_query,
        route_key,
        query_index,
        key_index,
        cotangent,
        light_out,
        heavy_out,
        heavy_query,
        heavy_key,
        heavy_value,
        outside=11,
    )
    block = width // lax.axis_size("dp")
    own_back, back_send, gain_attn_grad, *attn_grads = whole(
        light_backward_kernel,
        "light_backward",
        16,
        [((half, width), f32), ((half, width), bf16), ((1, width), f32)]
        + (
            [
                ((width // 2, right - left + last - first), bf16)
                for left, right, first, last in lane_cuts(heavy, light)
            ]
            * 2
            if tuned
            else [((width, 4 * heavy + 4 * light), bf16)]
        ),
        [
            ((width, 3 * light), bf16),
            ((light, length), bf16),
            ((light, length), f32),
            ((length, light), f32),
            ((length, light), f32),
            ((length, 3 * light), bf16),
        ],
        other_tokens,
        attn_input,
        q_light,
        k_light,
        v_light,
        out_back,
        heavy_grad,
        back_high,
        back_low,
        pick,
        tokens,
        light_query,
        light_key,
        light_value,
        outside=4,
    )
    small = small + jnp.pad(route_ffn_grad, ((4, 3), (0, 0)))
    small = small + jnp.pad(gain_attn_grad, ((0, 7), (0, 0)))
    if tuned:
        attn_keeps = attn_grads[:3]

        def middle_stage(orders, stage, token, pairs, extra, rider_lane):
            next_keeps, next_gots = [], []
            for lane, order in enumerate(orders):
                left = sorted(order[stage:])
                keep, send, *small = fold(
                    order[stage],
                    left.index(order[stage]),
                    block,
                    after(token, pairs[lane][0]),
                    *pairs[lane][1:],
                    extra=extra if lane == rider_lane else (),
                )
                if lane == rider_lane:
                    rider = small
                token = keep
                next_keeps.append(keep)
                next_gots.append(swap_bit(send, order[stage]))
            return token, next_keeps, next_gots, rider

        token, ffn_keeps, ffn_gots_next, rider = middle_stage(
            LANES, 2, gain_attn_grad, list(zip(ffn_keeps, ffn_gots)), (small, pair_swap(small)), 1
        )
        block_got = pair_swap(after(token, block_send))
        block_out = (block_own + block_got.astype(f32)).astype(bf16)
        back_got = pair_swap(after(token, back_send))
        input_grad = input_rule(tokens, gain_attn, own_middle, own_back, back_got)
        attn_gots = [
            swap_bit(after((*ffn_gots_next, block_out, input_grad), send), ATTN_LANES[lane][0])
            for lane, send in enumerate(attn_grads[3:])
        ]
        ffn_keep, ffn_send = last_fold(3, [after(token, ffn_keeps[0]), *ffn_keeps[1:]], ffn_gots_next)
        ffn_got = swap_bit(ffn_send, 3)
        token, attn_keeps, attn_gots, rider = middle_stage(
            ATTN_LANES,
            1,
            ffn_keep,
            [
                (attn_keeps[lane], attn_gots[lane], light_keeps[lane], got)
                for lane, got in enumerate(ffn_gots[RIDES.index(i)] for i in range(3))
            ],
            (*rider, ffn_gots_next[1]),
            0,
        )
        hg, hu, hd = final([heavy_ff] * 3, after(token, ffn_keep), ffn_got)
        token, attn_keeps, attn_gots, rider = middle_stage(
            ATTN_LANES, 2, hg, list(zip(attn_keeps, attn_gots)), tuple(rider), 0
        )
        attn_keep, attn_send, rider = last_fold(
            3, [after(token, attn_keeps[0]), attn_keeps[2]], attn_gots[::2], extra=tuple(rider)
        )
        attn_got = swap_bit(attn_send, 3)
        side_keep, side_send = last_fold(0, [after(attn_keep, attn_keeps[1])], attn_gots[1:2])
        side_got = swap_bit(side_send, 0)
        hv, ho, lu = final([heavy, heavy, light_ff], side_keep, side_got)
        widths = [heavy, heavy, light, light_ff, light, light, light, light_ff]
        pieces = final(widths, after(hv, attn_keep), attn_got, extra=(rider,))
        hq, hk, lq, lg, lo, lk, lv, ld, *small_summed = pieces
    else:
        small_summed = butterfly_sum(small)
        block_out = (block_own + pair_swap(block_send).astype(f32)).astype(bf16)
        input_grad = input_rule(tokens, gain_attn, own_middle, own_back, pair_swap(back_send))
    if not tuned:
        order = list(range(lax.axis_size("dp").bit_length() - 1))
        hg, hu, hd = (
            halving_sum(mm(send[:, :width], send[:, width:], 0, 0).astype(bf16), order)
            for send in sends
        )
        lg, lu, ld = jnp.split(halving_sum(light_parts[0], order), 3, axis=1)
        attn_sum = halving_sum(attn_grads[0], order)
        cuts = [heavy, 2 * heavy, 3 * heavy, 4 * heavy, 4 * heavy + light]
        cuts += [4 * heavy + 2 * light, 4 * heavy + 3 * light]
        hq, hk, hv, ho, lo, lq, lk, lv = jnp.split(attn_sum, cuts, axis=1)
    return (
        block_out,
        input_grad,
        small_summed[0],
        small_summed[1],
        small_summed[2],
        small_summed[3],
        small_summed[4],
        lq,
        lk,
        lv,
        lo.T,
        hq,
        hk,
        hv,
        ho.T,
        lg,
        lu,
        ld.T,
        hg,
        hu,
        hd.T,
    )


def solution(mesh):
    in_specs = (
        P(("dp", "tensor"), None),
        P(("dp", "tensor"), None),
        P(),
        P(),
        P(),
        P(),
        P(),
        P(None, "tensor"),
        P(None, "tensor"),
        P(None, "tensor"),
        P("tensor", None),
        P(None, "tensor"),
        P(None, "tensor"),
        P(None, "tensor"),
        P("tensor", None),
        P(None, "tensor"),
        P(None, "tensor"),
        P("tensor", None),
        P(None, "tensor"),
        P(None, "tensor"),
        P("tensor", None),
        P("dp", None),
        P("dp", None),
        P("dp", None),
    )
    out_specs = (
        P(("dp", "tensor"), None),
        P(("dp", "tensor"), None),
        P(),
        P(),
        P(),
        P(),
        P(),
        P("dp", "tensor"),
        P("dp", "tensor"),
        P("dp", "tensor"),
        P("tensor", "dp"),
        P("dp", "tensor"),
        P("dp", "tensor"),
        P("dp", "tensor"),
        P("tensor", "dp"),
        P("dp", "tensor"),
        P("dp", "tensor"),
        P("tensor", "dp"),
        P("dp", "tensor"),
        P("dp", "tensor"),
        P("tensor", "dp"),
    )
    return jax.shard_map(body, mesh=mesh, in_specs=in_specs, out_specs=out_specs, check_vma=False)
```

```python
import functools

import jax
import jax.numpy as jnp
from jax import lax
from jax.experimental import pallas as pl
from jax.experimental.pallas import tpu as pltpu
from jax.sharding import PartitionSpec as P

HEAD_DIM = 64
WINDOW = 128
EPS = 1e-06
VMEM_LIMIT = 20 * 1024 * 1024
f32 = jnp.float32
bf16 = jnp.bfloat16


def pair_swap(values):
    return lax.ppermute(values, "tensor", [(0, 1), (1, 0)])


def halving_sum(values, order):
    parts = lax.axis_size("dp")
    place = lax.axis_index("dp")
    bits = list(range(len(order) - 1, -1, -1))
    held = values.reshape((2,) * len(bits) + (values.shape[0] // parts, values.shape[1]))
    held = held.astype(jnp.bfloat16)
    for step, bit in enumerate(order):
        axis = bits.index(bit)
        bits.remove(bit)
        mine = (place >> bit) & 1
        keep = lax.dynamic_index_in_dim(held, mine, axis, keepdims=False)
        send = lax.dynamic_index_in_dim(held, 1 - mine, axis, keepdims=False)
        got = lax.ppermute(send, "dp", [(i, i ^ (1 << bit)) for i in range(parts)])
        held = keep.astype(jnp.float32) + got.astype(jnp.float32)
        if step < len(order) - 1:
            held = held.astype(jnp.bfloat16)
    return held


def butterfly_sum(values):
    parts = lax.axis_size("dp")
    values = values + pair_swap(values)
    for bit in range(parts.bit_length() - 1):
        values = values + lax.ppermute(values, "dp", [(i, i ^ (1 << bit)) for i in range(parts)])
    return values


PARTS = 16
LANES = ((0, 1, 2, 3), (1, 2, 0, 3), (2, 0, 1, 3))
RIDES = (1, 2, 0)
ATTN_LANES = ((0, 1, 2, 3), (1, 2, 3, 0), (2, 0, 1, 3))


def insert(number, bit, value):
    low = number & ((1 << bit) - 1)
    return ((number - low) << 1) | (value << bit) | low


def row_of(ref):
    return ref[...].reshape(1, -1)


def input_rule(tokens, gain, own_middle, own_back, got):
    normed_grad = own_back + got.astype(f32)
    values = tokens.astype(f32)
    factor = row_factor(values)
    scaled = values * factor
    gained = gain * normed_grad
    inner = jnp.mean(scaled * gained, axis=-1, keepdims=True)
    return (own_middle + factor * (gained - scaled * inner)).astype(bf16)


def after(token, values):
    return lax.optimization_barrier((values, token))[0]


def block_rows(index, block):
    return pl.ds(pl.multiple_of(index * block, 16), block)


def swap_bit(values, bit):
    parts = lax.axis_size("dp")
    return lax.ppermute(values, "dp", [(i, i ^ (1 << bit)) for i in range(parts)])


def my_bit(bit):
    return lax.shift_right_logical(lax.axis_index("dp"), bit) & 1


def mm(left, right, left_dim=1, right_dim=0):
    return lax.dot_general(
        left, right, (((left_dim,), (right_dim,)), ((), ())), preferred_element_type=f32
    )


def split_low(values):
    high = values.astype(bf16)
    return high, (values - high.astype(f32)).astype(bf16)


def sigmoid(values):
    return 1.0 / (1.0 + jnp.exp(-values))


def row_factor(values):
    return lax.rsqrt(jnp.mean(values * values, axis=-1, keepdims=True) + EPS)


def picks(index_ref, length):
    rows = lax.broadcasted_iota(jnp.int32, (length, index_ref.shape[1]), 0)
    return jnp.where(rows == index_ref[...], 1.0, 0.0).astype(bf16)


def row_picks(columns_ref, length):
    rows = columns_ref.shape[0]
    cols = lax.broadcasted_iota(jnp.int32, (rows, length), 1)
    return jnp.where(cols == columns_ref[...], 1.0, 0.0).astype(bf16)


def head_masks(width):
    lanes = lax.shift_right_logical(lax.broadcasted_iota(jnp.int32, (1, width), 1), 6)
    return [jnp.where(lanes == head, 1.0, 0.0).astype(f32) for head in range(width // HEAD_DIM)]


def stack_heads(values, masks):
    return jnp.concatenate([values * mask.astype(values.dtype) for mask in masks], axis=0)


def unstack_heads(values, masks):
    rows = values.shape[0] // len(masks)
    total = values[:rows] * masks[0]
    for head in range(1, len(masks)):
        total = total + values[head * rows : (head + 1) * rows] * masks[head]
    return total


def softmax_rows(scores, axis):
    exponent = jnp.exp(scores - jnp.max(scores, axis=axis, keepdims=True))
    return exponent * (1.0 / jnp.sum(exponent, axis=axis, keepdims=True))


def window_start(block, length):
    start = jnp.clip(block * WINDOW - WINDOW, 0, length - 3 * WINDOW)
    return pl.multiple_of(start, WINDOW)


def attn_forward_kernel(
    ready,
    other_ref,
    columns_ref,
    gain_ref,
    route_query_ref,
    route_key_ref,
    query_index_ref,
    ffn_index_ref,
    own_ref,
    cot_ref,
    hq_ref,
    hk_ref,
    hv_ref,
    ho_ref,
    wq_ref,
    wk_ref,
    wv_ref,
    wo_ref,
    partial_ref,
    input_ref,
    q_ref,
    k_ref,
    v_ref,
    result_ref,
    query_rows_ref,
    key_raw_ref,
    key_rows_ref,
    qh_ref,
    kh_ref,
    vh_ref,
    raw_ref,
    heavy_result_ref,
    token_rows_ref,
    swap_rows_ref,
    ffn_pick_ref,
    pick_ref,
):
    ready(5)
    side = lax.axis_index("tensor")
    half = own_ref.shape[0]
    length = 2 * half
    tile = 256
    for ref, place in ((other_ref, 1 - side), (own_ref, side)):
        if ref is own_ref:
            ready(6)
        for start in range(0, half, tile):
            values = ref[start : start + tile, :].astype(f32)
            normed = values * row_factor(values) * row_of(gain_ref)
            rows = pl.ds(pl.multiple_of(place * half + start, tile), tile)
            input_ref[rows, :] = normed.astype(bf16)
    routed = query_index_ref.shape[1]
    pick_ref[...] = picks(query_index_ref, length)
    ffn_pick_ref[...] = picks(ffn_index_ref, length)
    picker = row_picks(columns_ref, length)
    picked = mm(picker[: 2 * routed], input_ref[...])
    own_pick = ffn_pick_ref[pl.ds(pl.multiple_of(side * half, half), half), :]
    other_pick = ffn_pick_ref[pl.ds(pl.multiple_of((1 - side) * half, half), half), :]
    token_rows = mm(own_pick, own_ref[...], 0, 0) + mm(other_pick, other_ref[...], 0, 0)
    token_rows_ref[...] = token_rows.astype(bf16)
    query_rows = picked[:routed]
    key_raw = picked[routed:]
    query_score = sigmoid(jnp.sum(query_rows * row_of(route_query_ref), axis=-1, keepdims=True))
    key_score = sigmoid(jnp.sum(key_raw * row_of(route_key_ref), axis=-1, keepdims=True))
    query_rows_ref[...] = query_rows.astype(bf16)
    key_raw_ref[...] = key_raw.astype(bf16)
    key_rows_ref[...] = (key_score * key_raw).astype(bf16)
    ready(11)
    swap_rows_ref[routed:, :] = mm(own_pick, cot_ref[...], 0, 0).astype(bf16)
    qh_ref[...] = mm(query_rows_ref[...], hq_ref[...]).astype(bf16)
    kh_ref[...] = mm(key_rows_ref[...], hk_ref[...]).astype(bf16)
    vh_ref[...] = mm(key_rows_ref[...], hv_ref[...]).astype(bf16)
    pair = 2 * HEAD_DIM
    pair_masks = head_masks(pair)
    for start in range(0, qh_ref.shape[1], pair):
        cols = slice(start, start + pair)
        stacked = stack_heads(qh_ref[:, cols] * (HEAD_DIM**-0.5), pair_masks)
        probs = softmax_rows(mm(stacked, kh_ref[:, cols], 1, 1), -1)
        raw_ref[:, cols] = unstack_heads(mm(probs.astype(bf16), vh_ref[:, cols]), pair_masks)
    heavy_result_ref[...] = (query_score * raw_ref[...]).astype(bf16)
    high, low = split_low(mm(heavy_result_ref[...], ho_ref[...]))

    ready(15)
    for start in range(0, length, tile):
        rows = slice(start, start + tile)
        q_ref[rows, :] = mm(input_ref[rows, :], wq_ref[...]).astype(bf16)
        k_ref[rows, :] = mm(input_ref[rows, :], wk_ref[...]).astype(bf16)
        v_ref[rows, :] = mm(input_ref[rows, :], wv_ref[...]).astype(bf16)

    masks = head_masks(q_ref.shape[1])
    heads = len(masks)
    gap = lax.broadcasted_iota(jnp.int32, (WINDOW, 3 * WINDOW), 0) - lax.broadcasted_iota(
        jnp.int32, (WINDOW, 3 * WINDOW), 1
    )

    def one_block(block, carry):
        rows = pl.ds(pl.multiple_of(block * WINDOW, WINDOW), WINDOW)
        start = window_start(block, length)
        keys = pl.ds(start, 3 * WINDOW)
        stacked = stack_heads(q_ref[rows, :] * (HEAD_DIM**-0.5), masks)
        scores = mm(stacked, k_ref[keys, :], 1, 1)
        near = jnp.abs(gap + (block * WINDOW - start)) < WINDOW
        bias = jnp.where(near, 0.0, -1e30)
        probs = softmax_rows(scores + jnp.concatenate([bias] * heads, axis=0), -1)
        out = unstack_heads(mm(probs.astype(bf16), v_ref[keys, :]), masks)
        result_ref[rows, :] = out.astype(bf16)
        return carry

    lax.fori_loop(0, length // WINDOW, one_block, 0, unroll=4)
    spread = jnp.concatenate([high, low], axis=0)
    for start in range(0, length, tile):
        rows = slice(start, start + tile)
        pick = jnp.concatenate([pick_ref[rows, :]] * 2, axis=1)
        partial_ref[rows, :] = (mm(result_ref[rows, :], wo_ref[...]) + mm(pick, spread)).astype(bf16)
    swap_rows_ref[:routed, :] = mm(picker[2 * routed :], partial_ref[...]).astype(bf16)


def gelu_parts(values):
    density = jnp.exp(-0.5 * values * values) * 0.3989422804014327
    below = 0.5 * (1.0 + lax.erf(values * 0.7071067811865476))
    return values * below, below + values * density


def ffn_heavy_kernel(
    ready,
    hg_ref,
    hu_ref,
    hd_ref,
    token_rows_ref,
    mine_ref,
    got_ref,
    gain_ref,
    route_ref,
    send_x_ref,
    send_y_ref,
    send_z_ref,
    rows_back_ref,
    route_grad_ref,
):
    routed, model = token_rows_ref.shape
    rows = slice(0, routed)
    middle = token_rows_ref[...].astype(f32) + (
        mine_ref[rows, :].astype(f32) + got_ref[rows, :].astype(f32)
    )
    cot_rows = mine_ref[routed:, :] + got_ref[routed:, :]
    ready(2)
    rows_low = (middle * row_factor(middle) * row_of(gain_ref)).astype(bf16)
    ffn_rows = rows_low.astype(f32)
    send_x_ref[:, :model] = rows_low
    send_y_ref[:, :model] = rows_low
    send_z_ref[:, :model] = cot_rows
    score = sigmoid(jnp.sum(ffn_rows * row_of(route_ref), axis=-1, keepdims=True))
    chunk = 512
    score_grad = 0.0
    for start in range(0, hg_ref.shape[1], chunk):
        cols = slice(start, start + chunk)
        out_cols = slice(model + start, model + start + chunk)
        gate = mm(rows_low, hg_ref[:, cols])
        up = mm(rows_low, hu_ref[:, cols])
        act_grad = mm(cot_rows, hd_ref[cols, :], 1, 1)
        gelu, slope = gelu_parts(gate)
        mixed = gelu * up
        score_grad = score_grad + jnp.sum(act_grad * mixed, axis=-1, keepdims=True)
        scaled = score * act_grad
        send_x_ref[:, out_cols] = (scaled * up * slope).astype(bf16)
        send_y_ref[:, out_cols] = (scaled * gelu).astype(bf16)
        send_z_ref[:, out_cols] = (score * mixed).astype(bf16)
    logit_grad = score * (1.0 - score) * score_grad
    route_grad_ref[...] = jnp.sum(ffn_rows * logit_grad, axis=0, keepdims=True)
    rows_back_ref[...] = logit_grad * row_of(route_ref)


def ffn_light_kernel(
    ready,
    other_ref,
    mine_ref,
    got_ref,
    cot_other_ref,
    pick_ref,
    rows_back_ref,
    gate_grad_ref,
    up_grad_ref,
    act_heavy_ref,
    hg_ref,
    hu_ref,
    hd_ref,
    wg_ref,
    wu_ref,
    wd_ref,
    gain_ref,
    own_ref,
    cot_own_ref,
    back_ref,
    block_own_ref,
    block_send_ref,
    middle_ref,
    *rest,
):
    lane_refs = rest[:-5]
    light_grad_ref, act_ref, mix_ref, input_ref, cot_ref = rest[-5:]
    side = lax.axis_index("tensor")
    half = block_own_ref.shape[0]
    tile = 256
    ready(1)
    for ref, cot, place in ((other_ref, cot_other_ref, 1 - side), (own_ref, cot_own_ref, side)):
        if ref is own_ref:
            ready(3)
        for start in range(0, half, tile):
            rows = pl.ds(pl.multiple_of(place * half + start, tile), tile)
            branch = mine_ref[rows, :].astype(f32) + got_ref[rows, :].astype(f32)
            middle = ref[start : start + tile, :].astype(f32) + branch
            middle_ref[rows, :] = middle
            input_ref[rows, :] = (middle * row_factor(middle) * row_of(gain_ref)).astype(bf16)
            cot_ref[rows, :] = cot[start : start + tile, :]
    model = input_ref.shape[1]
    down_high, down_low = split_low(mm(act_heavy_ref[:, model:], hd_ref[...]))
    down = jnp.concatenate([down_high, down_low], axis=0)
    rows_back = (
        rows_back_ref[...]
        + mm(gate_grad_ref[:, model:], hg_ref[...], 1, 1)
        + mm(up_grad_ref[:, model:], hu_ref[...], 1, 1)
    )
    rows_back = jnp.concatenate(split_low(rows_back), axis=0)
    width = wg_ref.shape[1]
    for first in range(0, 2):
        place = side if first == 0 else 1 - side
        for start in range(0, half, tile):
            rows = pl.ds(pl.multiple_of(place * half + start, tile), tile)
            piece = slice(start, start + tile)
            gate = mm(input_ref[rows, :], wg_ref[...])
            up = mm(input_ref[rows, :], wu_ref[...])
            act_grad = mm(cot_ref[rows, :], wd_ref[...], 1, 1)
            gelu, slope = gelu_parts(gate)
            act_ref[rows, :] = (gelu * up).astype(bf16)
            mix_ref[rows, :width] = (act_grad * up * slope).astype(bf16)
            mix_ref[rows, width:] = (act_grad * gelu).astype(bf16)
            pick = jnp.concatenate([pick_ref[rows, :]] * 2, axis=1)
            branch = mm(act_ref[rows, :], wd_ref[...]) + mm(pick, down)
            if first == 0:
                block_own_ref[piece, :] = middle_ref[rows, :] + branch
            else:
                block_send_ref[piece, :] = branch.astype(bf16)
            back_ref[rows, :] = (
                mm(mix_ref[rows, :width], wg_ref[...], 1, 1)
                + mm(mix_ref[rows, width:], wu_ref[...], 1, 1)
                + mm(pick, rows_back)
            ).astype(bf16)
    light_grad_ref[:, : 2 * width] = mm(input_ref[...], mix_ref[...], 0, 0).astype(bf16)
    light_grad_ref[:, 2 * width :] = mm(cot_ref[...], act_ref[...], 0, 0).astype(bf16)
    for lane in range(len(lane_refs) // 2):
        lane_split(lane, lane_refs, 0, light_grad_ref, lane * width, (lane + 1) * width)


def lane_split(lane, lane_refs, left, grad_ref, first, last):
    bit = LANES[lane][0]
    mine = my_bit(bit)
    block = grad_ref.shape[0] // PARTS
    keep_ref, send_ref = lane_refs[lane], lane_refs[len(lane_refs) // 2 + lane]
    for p in range(PARTS // 2):
        rows = slice(p * block, (p + 1) * block)
        cols = slice(left, left + last - first)
        for ref, value in ((keep_ref, mine), (send_ref, 1 - mine)):
            ref[rows, cols] = grad_ref[block_rows(insert(p, bit, value), block), first:last]


def attn_backward_kernel(
    ready,
    cot_other_ref,
    middle_ref,
    mine_ref,
    got_ref,
    result_ref,
    query_rows_ref,
    key_raw_ref,
    key_rows_ref,
    qh_ref,
    kh_ref,
    vh_ref,
    raw_ref,
    heavy_result_ref,
    gain_ffn_ref,
    route_query_ref,
    route_key_ref,
    query_index_ref,
    key_index_ref,
    cot_own_ref,
    wo_ref,
    ho_ref,
    hq_ref,
    hk_ref,
    hv_ref,
    own_middle_ref,
    out_ref,
    grad_ref,
    back_high_ref,
    back_low_ref,
    pick_ref,
    small_ref,
    low_ref,
):
    ready(5)
    side = lax.axis_index("tensor")
    half = cot_own_ref.shape[0]
    length = 2 * half
    tile = 256
    scale = HEAD_DIM**-0.5
    heavy = qh_ref.shape[1]
    light = result_ref.shape[1]
    gain_ffn_grad = 0.0
    for cot, place, owned in ((cot_other_ref, 1 - side, False), (cot_own_ref, side, True)):
        if owned:
            ready(6)
        for start in range(0, half, tile):
            rows = pl.ds(pl.multiple_of(place * half + start, tile), tile)
            piece = slice(start, start + tile)
            normed_grad = mine_ref[rows, :].astype(f32) + got_ref[rows, :].astype(f32)
            middle = middle_ref[rows, :]
            factor = row_factor(middle)
            scaled = factor * middle
            gain_ffn_grad = gain_ffn_grad + jnp.sum(scaled * normed_grad, axis=0, keepdims=True)
            gained = row_of(gain_ffn_ref) * normed_grad
            inner = jnp.mean(scaled * gained, axis=-1, keepdims=True)
            grad = cot[piece, :].astype(f32) + factor * (gained - scaled * inner)
            if owned:
                own_middle_ref[piece, :] = grad
            low_ref[rows, :] = grad.astype(bf16)
    ready(11)
    for start in range(0, length, tile):
        rows = slice(start, start + tile)
        out_ref[rows, :] = mm(low_ref[rows, :], wo_ref[...], 1, 1).astype(bf16)
    grad_ref[:, 4 * heavy :] = mm(low_ref[...], result_ref[...], 0, 0).astype(bf16)

    routed = query_index_ref.shape[1]
    pick_ref[:, :routed] = picks(query_index_ref, length)
    pick_ref[:, routed:] = picks(key_index_ref, length)
    query_rows = query_rows_ref[...].astype(f32)
    key_raw = key_raw_ref[...].astype(f32)
    query_score = sigmoid(jnp.sum(query_rows * row_of(route_query_ref), axis=-1, keepdims=True))
    key_score = sigmoid(jnp.sum(key_raw * row_of(route_key_ref), axis=-1, keepdims=True))
    mid_rows = mm(pick_ref[:, :routed], low_ref[...], 0, 0).astype(bf16)
    grad_ref[:, 3 * heavy : 4 * heavy] = mm(mid_rows, heavy_result_ref[...], 0, 0).astype(bf16)
    heavy_out_grad = mm(mid_rows, ho_ref[...], 1, 1).astype(bf16)
    query_score_grad = jnp.sum(
        heavy_out_grad.astype(f32) * raw_ref[...], axis=-1, keepdims=True
    )
    raw_high, raw_low = split_low(query_score * heavy_out_grad.astype(f32))
    pair = 2 * HEAD_DIM
    pair_masks = head_masks(pair)
    stacked_score = jnp.concatenate([query_score] * 2, axis=0)
    q_parts, k_parts, v_parts = [], [], []
    for start in range(0, heavy, pair):
        cols = slice(start, start + pair)
        stacked = stack_heads(qh_ref[:, cols] * scale, pair_masks)
        probs = softmax_rows(mm(stacked, kh_ref[:, cols], 1, 1), -1)
        grad_stacked = stack_heads(heavy_out_grad[:, cols], pair_masks)
        probs_grad = stacked_score * mm(grad_stacked, vh_ref[:, cols], 1, 1)
        inner = jnp.sum(probs * probs_grad, axis=-1, keepdims=True)
        score_grad = (probs * (probs_grad - inner)).astype(bf16)
        probs_low = probs.astype(bf16)
        q_parts.append(unstack_heads(mm(score_grad, kh_ref[:, cols]) * scale, pair_masks))
        k_parts.append(mm(score_grad, stacked, 0, 0))
        v_parts.append(
            mm(probs_low, stack_heads(raw_high[:, cols], pair_masks), 0, 0)
            + mm(probs_low, stack_heads(raw_low[:, cols], pair_masks), 0, 0)
        )
    query_heavy_grad = jnp.concatenate(q_parts, axis=1).astype(bf16)
    key_heavy_grad = jnp.concatenate(k_parts, axis=1).astype(bf16)
    value_heavy_grad = jnp.concatenate(v_parts, axis=1).astype(bf16)
    grad_ref[:, :heavy] = mm(query_rows_ref[...], query_heavy_grad, 0, 0).astype(bf16)
    grad_ref[:, heavy : 2 * heavy] = mm(key_rows_ref[...], key_heavy_grad, 0, 0).astype(bf16)
    grad_ref[:, 2 * heavy : 3 * heavy] = mm(
        key_rows_ref[...], value_heavy_grad, 0, 0
    ).astype(bf16)
    key_rows_grad = mm(key_heavy_grad, hk_ref[...], 1, 1) + mm(
        value_heavy_grad, hv_ref[...], 1, 1
    )
    key_logit_grad = (
        key_score * (1.0 - key_score) * jnp.sum(key_rows_grad * key_raw, axis=-1, keepdims=True)
    )
    query_logit_grad = query_score * (1.0 - query_score) * query_score_grad
    key_raw_grad = key_score * key_rows_grad + key_logit_grad * row_of(route_key_ref)
    query_rows_grad = mm(query_heavy_grad, hq_ref[...], 1, 1)
    query_rows_grad = query_rows_grad + query_logit_grad * row_of(route_query_ref)
    small_ref[...] = jnp.zeros_like(small_ref)
    small_ref[1:2, :] = 0.5 * gain_ffn_grad
    small_ref[2:3, :] = jnp.sum(query_rows * query_logit_grad, axis=0, keepdims=True)
    small_ref[3:4, :] = jnp.sum(key_raw * key_logit_grad, axis=0, keepdims=True)
    high, low = split_low(jnp.concatenate([query_rows_grad, key_raw_grad], axis=0))
    back_high_ref[...] = high
    back_low_ref[...] = low


def lane_cuts(heavy, light):
    return (
        (0, 2 * heavy, 0, light),
        (2 * heavy, 4 * heavy, 0, 0),
        (4 * heavy, 4 * heavy + light, light, 3 * light),
    )


def light_backward_kernel(
    ready,
    other_ref,
    input_ref,
    q_ref,
    k_ref,
    v_ref,
    out_ref,
    heavy_grad_ref,
    back_high_ref,
    back_low_ref,
    pick_ref,
    own_ref,
    wq_ref,
    wk_ref,
    wv_ref,
    own_back_ref,
    send_ref,
    small_ref,
    *rest,
):
    grad_refs = rest[:-6]
    light_grad_ref, kt_ref, qt_grad_ref, k_grad_ref, v_grad_ref, mixed_ref = rest[-6:]
    side = lax.axis_index("tensor")
    half = own_ref.shape[0]
    length = 2 * half
    tile = 256
    scale = HEAD_DIM**-0.5
    kt_ref[...] = k_ref[...].T
    k_grad_ref[...] = jnp.zeros_like(k_grad_ref)
    v_grad_ref[...] = jnp.zeros_like(v_grad_ref)
    masks = head_masks(q_ref.shape[1])
    heads = len(masks)
    gap = lax.broadcasted_iota(jnp.int32, (3 * WINDOW, WINDOW), 1) - lax.broadcasted_iota(
        jnp.int32, (3 * WINDOW, WINDOW), 0
    )

    def one_block(block, carry):
        first = pl.multiple_of(block * WINDOW, WINDOW)
        rows = pl.ds(first, WINDOW)
        start = window_start(block, length)
        keys = pl.ds(start, 3 * WINDOW)
        stacked = stack_heads(q_ref[rows, :] * scale, masks)
        grad_stacked = stack_heads(out_ref[rows, :], masks)
        near = jnp.abs(gap + (block * WINDOW - start)) < WINDOW
        bias = jnp.where(near, 0.0, -1e30)
        scores = mm(k_ref[keys, :], stacked, 1, 1)
        probs = softmax_rows(scores + jnp.concatenate([bias] * heads, axis=1), 0)
        probs_grad = mm(v_ref[keys, :], grad_stacked, 1, 1)
        inner = jnp.sum(probs * probs_grad, axis=0, keepdims=True)
        score_grad = (probs * (probs_grad - inner)).astype(bf16)
        k_grad_ref[keys, :] += mm(score_grad, stacked)
        v_grad_ref[keys, :] += mm(probs.astype(bf16), grad_stacked)
        spread = mm(kt_ref[:, keys], score_grad) * scale
        for head in range(heads):
            lanes = slice(head * HEAD_DIM, (head + 1) * HEAD_DIM)
            qt_grad_ref[lanes, rows] = spread[lanes, head * WINDOW : (head + 1) * WINDOW]
        return carry

    lax.fori_loop(0, length // WINDOW, one_block, 0, unroll=True)
    light = q_ref.shape[1]
    mixed_ref[:, :light] = qt_grad_ref[...].T.astype(bf16)
    mixed_ref[:, light : 2 * light] = k_grad_ref[...].astype(bf16)
    mixed_ref[:, 2 * light :] = v_grad_ref[...].astype(bf16)
    heavy_cols = heavy_grad_ref.shape[1]
    heavy = (heavy_cols - light) // 4
    light_grad = mm(input_ref[...], mixed_ref[...], 0, 0).astype(bf16)
    ready(4)
    gain_attn_grad = 0.0
    for ref, place, owned in ((own_ref, side, True), (other_ref, 1 - side, False)):
        for start in range(0, half, tile):
            rows = pl.ds(pl.multiple_of(place * half + start, tile), tile)
            piece = slice(start, start + tile)
            pick = pick_ref[rows, :]
            back = (
                mm(mixed_ref[rows, :light], wq_ref[...], 1, 1)
                + mm(mixed_ref[rows, light : 2 * light], wk_ref[...], 1, 1)
                + mm(mixed_ref[rows, 2 * light :], wv_ref[...], 1, 1)
                + (mm(pick, back_high_ref[...]) + mm(pick, back_low_ref[...]))
            )
            values = ref[piece, :].astype(f32)
            gain_attn_grad = gain_attn_grad + jnp.sum(
                values * row_factor(values) * back, axis=0, keepdims=True
            )
            if owned:
                own_back_ref[piece, :] = back
            else:
                send_ref[piece, :] = back.astype(bf16)
    small_ref[...] = gain_attn_grad
    if len(grad_refs) == 1:
        grad_refs[0][:, :heavy_cols] = heavy_grad_ref[...]
        grad_refs[0][:, heavy_cols:] = light_grad
        return
    light_grad_ref[...] = light_grad
    for lane, (left, right, first, last) in enumerate(lane_cuts(heavy, light)):
        if right > left:
            lane_split(lane, grad_refs, 0, heavy_grad_ref, left, right)
        if last > first:
            lane_split(lane, grad_refs, right - left, light_grad_ref, first, last)


def join_kernel(lane, send_ref, got_ref, light_ref, next_keep_ref, next_send_ref, full_ref):
    model, heavy = full_ref.shape
    tall = next_send_ref.shape[0]
    light = light_ref.shape[1]
    for wrap in range(light_ref.shape[0] // tall):
        cols = slice(heavy + wrap * light, heavy + (wrap + 1) * light)
        next_send_ref[:, cols] = light_ref[wrap * tall : (wrap + 1) * tall, :]
    left = jnp.concatenate([send_ref[:, :model], got_ref[:, :model]], axis=0)
    right = jnp.concatenate([send_ref[:, model:], got_ref[:, model:]], axis=0)
    full_ref[...] = mm(left, right, 0, 0).astype(bf16)
    first, second = LANES[lane][:2]
    position = second - (1 if first < second else 0)
    mine, next_mine = my_bit(first), my_bit(second)
    block = model // PARTS
    for q in range(PARTS // 4):
        rows = slice(q * block, (q + 1) * block)
        for ref, value in ((next_keep_ref, next_mine), (next_send_ref, 1 - next_mine)):
            p = insert(q, position, value)
            ref[rows, :heavy] = full_ref[block_rows(insert(p, first, mine), block), :]


def pack_small(values, send_ref, left):
    high, low = split_low(values)
    both = jnp.concatenate([high.astype(f32), low.astype(f32)], axis=0).astype(bf16)
    wide = send_ref.shape[1] - left
    for i in range(both.shape[1] // wide):
        send_ref[16 * i : 16 * (i + 1), left:] = both[:, wide * i : wide * (i + 1)]


def unpack_small(got_ref, left, width):
    wide = got_ref.shape[1] - left
    both = jnp.concatenate(
        [got_ref[16 * i : 16 * (i + 1), left:] for i in range(width // wide)], axis=1
    ).astype(f32)
    return both[:8] + both[8:]


def fold_kernel(bit, position, block, pairs, *refs):
    next_keep_ref, next_send_ref = refs[2 * pairs :][-3:-1]
    sum_ref = refs[-1]
    extra = refs[2 * pairs : -3]
    left = 0
    for keep_ref, got_ref in zip(refs[: 2 * pairs : 2], refs[1 : 2 * pairs : 2]):
        rows, width = keep_ref.shape
        tall = min(rows, got_ref.shape[0])
        skip = got_ref.shape[1] - width * (rows // tall) if tall < rows else 0
        for wrap in range(rows // tall):
            piece = slice(wrap * tall, (wrap + 1) * tall)
            got = got_ref[:, skip + wrap * width : skip + (wrap + 1) * width]
            both = keep_ref[piece, :].astype(f32) + got.astype(f32)
            sum_ref[piece, left : left + width] = both.astype(bf16)
        left += width
    mine = my_bit(bit)
    for q in range(next_keep_ref.shape[0] // block):
        rows = slice(q * block, (q + 1) * block)
        next_keep_ref[rows, :] = sum_ref[block_rows(insert(q, position, mine), block), :]
        next_send_ref[rows, :left] = sum_ref[block_rows(insert(q, position, 1 - mine), block), :]
    if extra:
        *parts, small_ref = extra
        small = parts[0][...]
        if len(parts) == 2 and parts[1].dtype == f32:
            small = small + parts[1][...]
        elif len(parts) == 2:
            small = small + unpack_small(parts[1], parts[1].shape[1] - 128, small.shape[1])
        else:
            small = small + unpack_small(refs[1], refs[0].shape[1], small.shape[1])
        small_ref[...] = small
        pack_small(small, next_send_ref, left)


def last_fold_kernel(bit, lanes, *refs):
    extra = refs[2 * lanes : -3]
    keep_ref, send_ref, sum_ref = refs[-3:]
    left = 0
    for lane in range(lanes):
        width = refs[lane].shape[1]
        both = refs[lane][...].astype(f32) + refs[lanes + lane][:, :width].astype(f32)
        sum_ref[:, left : left + width] = both
        left += width
    mine = my_bit(bit)
    block = keep_ref.shape[0]
    keep_ref[...] = sum_ref[block_rows(mine, block), :]
    send_ref[:, :left] = sum_ref[block_rows(1 - mine, block), :].astype(bf16)
    if extra:
        small = extra[0][...]
        small = small + unpack_small(refs[lanes], refs[0].shape[1], small.shape[1])
        extra[1][...] = small
        pack_small(small, send_ref, left)


def final_kernel(widths, keep_ref, got_ref, *refs):
    left = 0
    outs = refs
    if len(refs) > len(widths):
        small_ref, *outs = refs
        total = keep_ref.shape[1]
        small = small_ref[...] + unpack_small(got_ref, total, small_ref.shape[1])
        for i, out_ref in enumerate(outs[len(widths) :]):
            out_ref[...] = small[i]
    for width, out_ref in zip(widths, outs):
        cols = slice(left, left + width)
        out_ref[...] = keep_ref[:, cols] + got_ref[:, cols].astype(f32)
        left += width


def fold(bit, position, block, *pairs, extra=()):
    rows = pairs[0].shape[0]
    width = sum(pair.shape[1] for pair in pairs[::2])
    ride = 128 if extra else 0
    return whole(
        functools.partial(fold_ride if extra else fold_kernel, bit, position, block, len(pairs) // 2),
        "fold",
        2,
        [((rows // 2, width), bf16), ((rows // 2, width + ride), bf16)]
        + [(item.shape, f32) for item in extra[:1]],
        [((rows, width), bf16)],
        *pairs,
        *extra,
    )


def fold_ride(bit, position, block, pairs, *refs):
    keep_ref, send_ref, small_ref, sum_ref = refs[-4:]
    fold_kernel(bit, position, block, pairs, *refs[:-4], small_ref, keep_ref, send_ref, sum_ref)


def last_fold(bit, keeps, gots, extra=()):
    rows = keeps[0].shape[0]
    width = sum(keep.shape[1] for keep in keeps)
    ride = 256 if extra else 0
    return whole(
        functools.partial(last_ride if extra else last_fold_kernel, bit, len(keeps)),
        "last_fold",
        2,
        [((rows // 2, width), f32), ((rows // 2, width + ride), bf16)]
        + [(item.shape, f32) for item in extra[:1]],
        [((rows, width), f32)],
        *keeps,
        *gots,
        *extra,
    )


def last_ride(bit, lanes, *refs):
    keep_ref, send_ref, small_ref, sum_ref = refs[-4:]
    last_fold_kernel(bit, lanes, *refs[:-4], small_ref, keep_ref, send_ref, sum_ref)


def final(widths, keep, got, extra=()):
    return whole(
        functools.partial(final_kernel, widths),
        "final",
        2,
        [((keep.shape[0], width), f32, 0) for width in widths]
        + [((item.shape[1],), f32, 0) for item in extra for _ in range(5)],
        [],
        keep,
        got,
        *extra,
    )


def whole(kernel, name, micros, outs, scratch, *operands, outside=0):
    inside = len(operands) - outside
    spaces = [pltpu.VMEM] * inside + [pltpu.HBM] * outside
    operands = [
        pltpu.with_memory_space_constraint(item, space) for item, space in zip(operands, spaces)
    ]
    shapes = [
        pltpu.VMEM(*out) if len(out) == 2 else jax.ShapeDtypeStruct(*out[:2]) for out in outs
    ]
    stage = [pltpu.VMEM(item.shape, item.dtype) for item in operands[inside:]]
    if outside:
        stage.append(pltpu.SemaphoreType.DMA((outside,)))

    def staged(*refs):
        if not outside:
            return kernel(*refs)
        sources, kept, sems = refs[inside : inside + outside], refs[-1 - outside : -1], refs[-1]
        copies = [
            pltpu.make_async_copy(source, target, sems.at[i])
            for i, (source, target) in enumerate(zip(sources, kept))
        ]
        for copy in copies:
            copy.start()
        waited = [False] * outside

        def ready(count):
            for i in range(count):
                if not waited[i]:
                    copies[i].wait()
                    waited[i] = True

        kernel(ready, *refs[:inside], *kept, *refs[inside + outside : -1 - outside])

    return pl.pallas_call(
        staged,
        name=name,
        out_shape=shapes,
        in_specs=[pl.BlockSpec(memory_space=space) for space in spaces],
        out_specs=[pl.BlockSpec(memory_space=pltpu.VMEM)] * len(outs),
        scratch_shapes=[pltpu.VMEM(shape, dtype) for shape, dtype in scratch] + stage,
        compiler_params=pltpu.CompilerParams(vmem_limit_bytes=VMEM_LIMIT),
        cost_estimate=pl.CostEstimate(
            flops=micros * 10**9, transcendentals=0, bytes_accessed=micros * 10**6
        ),
    )(*operands)


def body(
    tokens,
    cotangent,
    gain_attn,
    gain_ffn,
    route_query,
    route_key,
    route_ffn,
    light_query,
    light_key,
    light_value,
    light_out,
    heavy_query,
    heavy_key,
    heavy_value,
    heavy_out,
    light_gate,
    light_up,
    light_down,
    heavy_gate,
    heavy_up,
    heavy_down,
    query_index,
    key_index,
    ffn_index,
):
    half, width = tokens.shape
    length = 2 * half
    routed = query_index.shape[1]
    light = light_query.shape[1]
    heavy = heavy_query.shape[1]
    light_ff = light_gate.shape[1]
    heavy_ff = heavy_gate.shape[1]
    other_tokens = pair_swap(tokens)
    attn_weights = (
        heavy_query,
        heavy_key,
        heavy_value,
        heavy_out,
        light_query,
        light_key,
        light_value,
        light_out,
    )
    columns = jnp.concatenate([query_index, key_index, ffn_index], axis=1).reshape(-1, 1)
    attn_partial, *saved, token_rows, swap_rows, ffn_pick = whole(
        attn_forward_kernel,
        "attn_forward",
        16,
        [((length, width), bf16)] * 2
        + [((length, light), bf16)] * 4
        + [((routed, width), bf16)] * 3
        + [((routed, heavy), bf16)] * 3
        + [((routed, heavy), f32), ((routed, heavy), bf16)]
        + [((routed, width), bf16), ((2 * routed, width), bf16), ((length, routed), bf16)],
        [((length, routed), bf16)],
        other_tokens,
        columns,
        gain_attn,
        route_query,
        route_key,
        query_index,
        ffn_index,
        tokens,
        cotangent,
        *attn_weights,
        outside=7 + len(attn_weights),
    )
    got_rows = pair_swap(swap_rows)
    other_cotangent = pair_swap(after(got_rows, cotangent))
    partial_got = pair_swap(after(got_rows, attn_partial))
    tuned = lax.axis_size("dp") == PARTS
    *sends, rows_back, route_ffn_grad = whole(
        ffn_heavy_kernel,
        "ffn_heavy",
        12,
        [((routed, width + heavy_ff), bf16)] * 3 + [((routed, width), f32), ((1, width), f32)],
        [],
        heavy_gate,
        heavy_up,
        heavy_down,
        token_rows,
        swap_rows,
        got_rows,
        gain_ffn,
        route_ffn,
        outside=2,
    )
    if tuned:
        gots = [swap_bit(send, order[0]) for send, order in zip(sends, LANES)]
    ffn_back, block_own, block_send, middle, *light_parts = whole(
        ffn_light_kernel,
        "ffn_light",
        12,
        [
            ((length, width), bf16),
            ((half, width), f32),
            ((half, width), bf16),
            ((length, width), f32),
        ]
        + ([((width // 2, light_ff), bf16)] * 6 if tuned else [((width, 3 * light_ff), bf16)]),
        ([((width, 3 * light_ff), bf16)] if tuned else [])
        + [
            ((length, light_ff), bf16),
            ((length, 2 * light_ff), bf16),
            ((length, width), bf16),
            ((length, width), bf16),
        ],
        other_tokens,
        attn_partial,
        partial_got,
        other_cotangent,
        ffn_pick,
        rows_back,
        *sends,
        heavy_gate,
        heavy_up,
        heavy_down,
        light_gate,
        light_up,
        light_down,
        gain_ffn,
        tokens,
        cotangent,
        outside=3,
    )
    if tuned:
        back_got = pair_swap(after(tuple(gots), ffn_back))
        light_keeps = light_parts[:3]
        light_sends = light_parts[3:]
        token = ffn_back
        ffn_keeps, ffn_sends = [], []
        for lane in range(3):
            keep, send = whole(
                functools.partial(join_kernel, lane),
                "join",
                3,
                [((width // 4, heavy_ff), bf16), ((width // 4, heavy_ff + 2 * light_ff), bf16)],
                [((width, heavy_ff), bf16)],
                after(token, sends[lane]),
                gots[lane],
                light_sends[RIDES[lane]],
            )
            token = keep
            ffn_keeps.append(keep)
            ffn_sends.append(send)
        ffn_gots = [swap_bit(send, order[1]) for send, order in zip(ffn_sends, LANES)]
        ffn_back = after(token, ffn_back)
    else:
        back_got = pair_swap(ffn_back)
    attn_input, q_light, k_light, v_light, *routed_saved = saved
    own_middle, out_back, heavy_grad, back_high, back_low, pick, small = whole(
        attn_backward_kernel,
        "attn_backward",
        10,
        [
            ((half, width), f32),
            ((length, light), bf16),
            ((width, 4 * heavy + light), bf16),
            ((2 * routed, width), bf16),
            ((2 * routed, width), bf16),
            ((length, 2 * routed), bf16),
            ((8, width), f32),
        ],
        [((length, width), bf16)],
        other_cotangent,
        middle,
        ffn_back,
        back_got,
        *routed_saved,
        gain_ffn,
        route_query,
        route_key,
        query_index,
        key_index,
        cotangent,
        light_out,
        heavy_out,
        heavy_query,
        heavy_key,
        heavy_value,
        outside=11,
    )
    block = width // lax.axis_size("dp")
    own_back, back_send, gain_attn_grad, *attn_grads = whole(
        light_backward_kernel,
        "light_backward",
        16,
        [((half, width), f32), ((half, width), bf16), ((1, width), f32)]
        + (
            [
                ((width // 2, right - left + last - first), bf16)
                for left, right, first, last in lane_cuts(heavy, light)
            ]
            * 2
            if tuned
            else [((width, 4 * heavy + 4 * light), bf16)]
        ),
        [
            ((width, 3 * light), bf16),
            ((light, length), bf16),
            ((light, length), f32),
            ((length, light), f32),
            ((length, light), f32),
            ((length, 3 * light), bf16),
        ],
        other_tokens,
        attn_input,
        q_light,
        k_light,
        v_light,
        out_back,
        heavy_grad,
        back_high,
        back_low,
        pick,
        tokens,
        light_query,
        light_key,
        light_value,
        outside=4,
    )
    small = small + jnp.pad(route_ffn_grad, ((4, 3), (0, 0)))
    small = small + jnp.pad(gain_attn_grad, ((0, 7), (0, 0)))
    if tuned:
        attn_keeps = attn_grads[:3]

        def middle_stage(orders, stage, token, pairs, extra, rider_lane):
            next_keeps, next_gots = [], []
            for lane, order in enumerate(orders):
                left = sorted(order[stage:])
                keep, send, *small = fold(
                    order[stage],
                    left.index(order[stage]),
                    block,
                    after(token, pairs[lane][0]),
                    *pairs[lane][1:],
                    extra=extra if lane == rider_lane else (),
                )
                if lane == rider_lane:
                    rider = small
                token = keep
                next_keeps.append(keep)
                next_gots.append(swap_bit(send, order[stage]))
            return token, next_keeps, next_gots, rider

        token, ffn_keeps, ffn_gots_next, rider = middle_stage(
            LANES, 2, gain_attn_grad, list(zip(ffn_keeps, ffn_gots)), (small, pair_swap(small)), 1
        )
        block_got = pair_swap(after(token, block_send))
        block_out = (block_own + block_got.astype(f32)).astype(bf16)
        back_got = pair_swap(after(token, back_send))
        input_grad = input_rule(tokens, gain_attn, own_middle, own_back, back_got)
        attn_gots = [
            swap_bit(after((*ffn_gots_next, block_out, input_grad), send), ATTN_LANES[lane][0])
            for lane, send in enumerate(attn_grads[3:])
        ]
        ffn_keep, ffn_send = last_fold(3, [after(token, ffn_keeps[0]), *ffn_keeps[1:]], ffn_gots_next)
        ffn_got = swap_bit(ffn_send, 3)
        token, attn_keeps, attn_gots, rider = middle_stage(
            ATTN_LANES,
            1,
            ffn_keep,
            [
                (attn_keeps[lane], attn_gots[lane], light_keeps[lane], got)
                for lane, got in enumerate(ffn_gots[RIDES.index(i)] for i in range(3))
            ],
            (*rider, ffn_gots_next[1]),
            0,
        )
        hg, hu, hd = final([heavy_ff] * 3, after(token, ffn_keep), ffn_got)
        token, attn_keeps, attn_gots, rider = middle_stage(
            ATTN_LANES, 2, hg, list(zip(attn_keeps, attn_gots)), tuple(rider), 0
        )
        attn_keep, attn_send, rider = last_fold(
            3, [after(token, attn_keeps[0]), attn_keeps[2]], attn_gots[::2], extra=tuple(rider)
        )
        attn_got = swap_bit(attn_send, 3)
        side_keep, side_send = last_fold(0, [after(attn_keep, attn_keeps[1])], attn_gots[1:2])
        side_got = swap_bit(side_send, 0)
        hv, ho, lu = final([heavy, heavy, light_ff], side_keep, side_got)
        widths = [heavy, heavy, light, light_ff, light, light, light, light_ff]
        pieces = final(widths, after(hv, attn_keep), attn_got, extra=(rider,))
        hq, hk, lq, lg, lo, lk, lv, ld, *small_summed = pieces
    else:
        small_summed = butterfly_sum(small)
        block_out = (block_own + pair_swap(block_send).astype(f32)).astype(bf16)
        input_grad = input_rule(tokens, gain_attn, own_middle, own_back, pair_swap(back_send))
    if not tuned:
        order = list(range(lax.axis_size("dp").bit_length() - 1))
        hg, hu, hd = (
            halving_sum(mm(send[:, :width], send[:, width:], 0, 0).astype(bf16), order)
            for send in sends
        )
        lg, lu, ld = jnp.split(halving_sum(light_parts[0], order), 3, axis=1)
        attn_sum = halving_sum(attn_grads[0], order)
        cuts = [heavy, 2 * heavy, 3 * heavy, 4 * heavy, 4 * heavy + light]
        cuts += [4 * heavy + 2 * light, 4 * heavy + 3 * light]
        hq, hk, hv, ho, lo, lq, lk, lv = jnp.split(attn_sum, cuts, axis=1)
    return (
        block_out,
        input_grad,
        small_summed[0],
        small_summed[1],
        small_summed[2],
        small_summed[3],
        small_summed[4],
        lq,
        lk,
        lv,
        lo.T,
        hq,
        hk,
        hv,
        ho.T,
        lg,
        lu,
        ld.T,
        hg,
        hu,
        hd.T,
    )


def solution(mesh):
    in_specs = (
        P(("dp", "tensor"), None),
        P(("dp", "tensor"), None),
        P(),
        P(),
        P(),
        P(),
        P(),
        P(None, "tensor"),
        P(None, "tensor"),
        P(None, "tensor"),
        P("tensor", None),
        P(None, "tensor"),
        P(None, "tensor"),
        P(None, "tensor"),
        P("tensor", None),
        P(None, "tensor"),
        P(None, "tensor"),
        P("tensor", None),
        P(None, "tensor"),
        P(None, "tensor"),
        P("tensor", None),
        P("dp", None),
        P("dp", None),
        P("dp", None),
    )
    out_specs = (
        P(("dp", "tensor"), None),
        P(("dp", "tensor"), None),
        P(),
        P(),
        P(),
        P(),
        P(),
        P("dp", "tensor"),
        P("dp", "tensor"),
        P("dp", "tensor"),
        P("tensor", "dp"),
        P("dp", "tensor"),
        P("dp", "tensor"),
        P("dp", "tensor"),
        P("tensor", "dp"),
        P("dp", "tensor"),
        P("dp", "tensor"),
        P("tensor", "dp"),
        P("dp", "tensor"),
        P("dp", "tensor"),
        P("tensor", "dp"),
    )
    return jax.shard_map(body, mesh=mesh, in_specs=in_specs, out_specs=out_specs, check_vma=False)
```

```python
import functools

import jax
import jax.numpy as jnp
from jax import lax
from jax.experimental import pallas as pl
from jax.experimental.pallas import tpu as pltpu
from jax.sharding import PartitionSpec as P

HEAD_DIM = 64
WINDOW = 128
EPS = 1e-06
VMEM_LIMIT = 20 * 1024 * 1024
f32 = jnp.float32
bf16 = jnp.bfloat16


def pair_swap(values):
    return lax.ppermute(values, "tensor", [(0, 1), (1, 0)])


def halving_sum(values, order):
    parts = lax.axis_size("dp")
    place = lax.axis_index("dp")
    bits = list(range(len(order) - 1, -1, -1))
    held = values.reshape((2,) * len(bits) + (values.shape[0] // parts, values.shape[1]))
    held = held.astype(jnp.bfloat16)
    for step, bit in enumerate(order):
        axis = bits.index(bit)
        bits.remove(bit)
        mine = (place >> bit) & 1
        keep = lax.dynamic_index_in_dim(held, mine, axis, keepdims=False)
        send = lax.dynamic_index_in_dim(held, 1 - mine, axis, keepdims=False)
        got = lax.ppermute(send, "dp", [(i, i ^ (1 << bit)) for i in range(parts)])
        held = keep.astype(jnp.float32) + got.astype(jnp.float32)
        if step < len(order) - 1:
            held = held.astype(jnp.bfloat16)
    return held


def butterfly_sum(values):
    parts = lax.axis_size("dp")
    values = values + pair_swap(values)
    for bit in range(parts.bit_length() - 1):
        values = values + lax.ppermute(values, "dp", [(i, i ^ (1 << bit)) for i in range(parts)])
    return values


PARTS = 16
LANES = ((0, 1, 2, 3), (1, 2, 0, 3), (2, 0, 1, 3))
RIDES = (1, 2, 0)
ATTN_LANES = ((0, 1, 2, 3), (1, 0, 3, 2), (2, 0, 1, 3))


def insert(number, bit, value):
    low = number & ((1 << bit) - 1)
    return ((number - low) << 1) | (value << bit) | low


def row_of(ref):
    return ref[...].reshape(1, -1)


def input_rule(tokens, gain, own_middle, own_back, got):
    normed_grad = own_back + got.astype(f32)
    values = tokens.astype(f32)
    factor = row_factor(values)
    scaled = values * factor
    gained = gain * normed_grad
    inner = jnp.mean(scaled * gained, axis=-1, keepdims=True)
    return (own_middle + factor * (gained - scaled * inner)).astype(bf16)


def after(token, values):
    return lax.optimization_barrier((values, token))[0]


def block_rows(index, block):
    return pl.ds(pl.multiple_of(index * block, 16), block)


def swap_bit(values, bit):
    parts = lax.axis_size("dp")
    return lax.ppermute(values, "dp", [(i, i ^ (1 << bit)) for i in range(parts)])


def my_bit(bit):
    return lax.shift_right_logical(lax.axis_index("dp"), bit) & 1


def mm(left, right, left_dim=1, right_dim=0):
    return lax.dot_general(
        left, right, (((left_dim,), (right_dim,)), ((), ())), preferred_element_type=f32
    )


def split_low(values):
    high = values.astype(bf16)
    return high, (values - high.astype(f32)).astype(bf16)


def sigmoid(values):
    return 1.0 / (1.0 + jnp.exp(-values))


def row_factor(values):
    return lax.rsqrt(jnp.mean(values * values, axis=-1, keepdims=True) + EPS)


def picks(index_ref, length):
    rows = lax.broadcasted_iota(jnp.int32, (length, index_ref.shape[1]), 0)
    return jnp.where(rows == index_ref[...], 1.0, 0.0).astype(bf16)


def row_picks(columns_ref, length):
    rows = columns_ref.shape[0]
    cols = lax.broadcasted_iota(jnp.int32, (rows, length), 1)
    return jnp.where(cols == columns_ref[...], 1.0, 0.0).astype(bf16)


def head_masks(width):
    lanes = lax.shift_right_logical(lax.broadcasted_iota(jnp.int32, (1, width), 1), 6)
    return [jnp.where(lanes == head, 1.0, 0.0).astype(f32) for head in range(width // HEAD_DIM)]


def stack_heads(values, masks):
    return jnp.concatenate([values * mask.astype(values.dtype) for mask in masks], axis=0)


def unstack_heads(values, masks):
    rows = values.shape[0] // len(masks)
    total = values[:rows] * masks[0]
    for head in range(1, len(masks)):
        total = total + values[head * rows : (head + 1) * rows] * masks[head]
    return total


def softmax_rows(scores, axis):
    exponent = jnp.exp(scores - jnp.max(scores, axis=axis, keepdims=True))
    return exponent * (1.0 / jnp.sum(exponent, axis=axis, keepdims=True))


def window_start(block, length):
    start = jnp.clip(block * WINDOW - WINDOW, 0, length - 3 * WINDOW)
    return pl.multiple_of(start, WINDOW)


def attn_forward_kernel(
    ready,
    other_ref,
    columns_ref,
    gain_ref,
    route_query_ref,
    route_key_ref,
    query_index_ref,
    ffn_index_ref,
    own_ref,
    cot_ref,
    hq_ref,
    hk_ref,
    hv_ref,
    ho_ref,
    wq_ref,
    wk_ref,
    wv_ref,
    wo_ref,
    partial_ref,
    input_ref,
    q_ref,
    k_ref,
    v_ref,
    result_ref,
    query_rows_ref,
    key_raw_ref,
    key_rows_ref,
    qh_ref,
    kh_ref,
    vh_ref,
    raw_ref,
    heavy_result_ref,
    token_rows_ref,
    swap_rows_ref,
    ffn_pick_ref,
    pick_ref,
):
    ready(5)
    side = lax.axis_index("tensor")
    half = own_ref.shape[0]
    length = 2 * half
    tile = 256
    for ref, place in ((other_ref, 1 - side), (own_ref, side)):
        if ref is own_ref:
            ready(6)
        for start in range(0, half, tile):
            values = ref[start : start + tile, :].astype(f32)
            normed = values * row_factor(values) * row_of(gain_ref)
            rows = pl.ds(pl.multiple_of(place * half + start, tile), tile)
            input_ref[rows, :] = normed.astype(bf16)
    routed = query_index_ref.shape[1]
    pick_ref[...] = picks(query_index_ref, length)
    ffn_pick_ref[...] = picks(ffn_index_ref, length)
    picker = row_picks(columns_ref, length)
    picked = mm(picker[: 2 * routed], input_ref[...])
    own_pick = ffn_pick_ref[pl.ds(pl.multiple_of(side * half, half), half), :]
    other_pick = ffn_pick_ref[pl.ds(pl.multiple_of((1 - side) * half, half), half), :]
    token_rows = mm(own_pick, own_ref[...], 0, 0) + mm(other_pick, other_ref[...], 0, 0)
    token_rows_ref[...] = token_rows.astype(bf16)
    query_rows = picked[:routed]
    key_raw = picked[routed:]
    query_score = sigmoid(jnp.sum(query_rows * row_of(route_query_ref), axis=-1, keepdims=True))
    key_score = sigmoid(jnp.sum(key_raw * row_of(route_key_ref), axis=-1, keepdims=True))
    query_rows_ref[...] = query_rows.astype(bf16)
    key_raw_ref[...] = key_raw.astype(bf16)
    key_rows_ref[...] = (key_score * key_raw).astype(bf16)
    ready(11)
    swap_rows_ref[routed:, :] = mm(own_pick, cot_ref[...], 0, 0).astype(bf16)
    qh_ref[...] = mm(query_rows_ref[...], hq_ref[...]).astype(bf16)
    kh_ref[...] = mm(key_rows_ref[...], hk_ref[...]).astype(bf16)
    vh_ref[...] = mm(key_rows_ref[...], hv_ref[...]).astype(bf16)
    pair = 2 * HEAD_DIM
    pair_masks = head_masks(pair)
    for start in range(0, qh_ref.shape[1], pair):
        cols = slice(start, start + pair)
        stacked = stack_heads(qh_ref[:, cols] * (HEAD_DIM**-0.5), pair_masks)
        probs = softmax_rows(mm(stacked, kh_ref[:, cols], 1, 1), -1)
        raw_ref[:, cols] = unstack_heads(mm(probs.astype(bf16), vh_ref[:, cols]), pair_masks)
    heavy_result_ref[...] = (query_score * raw_ref[...]).astype(bf16)
    high, low = split_low(mm(heavy_result_ref[...], ho_ref[...]))

    ready(15)
    for start in range(0, length, tile):
        rows = slice(start, start + tile)
        q_ref[rows, :] = mm(input_ref[rows, :], wq_ref[...]).astype(bf16)
        k_ref[rows, :] = mm(input_ref[rows, :], wk_ref[...]).astype(bf16)
        v_ref[rows, :] = mm(input_ref[rows, :], wv_ref[...]).astype(bf16)

    masks = head_masks(q_ref.shape[1])
    heads = len(masks)
    gap = lax.broadcasted_iota(jnp.int32, (WINDOW, 3 * WINDOW), 0) - lax.broadcasted_iota(
        jnp.int32, (WINDOW, 3 * WINDOW), 1
    )

    def one_block(block, carry):
        rows = pl.ds(pl.multiple_of(block * WINDOW, WINDOW), WINDOW)
        start = window_start(block, length)
        keys = pl.ds(start, 3 * WINDOW)
        stacked = stack_heads(q_ref[rows, :] * (HEAD_DIM**-0.5), masks)
        scores = mm(stacked, k_ref[keys, :], 1, 1)
        near = jnp.abs(gap + (block * WINDOW - start)) < WINDOW
        bias = jnp.where(near, 0.0, -1e30)
        probs = softmax_rows(scores + jnp.concatenate([bias] * heads, axis=0), -1)
        out = unstack_heads(mm(probs.astype(bf16), v_ref[keys, :]), masks)
        result_ref[rows, :] = out.astype(bf16)
        return carry

    lax.fori_loop(0, length // WINDOW, one_block, 0, unroll=4)
    spread = jnp.concatenate([high, low], axis=0)
    for start in range(0, length, tile):
        rows = slice(start, start + tile)
        pick = jnp.concatenate([pick_ref[rows, :]] * 2, axis=1)
        partial_ref[rows, :] = (mm(result_ref[rows, :], wo_ref[...]) + mm(pick, spread)).astype(bf16)
    swap_rows_ref[:routed, :] = mm(picker[2 * routed :], partial_ref[...]).astype(bf16)


def gelu_parts(values):
    density = jnp.exp(-0.5 * values * values) * 0.3989422804014327
    below = 0.5 * (1.0 + lax.erf(values * 0.7071067811865476))
    return values * below, below + values * density


def ffn_heavy_kernel(
    ready,
    hg_ref,
    hu_ref,
    hd_ref,
    token_rows_ref,
    mine_ref,
    got_ref,
    gain_ref,
    route_ref,
    send_x_ref,
    send_y_ref,
    send_z_ref,
    rows_back_ref,
    route_grad_ref,
):
    routed, model = token_rows_ref.shape
    rows = slice(0, routed)
    middle = token_rows_ref[...].astype(f32) + (
        mine_ref[rows, :].astype(f32) + got_ref[rows, :].astype(f32)
    )
    cot_rows = mine_ref[routed:, :] + got_ref[routed:, :]
    ready(2)
    rows_low = (middle * row_factor(middle) * row_of(gain_ref)).astype(bf16)
    ffn_rows = rows_low.astype(f32)
    send_x_ref[:, :model] = rows_low
    send_y_ref[:, :model] = rows_low
    send_z_ref[:, :model] = cot_rows
    score = sigmoid(jnp.sum(ffn_rows * row_of(route_ref), axis=-1, keepdims=True))
    chunk = 512
    score_grad = 0.0
    for start in range(0, hg_ref.shape[1], chunk):
        cols = slice(start, start + chunk)
        out_cols = slice(model + start, model + start + chunk)
        gate = mm(rows_low, hg_ref[:, cols])
        up = mm(rows_low, hu_ref[:, cols])
        act_grad = mm(cot_rows, hd_ref[cols, :], 1, 1)
        gelu, slope = gelu_parts(gate)
        mixed = gelu * up
        score_grad = score_grad + jnp.sum(act_grad * mixed, axis=-1, keepdims=True)
        scaled = score * act_grad
        send_x_ref[:, out_cols] = (scaled * up * slope).astype(bf16)
        send_y_ref[:, out_cols] = (scaled * gelu).astype(bf16)
        send_z_ref[:, out_cols] = (score * mixed).astype(bf16)
    logit_grad = score * (1.0 - score) * score_grad
    route_grad_ref[...] = jnp.sum(ffn_rows * logit_grad, axis=0, keepdims=True)
    rows_back_ref[...] = logit_grad * row_of(route_ref)


def ffn_light_kernel(
    ready,
    other_ref,
    mine_ref,
    got_ref,
    cot_other_ref,
    pick_ref,
    rows_back_ref,
    gate_grad_ref,
    up_grad_ref,
    act_heavy_ref,
    hg_ref,
    hu_ref,
    hd_ref,
    wg_ref,
    wu_ref,
    wd_ref,
    gain_ref,
    own_ref,
    cot_own_ref,
    back_ref,
    block_own_ref,
    block_send_ref,
    middle_ref,
    *rest,
):
    lane_refs = rest[:-5]
    light_grad_ref, act_ref, mix_ref, input_ref, cot_ref = rest[-5:]
    side = lax.axis_index("tensor")
    half = block_own_ref.shape[0]
    tile = 256
    ready(1)
    for ref, cot, place in ((other_ref, cot_other_ref, 1 - side), (own_ref, cot_own_ref, side)):
        if ref is own_ref:
            ready(3)
        for start in range(0, half, tile):
            rows = pl.ds(pl.multiple_of(place * half + start, tile), tile)
            branch = mine_ref[rows, :].astype(f32) + got_ref[rows, :].astype(f32)
            middle = ref[start : start + tile, :].astype(f32) + branch
            middle_ref[rows, :] = middle
            input_ref[rows, :] = (middle * row_factor(middle) * row_of(gain_ref)).astype(bf16)
            cot_ref[rows, :] = cot[start : start + tile, :]
    model = input_ref.shape[1]
    down_high, down_low = split_low(mm(act_heavy_ref[:, model:], hd_ref[...]))
    down = jnp.concatenate([down_high, down_low], axis=0)
    rows_back = (
        rows_back_ref[...]
        + mm(gate_grad_ref[:, model:], hg_ref[...], 1, 1)
        + mm(up_grad_ref[:, model:], hu_ref[...], 1, 1)
    )
    rows_back = jnp.concatenate(split_low(rows_back), axis=0)
    width = wg_ref.shape[1]
    for first in range(0, 2):
        place = side if first == 0 else 1 - side
        for start in range(0, half, tile):
            rows = pl.ds(pl.multiple_of(place * half + start, tile), tile)
            piece = slice(start, start + tile)
            gate = mm(input_ref[rows, :], wg_ref[...])
            up = mm(input_ref[rows, :], wu_ref[...])
            act_grad = mm(cot_ref[rows, :], wd_ref[...], 1, 1)
            gelu, slope = gelu_parts(gate)
            act_ref[rows, :] = (gelu * up).astype(bf16)
            mix_ref[rows, :width] = (act_grad * up * slope).astype(bf16)
            mix_ref[rows, width:] = (act_grad * gelu).astype(bf16)
            pick = jnp.concatenate([pick_ref[rows, :]] * 2, axis=1)
            branch = mm(act_ref[rows, :], wd_ref[...]) + mm(pick, down)
            if first == 0:
                block_own_ref[piece, :] = middle_ref[rows, :] + branch
            else:
                block_send_ref[piece, :] = branch.astype(bf16)
            back_ref[rows, :] = (
                mm(mix_ref[rows, :width], wg_ref[...], 1, 1)
                + mm(mix_ref[rows, width:], wu_ref[...], 1, 1)
                + mm(pick, rows_back)
            ).astype(bf16)
    light_grad_ref[:, : 2 * width] = mm(input_ref[...], mix_ref[...], 0, 0).astype(bf16)
    light_grad_ref[:, 2 * width :] = mm(cot_ref[...], act_ref[...], 0, 0).astype(bf16)
    for lane in range(len(lane_refs) // 2):
        lane_split(lane, lane_refs, 0, light_grad_ref, lane * width, (lane + 1) * width)


def lane_split(lane, lane_refs, left, grad_ref, first, last):
    bit = LANES[lane][0]
    mine = my_bit(bit)
    block = grad_ref.shape[0] // PARTS
    keep_ref, send_ref = lane_refs[lane], lane_refs[len(lane_refs) // 2 + lane]
    for p in range(PARTS // 2):
        rows = slice(p * block, (p + 1) * block)
        cols = slice(left, left + last - first)
        for ref, value in ((keep_ref, mine), (send_ref, 1 - mine)):
            ref[rows, cols] = grad_ref[block_rows(insert(p, bit, value), block), first:last]


def attn_backward_kernel(
    ready,
    cot_other_ref,
    middle_ref,
    mine_ref,
    got_ref,
    result_ref,
    query_rows_ref,
    key_raw_ref,
    key_rows_ref,
    qh_ref,
    kh_ref,
    vh_ref,
    raw_ref,
    heavy_result_ref,
    gain_ffn_ref,
    route_query_ref,
    route_key_ref,
    query_index_ref,
    key_index_ref,
    cot_own_ref,
    wo_ref,
    ho_ref,
    hq_ref,
    hk_ref,
    hv_ref,
    own_middle_ref,
    out_ref,
    grad_ref,
    back_high_ref,
    back_low_ref,
    pick_ref,
    small_ref,
    low_ref,
):
    ready(5)
    side = lax.axis_index("tensor")
    half = cot_own_ref.shape[0]
    length = 2 * half
    tile = 256
    scale = HEAD_DIM**-0.5
    heavy = qh_ref.shape[1]
    light = result_ref.shape[1]
    gain_ffn_grad = 0.0
    for cot, place, owned in ((cot_other_ref, 1 - side, False), (cot_own_ref, side, True)):
        if owned:
            ready(6)
        for start in range(0, half, tile):
            rows = pl.ds(pl.multiple_of(place * half + start, tile), tile)
            piece = slice(start, start + tile)
            normed_grad = mine_ref[rows, :].astype(f32) + got_ref[rows, :].astype(f32)
            middle = middle_ref[rows, :]
            factor = row_factor(middle)
            scaled = factor * middle
            gain_ffn_grad = gain_ffn_grad + jnp.sum(scaled * normed_grad, axis=0, keepdims=True)
            gained = row_of(gain_ffn_ref) * normed_grad
            inner = jnp.mean(scaled * gained, axis=-1, keepdims=True)
            grad = cot[piece, :].astype(f32) + factor * (gained - scaled * inner)
            if owned:
                own_middle_ref[piece, :] = grad
            low_ref[rows, :] = grad.astype(bf16)
    ready(11)
    for start in range(0, length, tile):
        rows = slice(start, start + tile)
        out_ref[rows, :] = mm(low_ref[rows, :], wo_ref[...], 1, 1).astype(bf16)
    grad_ref[:, 4 * heavy :] = mm(low_ref[...], result_ref[...], 0, 0).astype(bf16)

    routed = query_index_ref.shape[1]
    pick_ref[:, :routed] = picks(query_index_ref, length)
    pick_ref[:, routed:] = picks(key_index_ref, length)
    query_rows = query_rows_ref[...].astype(f32)
    key_raw = key_raw_ref[...].astype(f32)
    query_score = sigmoid(jnp.sum(query_rows * row_of(route_query_ref), axis=-1, keepdims=True))
    key_score = sigmoid(jnp.sum(key_raw * row_of(route_key_ref), axis=-1, keepdims=True))
    mid_rows = mm(pick_ref[:, :routed], low_ref[...], 0, 0).astype(bf16)
    grad_ref[:, 3 * heavy : 4 * heavy] = mm(mid_rows, heavy_result_ref[...], 0, 0).astype(bf16)
    heavy_out_grad = mm(mid_rows, ho_ref[...], 1, 1).astype(bf16)
    query_score_grad = jnp.sum(
        heavy_out_grad.astype(f32) * raw_ref[...], axis=-1, keepdims=True
    )
    raw_high, raw_low = split_low(query_score * heavy_out_grad.astype(f32))
    pair = 2 * HEAD_DIM
    pair_masks = head_masks(pair)
    stacked_score = jnp.concatenate([query_score] * 2, axis=0)
    q_parts, k_parts, v_parts = [], [], []
    for start in range(0, heavy, pair):
        cols = slice(start, start + pair)
        stacked = stack_heads(qh_ref[:, cols] * scale, pair_masks)
        probs = softmax_rows(mm(stacked, kh_ref[:, cols], 1, 1), -1)
        grad_stacked = stack_heads(heavy_out_grad[:, cols], pair_masks)
        probs_grad = stacked_score * mm(grad_stacked, vh_ref[:, cols], 1, 1)
        inner = jnp.sum(probs * probs_grad, axis=-1, keepdims=True)
        score_grad = (probs * (probs_grad - inner)).astype(bf16)
        probs_low = probs.astype(bf16)
        q_parts.append(unstack_heads(mm(score_grad, kh_ref[:, cols]) * scale, pair_masks))
        k_parts.append(mm(score_grad, stacked, 0, 0))
        v_parts.append(
            mm(probs_low, stack_heads(raw_high[:, cols], pair_masks), 0, 0)
            + mm(probs_low, stack_heads(raw_low[:, cols], pair_masks), 0, 0)
        )
    query_heavy_grad = jnp.concatenate(q_parts, axis=1).astype(bf16)
    key_heavy_grad = jnp.concatenate(k_parts, axis=1).astype(bf16)
    value_heavy_grad = jnp.concatenate(v_parts, axis=1).astype(bf16)
    grad_ref[:, :heavy] = mm(query_rows_ref[...], query_heavy_grad, 0, 0).astype(bf16)
    grad_ref[:, heavy : 2 * heavy] = mm(key_rows_ref[...], key_heavy_grad, 0, 0).astype(bf16)
    grad_ref[:, 2 * heavy : 3 * heavy] = mm(
        key_rows_ref[...], value_heavy_grad, 0, 0
    ).astype(bf16)
    key_rows_grad = mm(key_heavy_grad, hk_ref[...], 1, 1) + mm(
        value_heavy_grad, hv_ref[...], 1, 1
    )
    key_logit_grad = (
        key_score * (1.0 - key_score) * jnp.sum(key_rows_grad * key_raw, axis=-1, keepdims=True)
    )
    query_logit_grad = query_score * (1.0 - query_score) * query_score_grad
    key_raw_grad = key_score * key_rows_grad + key_logit_grad * row_of(route_key_ref)
    query_rows_grad = mm(query_heavy_grad, hq_ref[...], 1, 1)
    query_rows_grad = query_rows_grad + query_logit_grad * row_of(route_query_ref)
    small_ref[...] = jnp.zeros_like(small_ref)
    small_ref[1:2, :] = 0.5 * gain_ffn_grad
    small_ref[2:3, :] = jnp.sum(query_rows * query_logit_grad, axis=0, keepdims=True)
    small_ref[3:4, :] = jnp.sum(key_raw * key_logit_grad, axis=0, keepdims=True)
    high, low = split_low(jnp.concatenate([query_rows_grad, key_raw_grad], axis=0))
    back_high_ref[...] = high
    back_low_ref[...] = low


def lane_cuts(heavy, light):
    return (
        (0, 2 * heavy, 0, light),
        (2 * heavy, 4 * heavy, 0, 0),
        (4 * heavy, 4 * heavy + light, light, 3 * light),
    )


def light_backward_kernel(
    ready,
    other_ref,
    input_ref,
    q_ref,
    k_ref,
    v_ref,
    out_ref,
    heavy_grad_ref,
    back_high_ref,
    back_low_ref,
    pick_ref,
    own_ref,
    wq_ref,
    wk_ref,
    wv_ref,
    own_back_ref,
    send_ref,
    small_ref,
    *rest,
):
    grad_refs = rest[:-6]
    light_grad_ref, kt_ref, qt_grad_ref, k_grad_ref, v_grad_ref, mixed_ref = rest[-6:]
    side = lax.axis_index("tensor")
    half = own_ref.shape[0]
    length = 2 * half
    tile = 256
    scale = HEAD_DIM**-0.5
    kt_ref[...] = k_ref[...].T
    k_grad_ref[...] = jnp.zeros_like(k_grad_ref)
    v_grad_ref[...] = jnp.zeros_like(v_grad_ref)
    masks = head_masks(q_ref.shape[1])
    heads = len(masks)
    gap = lax.broadcasted_iota(jnp.int32, (3 * WINDOW, WINDOW), 1) - lax.broadcasted_iota(
        jnp.int32, (3 * WINDOW, WINDOW), 0
    )

    def one_block(block, carry):
        first = pl.multiple_of(block * WINDOW, WINDOW)
        rows = pl.ds(first, WINDOW)
        start = window_start(block, length)
        keys = pl.ds(start, 3 * WINDOW)
        stacked = stack_heads(q_ref[rows, :] * scale, masks)
        grad_stacked = stack_heads(out_ref[rows, :], masks)
        near = jnp.abs(gap + (block * WINDOW - start)) < WINDOW
        bias = jnp.where(near, 0.0, -1e30)
        scores = mm(k_ref[keys, :], stacked, 1, 1)
        probs = softmax_rows(scores + jnp.concatenate([bias] * heads, axis=1), 0)
        probs_grad = mm(v_ref[keys, :], grad_stacked, 1, 1)
        inner = jnp.sum(probs * probs_grad, axis=0, keepdims=True)
        score_grad = (probs * (probs_grad - inner)).astype(bf16)
        k_grad_ref[keys, :] += mm(score_grad, stacked)
        v_grad_ref[keys, :] += mm(probs.astype(bf16), grad_stacked)
        spread = mm(kt_ref[:, keys], score_grad) * scale
        for head in range(heads):
            lanes = slice(head * HEAD_DIM, (head + 1) * HEAD_DIM)
            qt_grad_ref[lanes, rows] = spread[lanes, head * WINDOW : (head + 1) * WINDOW]
        return carry

    lax.fori_loop(0, length // WINDOW, one_block, 0, unroll=True)
    light = q_ref.shape[1]
    mixed_ref[:, :light] = qt_grad_ref[...].T.astype(bf16)
    mixed_ref[:, light : 2 * light] = k_grad_ref[...].astype(bf16)
    mixed_ref[:, 2 * light :] = v_grad_ref[...].astype(bf16)
    heavy_cols = heavy_grad_ref.shape[1]
    heavy = (heavy_cols - light) // 4
    light_grad = mm(input_ref[...], mixed_ref[...], 0, 0).astype(bf16)
    ready(4)
    gain_attn_grad = 0.0
    for ref, place, owned in ((own_ref, side, True), (other_ref, 1 - side, False)):
        for start in range(0, half, tile):
            rows = pl.ds(pl.multiple_of(place * half + start, tile), tile)
            piece = slice(start, start + tile)
            pick = pick_ref[rows, :]
            back = (
                mm(mixed_ref[rows, :light], wq_ref[...], 1, 1)
                + mm(mixed_ref[rows, light : 2 * light], wk_ref[...], 1, 1)
                + mm(mixed_ref[rows, 2 * light :], wv_ref[...], 1, 1)
                + (mm(pick, back_high_ref[...]) + mm(pick, back_low_ref[...]))
            )
            values = ref[piece, :].astype(f32)
            gain_attn_grad = gain_attn_grad + jnp.sum(
                values * row_factor(values) * back, axis=0, keepdims=True
            )
            if owned:
                own_back_ref[piece, :] = back
            else:
                send_ref[piece, :] = back.astype(bf16)
    small_ref[...] = gain_attn_grad
    if len(grad_refs) == 1:
        grad_refs[0][:, :heavy_cols] = heavy_grad_ref[...]
        grad_refs[0][:, heavy_cols:] = light_grad
        return
    light_grad_ref[...] = light_grad
    for lane, (left, right, first, last) in enumerate(lane_cuts(heavy, light)):
        if right > left:
            lane_split(lane, grad_refs, 0, heavy_grad_ref, left, right)
        if last > first:
            lane_split(lane, grad_refs, right - left, light_grad_ref, first, last)


def join_kernel(lane, send_ref, got_ref, light_ref, next_keep_ref, next_send_ref, full_ref):
    model, heavy = full_ref.shape
    tall = next_send_ref.shape[0]
    light = light_ref.shape[1]
    for wrap in range(light_ref.shape[0] // tall):
        cols = slice(heavy + wrap * light, heavy + (wrap + 1) * light)
        next_send_ref[:, cols] = light_ref[wrap * tall : (wrap + 1) * tall, :]
    left = jnp.concatenate([send_ref[:, :model], got_ref[:, :model]], axis=0)
    right = jnp.concatenate([send_ref[:, model:], got_ref[:, model:]], axis=0)
    full_ref[...] = mm(left, right, 0, 0).astype(bf16)
    first, second = LANES[lane][:2]
    position = second - (1 if first < second else 0)
    mine, next_mine = my_bit(first), my_bit(second)
    block = model // PARTS
    for q in range(PARTS // 4):
        rows = slice(q * block, (q + 1) * block)
        for ref, value in ((next_keep_ref, next_mine), (next_send_ref, 1 - next_mine)):
            p = insert(q, position, value)
            ref[rows, :heavy] = full_ref[block_rows(insert(p, first, mine), block), :]


def pack_small(values, send_ref, left):
    high, low = split_low(values)
    both = jnp.concatenate([high.astype(f32), low.astype(f32)], axis=0).astype(bf16)
    wide = send_ref.shape[1] - left
    for i in range(both.shape[1] // wide):
        send_ref[16 * i : 16 * (i + 1), left:] = both[:, wide * i : wide * (i + 1)]


def unpack_small(got_ref, left, width):
    wide = got_ref.shape[1] - left
    both = jnp.concatenate(
        [got_ref[16 * i : 16 * (i + 1), left:] for i in range(width // wide)], axis=1
    ).astype(f32)
    return both[:8] + both[8:]


def fold_kernel(bit, position, block, pairs, *refs):
    next_keep_ref, next_send_ref = refs[2 * pairs :][-3:-1]
    sum_ref = refs[-1]
    extra = refs[2 * pairs : -3]
    left = 0
    for keep_ref, got_ref in zip(refs[: 2 * pairs : 2], refs[1 : 2 * pairs : 2]):
        rows, width = keep_ref.shape
        tall = min(rows, got_ref.shape[0])
        skip = got_ref.shape[1] - width * (rows // tall) if tall < rows else 0
        for wrap in range(rows // tall):
            piece = slice(wrap * tall, (wrap + 1) * tall)
            got = got_ref[:, skip + wrap * width : skip + (wrap + 1) * width]
            both = keep_ref[piece, :].astype(f32) + got.astype(f32)
            sum_ref[piece, left : left + width] = both.astype(bf16)
        left += width
    mine = my_bit(bit)
    for q in range(next_keep_ref.shape[0] // block):
        rows = slice(q * block, (q + 1) * block)
        next_keep_ref[rows, :] = sum_ref[block_rows(insert(q, position, mine), block), :]
        next_send_ref[rows, :left] = sum_ref[block_rows(insert(q, position, 1 - mine), block), :]
    if extra:
        *parts, small_ref = extra
        small = parts[0][...]
        if len(parts) == 2 and parts[1].dtype == f32:
            small = small + parts[1][...]
        elif len(parts) == 2:
            small = small + unpack_small(parts[1], parts[1].shape[1] - 128, small.shape[1])
        else:
            small = small + unpack_small(refs[1], refs[0].shape[1], small.shape[1])
        small_ref[...] = small
        pack_small(small, next_send_ref, left)


def last_fold_kernel(bit, lanes, *refs):
    extra = refs[2 * lanes : -3]
    keep_ref, send_ref, sum_ref = refs[-3:]
    left = 0
    for lane in range(lanes):
        width = refs[lane].shape[1]
        both = refs[lane][...].astype(f32) + refs[lanes + lane][:, :width].astype(f32)
        sum_ref[:, left : left + width] = both
        left += width
    mine = my_bit(bit)
    block = keep_ref.shape[0]
    keep_ref[...] = sum_ref[block_rows(mine, block), :]
    send_ref[:, :left] = sum_ref[block_rows(1 - mine, block), :].astype(bf16)
    if extra:
        small = extra[0][...]
        small = small + unpack_small(refs[lanes], refs[0].shape[1], small.shape[1])
        extra[1][...] = small
        pack_small(small, send_ref, left)


def final_kernel(widths, keep_ref, got_ref, *refs):
    left = 0
    outs = refs
    if len(refs) > len(widths):
        small_ref, *outs = refs
        total = keep_ref.shape[1]
        small = small_ref[...] + unpack_small(got_ref, total, small_ref.shape[1])
        for i, out_ref in enumerate(outs[len(widths) :]):
            out_ref[...] = small[i]
    for width, out_ref in zip(widths, outs):
        cols = slice(left, left + width)
        out_ref[...] = keep_ref[:, cols] + got_ref[:, cols].astype(f32)
        left += width


def fold(bit, position, block, *pairs, extra=()):
    rows = pairs[0].shape[0]
    width = sum(pair.shape[1] for pair in pairs[::2])
    ride = 128 if extra else 0
    return whole(
        functools.partial(fold_ride if extra else fold_kernel, bit, position, block, len(pairs) // 2),
        "fold",
        2,
        [((rows // 2, width), bf16), ((rows // 2, width + ride), bf16)]
        + [(item.shape, f32) for item in extra[:1]],
        [((rows, width), bf16)],
        *pairs,
        *extra,
    )


def fold_ride(bit, position, block, pairs, *refs):
    keep_ref, send_ref, small_ref, sum_ref = refs[-4:]
    fold_kernel(bit, position, block, pairs, *refs[:-4], small_ref, keep_ref, send_ref, sum_ref)


def last_fold(bit, keeps, gots, extra=()):
    rows = keeps[0].shape[0]
    width = sum(keep.shape[1] for keep in keeps)
    ride = 256 if extra else 0
    return whole(
        functools.partial(last_ride if extra else last_fold_kernel, bit, len(keeps)),
        "last_fold",
        2,
        [((rows // 2, width), f32), ((rows // 2, width + ride), bf16)]
        + [(item.shape, f32) for item in extra[:1]],
        [((rows, width), f32)],
        *keeps,
        *gots,
        *extra,
    )


def last_ride(bit, lanes, *refs):
    keep_ref, send_ref, small_ref, sum_ref = refs[-4:]
    last_fold_kernel(bit, lanes, *refs[:-4], small_ref, keep_ref, send_ref, sum_ref)


def final(widths, keep, got, extra=()):
    return whole(
        functools.partial(final_kernel, widths),
        "final",
        2,
        [((keep.shape[0], width), f32, 0) for width in widths]
        + [((item.shape[1],), f32, 0) for item in extra for _ in range(5)],
        [],
        keep,
        got,
        *extra,
    )


def whole(kernel, name, micros, outs, scratch, *operands, outside=0):
    inside = len(operands) - outside
    spaces = [pltpu.VMEM] * inside + [pltpu.HBM] * outside
    operands = [
        pltpu.with_memory_space_constraint(item, space) for item, space in zip(operands, spaces)
    ]
    shapes = [
        pltpu.VMEM(*out) if len(out) == 2 else jax.ShapeDtypeStruct(*out[:2]) for out in outs
    ]
    stage = [pltpu.VMEM(item.shape, item.dtype) for item in operands[inside:]]
    if outside:
        stage.append(pltpu.SemaphoreType.DMA((outside,)))

    def staged(*refs):
        if not outside:
            return kernel(*refs)
        sources, kept, sems = refs[inside : inside + outside], refs[-1 - outside : -1], refs[-1]
        copies = [
            pltpu.make_async_copy(source, target, sems.at[i])
            for i, (source, target) in enumerate(zip(sources, kept))
        ]
        for copy in copies:
            copy.start()
        waited = [False] * outside

        def ready(count):
            for i in range(count):
                if not waited[i]:
                    copies[i].wait()
                    waited[i] = True

        kernel(ready, *refs[:inside], *kept, *refs[inside + outside : -1 - outside])

    return pl.pallas_call(
        staged,
        name=name,
        out_shape=shapes,
        in_specs=[pl.BlockSpec(memory_space=space) for space in spaces],
        out_specs=[pl.BlockSpec(memory_space=pltpu.VMEM)] * len(outs),
        scratch_shapes=[pltpu.VMEM(shape, dtype) for shape, dtype in scratch] + stage,
        compiler_params=pltpu.CompilerParams(vmem_limit_bytes=VMEM_LIMIT),
        cost_estimate=pl.CostEstimate(
            flops=micros * 10**9, transcendentals=0, bytes_accessed=micros * 10**6
        ),
    )(*operands)


def body(
    tokens,
    cotangent,
    gain_attn,
    gain_ffn,
    route_query,
    route_key,
    route_ffn,
    light_query,
    light_key,
    light_value,
    light_out,
    heavy_query,
    heavy_key,
    heavy_value,
    heavy_out,
    light_gate,
    light_up,
    light_down,
    heavy_gate,
    heavy_up,
    heavy_down,
    query_index,
    key_index,
    ffn_index,
):
    half, width = tokens.shape
    length = 2 * half
    routed = query_index.shape[1]
    light = light_query.shape[1]
    heavy = heavy_query.shape[1]
    light_ff = light_gate.shape[1]
    heavy_ff = heavy_gate.shape[1]
    other_tokens = pair_swap(tokens)
    attn_weights = (
        heavy_query,
        heavy_key,
        heavy_value,
        heavy_out,
        light_query,
        light_key,
        light_value,
        light_out,
    )
    columns = jnp.concatenate([query_index, key_index, ffn_index], axis=1).reshape(-1, 1)
    attn_partial, *saved, token_rows, swap_rows, ffn_pick = whole(
        attn_forward_kernel,
        "attn_forward",
        16,
        [((length, width), bf16)] * 2
        + [((length, light), bf16)] * 4
        + [((routed, width), bf16)] * 3
        + [((routed, heavy), bf16)] * 3
        + [((routed, heavy), f32), ((routed, heavy), bf16)]
        + [((routed, width), bf16), ((2 * routed, width), bf16), ((length, routed), bf16)],
        [((length, routed), bf16)],
        other_tokens,
        columns,
        gain_attn,
        route_query,
        route_key,
        query_index,
        ffn_index,
        tokens,
        cotangent,
        *attn_weights,
        outside=7 + len(attn_weights),
    )
    got_rows = pair_swap(swap_rows)
    other_cotangent = pair_swap(after(got_rows, cotangent))
    partial_got = pair_swap(after(got_rows, attn_partial))
    tuned = lax.axis_size("dp") == PARTS
    *sends, rows_back, route_ffn_grad = whole(
        ffn_heavy_kernel,
        "ffn_heavy",
        12,
        [((routed, width + heavy_ff), bf16)] * 3 + [((routed, width), f32), ((1, width), f32)],
        [],
        heavy_gate,
        heavy_up,
        heavy_down,
        token_rows,
        swap_rows,
        got_rows,
        gain_ffn,
        route_ffn,
        outside=2,
    )
    if tuned:
        gots = [swap_bit(send, order[0]) for send, order in zip(sends, LANES)]
    ffn_back, block_own, block_send, middle, *light_parts = whole(
        ffn_light_kernel,
        "ffn_light",
        12,
        [
            ((length, width), bf16),
            ((half, width), f32),
            ((half, width), bf16),
            ((length, width), f32),
        ]
        + ([((width // 2, light_ff), bf16)] * 6 if tuned else [((width, 3 * light_ff), bf16)]),
        ([((width, 3 * light_ff), bf16)] if tuned else [])
        + [
            ((length, light_ff), bf16),
            ((length, 2 * light_ff), bf16),
            ((length, width), bf16),
            ((length, width), bf16),
        ],
        other_tokens,
        attn_partial,
        partial_got,
        other_cotangent,
        ffn_pick,
        rows_back,
        *sends,
        heavy_gate,
        heavy_up,
        heavy_down,
        light_gate,
        light_up,
        light_down,
        gain_ffn,
        tokens,
        cotangent,
        outside=3,
    )
    if tuned:
        back_got = pair_swap(after(tuple(gots), ffn_back))
        light_keeps = light_parts[:3]
        light_sends = light_parts[3:]
        token = ffn_back
        ffn_keeps, ffn_sends = [], []
        for lane in range(3):
            keep, send = whole(
                functools.partial(join_kernel, lane),
                "join",
                3,
                [((width // 4, heavy_ff), bf16), ((width // 4, heavy_ff + 2 * light_ff), bf16)],
                [((width, heavy_ff), bf16)],
                after(token, sends[lane]),
                gots[lane],
                light_sends[RIDES[lane]],
            )
            token = keep
            ffn_keeps.append(keep)
            ffn_sends.append(send)
        ffn_gots = [swap_bit(send, order[1]) for send, order in zip(ffn_sends, LANES)]
        ffn_back = after(token, ffn_back)
    else:
        back_got = pair_swap(ffn_back)
    attn_input, q_light, k_light, v_light, *routed_saved = saved
    own_middle, out_back, heavy_grad, back_high, back_low, pick, small = whole(
        attn_backward_kernel,
        "attn_backward",
        10,
        [
            ((half, width), f32),
            ((length, light), bf16),
            ((width, 4 * heavy + light), bf16),
            ((2 * routed, width), bf16),
            ((2 * routed, width), bf16),
            ((length, 2 * routed), bf16),
            ((8, width), f32),
        ],
        [((length, width), bf16)],
        other_cotangent,
        middle,
        ffn_back,
        back_got,
        *routed_saved,
        gain_ffn,
        route_query,
        route_key,
        query_index,
        key_index,
        cotangent,
        light_out,
        heavy_out,
        heavy_query,
        heavy_key,
        heavy_value,
        outside=11,
    )
    block = width // lax.axis_size("dp")
    own_back, back_send, gain_attn_grad, *attn_grads = whole(
        light_backward_kernel,
        "light_backward",
        16,
        [((half, width), f32), ((half, width), bf16), ((1, width), f32)]
        + (
            [
                ((width // 2, right - left + last - first), bf16)
                for left, right, first, last in lane_cuts(heavy, light)
            ]
            * 2
            if tuned
            else [((width, 4 * heavy + 4 * light), bf16)]
        ),
        [
            ((width, 3 * light), bf16),
            ((light, length), bf16),
            ((light, length), f32),
            ((length, light), f32),
            ((length, light), f32),
            ((length, 3 * light), bf16),
        ],
        other_tokens,
        attn_input,
        q_light,
        k_light,
        v_light,
        out_back,
        heavy_grad,
        back_high,
        back_low,
        pick,
        tokens,
        light_query,
        light_key,
        light_value,
        outside=4,
    )
    small = small + jnp.pad(route_ffn_grad, ((4, 3), (0, 0)))
    small = small + jnp.pad(gain_attn_grad, ((0, 7), (0, 0)))
    if tuned:
        attn_keeps = attn_grads[:3]

        def middle_stage(orders, stage, token, pairs, extra, rider_lane):
            next_keeps, next_gots = [], []
            for lane, order in enumerate(orders):
                left = sorted(order[stage:])
                keep, send, *small = fold(
                    order[stage],
                    left.index(order[stage]),
                    block,
                    after(token, pairs[lane][0]),
                    *pairs[lane][1:],
                    extra=extra if lane == rider_lane else (),
                )
                if lane == rider_lane:
                    rider = small
                token = keep
                next_keeps.append(keep)
                next_gots.append(swap_bit(send, order[stage]))
            return token, next_keeps, next_gots, rider

        token, ffn_keeps, ffn_gots_next, rider = middle_stage(
            LANES, 2, gain_attn_grad, list(zip(ffn_keeps, ffn_gots)), (small, pair_swap(small)), 1
        )
        block_got = pair_swap(after(token, block_send))
        block_out = (block_own + block_got.astype(f32)).astype(bf16)
        back_got = pair_swap(after(token, back_send))
        input_grad = input_rule(tokens, gain_attn, own_middle, own_back, back_got)
        attn_gots = [
            swap_bit(after((*ffn_gots_next, block_out, input_grad), send), ATTN_LANES[lane][0])
            for lane, send in enumerate(attn_grads[3:])
        ]
        ffn_keep, ffn_send = last_fold(3, [after(token, ffn_keeps[0]), *ffn_keeps[1:]], ffn_gots_next)
        ffn_got = swap_bit(ffn_send, 3)
        token, attn_keeps, attn_gots, rider = middle_stage(
            ATTN_LANES,
            1,
            ffn_keep,
            [
                (attn_keeps[lane], attn_gots[lane], light_keeps[lane], got)
                for lane, got in enumerate(ffn_gots[RIDES.index(i)] for i in range(3))
            ],
            (*rider, ffn_gots_next[1]),
            0,
        )
        hg, hu, hd = final([heavy_ff] * 3, after(token, ffn_keep), ffn_got)
        token, attn_keeps, attn_gots, rider = middle_stage(
            ATTN_LANES, 2, hg, list(zip(attn_keeps, attn_gots)), tuple(rider), 0
        )
        side_keep, side_send = last_fold(2, [after(token, attn_keeps[1])], attn_gots[1:2])
        side_got = swap_bit(side_send, 2)
        attn_keep, attn_send, rider = last_fold(
            3, [after(side_keep, attn_keeps[0]), attn_keeps[2]], attn_gots[::2], extra=tuple(rider)
        )
        attn_got = swap_bit(attn_send, 3)
        hv, ho, lu = final([heavy, heavy, light_ff], side_keep, side_got)
        widths = [heavy, heavy, light, light_ff, light, light, light, light_ff]
        pieces = final(widths, after(hv, attn_keep), attn_got, extra=(rider,))
        hq, hk, lq, lg, lo, lk, lv, ld, *small_summed = pieces
    else:
        small_summed = butterfly_sum(small)
        block_out = (block_own + pair_swap(block_send).astype(f32)).astype(bf16)
        input_grad = input_rule(tokens, gain_attn, own_middle, own_back, pair_swap(back_send))
    if not tuned:
        order = list(range(lax.axis_size("dp").bit_length() - 1))
        hg, hu, hd = (
            halving_sum(mm(send[:, :width], send[:, width:], 0, 0).astype(bf16), order)
            for send in sends
        )
        lg, lu, ld = jnp.split(halving_sum(light_parts[0], order), 3, axis=1)
        attn_sum = halving_sum(attn_grads[0], order)
        cuts = [heavy, 2 * heavy, 3 * heavy, 4 * heavy, 4 * heavy + light]
        cuts += [4 * heavy + 2 * light, 4 * heavy + 3 * light]
        hq, hk, hv, ho, lo, lq, lk, lv = jnp.split(attn_sum, cuts, axis=1)
    return (
        block_out,
        input_grad,
        small_summed[0],
        small_summed[1],
        small_summed[2],
        small_summed[3],
        small_summed[4],
        lq,
        lk,
        lv,
        lo.T,
        hq,
        hk,
        hv,
        ho.T,
        lg,
        lu,
        ld.T,
        hg,
        hu,
        hd.T,
    )


def solution(mesh):
    in_specs = (
        P(("dp", "tensor"), None),
        P(("dp", "tensor"), None),
        P(),
        P(),
        P(),
        P(),
        P(),
        P(None, "tensor"),
        P(None, "tensor"),
        P(None, "tensor"),
        P("tensor", None),
        P(None, "tensor"),
        P(None, "tensor"),
        P(None, "tensor"),
        P("tensor", None),
        P(None, "tensor"),
        P(None, "tensor"),
        P("tensor", None),
        P(None, "tensor"),
        P(None, "tensor"),
        P("tensor", None),
        P("dp", None),
        P("dp", None),
        P("dp", None),
    )
    out_specs = (
        P(("dp", "tensor"), None),
        P(("dp", "tensor"), None),
        P(),
        P(),
        P(),
        P(),
        P(),
        P("dp", "tensor"),
        P("dp", "tensor"),
        P("dp", "tensor"),
        P("tensor", "dp"),
        P("dp", "tensor"),
        P("dp", "tensor"),
        P("dp", "tensor"),
        P("tensor", "dp"),
        P("dp", "tensor"),
        P("dp", "tensor"),
        P("tensor", "dp"),
        P("dp", "tensor"),
        P("dp", "tensor"),
        P("tensor", "dp"),
    )
    return jax.shard_map(body, mesh=mesh, in_specs=in_specs, out_specs=out_specs, check_vma=False)
```

```python
import functools

import jax
import jax.numpy as jnp
from jax import lax
from jax.experimental import pallas as pl
from jax.experimental.pallas import tpu as pltpu
from jax.sharding import PartitionSpec as P

HEAD_DIM = 64
WINDOW = 128
EPS = 1e-06
VMEM_LIMIT = 20 * 1024 * 1024
f32 = jnp.float32
bf16 = jnp.bfloat16


def pair_swap(values):
    return lax.ppermute(values, "tensor", [(0, 1), (1, 0)])


def halving_sum(values, order):
    parts = lax.axis_size("dp")
    place = lax.axis_index("dp")
    bits = list(range(len(order) - 1, -1, -1))
    held = values.reshape((2,) * len(bits) + (values.shape[0] // parts, values.shape[1]))
    held = held.astype(jnp.bfloat16)
    for step, bit in enumerate(order):
        axis = bits.index(bit)
        bits.remove(bit)
        mine = (place >> bit) & 1
        keep = lax.dynamic_index_in_dim(held, mine, axis, keepdims=False)
        send = lax.dynamic_index_in_dim(held, 1 - mine, axis, keepdims=False)
        got = lax.ppermute(send, "dp", [(i, i ^ (1 << bit)) for i in range(parts)])
        held = keep.astype(jnp.float32) + got.astype(jnp.float32)
        if step < len(order) - 1:
            held = held.astype(jnp.bfloat16)
    return held


def butterfly_sum(values):
    parts = lax.axis_size("dp")
    values = values + pair_swap(values)
    for bit in range(parts.bit_length() - 1):
        values = values + lax.ppermute(values, "dp", [(i, i ^ (1 << bit)) for i in range(parts)])
    return values


PARTS = 16
LANES = ((0, 1, 2, 3), (1, 2, 0, 3), (2, 0, 1, 3))
RIDES = (1, 2, 0)
ATTN_LANES = ((0, 1, 2, 3), (1, 0, 3, 2), (2, 0, 1, 3))


def insert(number, bit, value):
    low = number & ((1 << bit) - 1)
    return ((number - low) << 1) | (value << bit) | low


def row_of(ref):
    return ref[...].reshape(1, -1)


def input_rule(tokens, gain, own_middle, own_back, got):
    normed_grad = own_back + got.astype(f32)
    values = tokens.astype(f32)
    factor = row_factor(values)
    scaled = values * factor
    gained = gain * normed_grad
    inner = jnp.mean(scaled * gained, axis=-1, keepdims=True)
    return (own_middle + factor * (gained - scaled * inner)).astype(bf16)


def after(token, values):
    return lax.optimization_barrier((values, token))[0]


def block_rows(index, block):
    return pl.ds(pl.multiple_of(index * block, 16), block)


def swap_bit(values, bit):
    parts = lax.axis_size("dp")
    return lax.ppermute(values, "dp", [(i, i ^ (1 << bit)) for i in range(parts)])


def my_bit(bit):
    return lax.shift_right_logical(lax.axis_index("dp"), bit) & 1


def mm(left, right, left_dim=1, right_dim=0):
    return lax.dot_general(
        left, right, (((left_dim,), (right_dim,)), ((), ())), preferred_element_type=f32
    )


def split_low(values):
    high = values.astype(bf16)
    return high, (values - high.astype(f32)).astype(bf16)


def sigmoid(values):
    return 1.0 / (1.0 + jnp.exp(-values))


def row_factor(values):
    return lax.rsqrt(jnp.mean(values * values, axis=-1, keepdims=True) + EPS)


def picks(index_ref, length):
    rows = lax.broadcasted_iota(jnp.int32, (length, index_ref.shape[1]), 0)
    return jnp.where(rows == index_ref[...], 1.0, 0.0).astype(bf16)


def row_picks(columns_ref, length):
    rows = columns_ref.shape[0]
    cols = lax.broadcasted_iota(jnp.int32, (rows, length), 1)
    return jnp.where(cols == columns_ref[...], 1.0, 0.0).astype(bf16)


def head_masks(width):
    lanes = lax.shift_right_logical(lax.broadcasted_iota(jnp.int32, (1, width), 1), 6)
    return [jnp.where(lanes == head, 1.0, 0.0).astype(f32) for head in range(width // HEAD_DIM)]


def stack_heads(values, masks):
    return jnp.concatenate([values * mask.astype(values.dtype) for mask in masks], axis=0)


def unstack_heads(values, masks):
    rows = values.shape[0] // len(masks)
    total = values[:rows] * masks[0]
    for head in range(1, len(masks)):
        total = total + values[head * rows : (head + 1) * rows] * masks[head]
    return total


def softmax_rows(scores, axis):
    exponent = jnp.exp(scores - jnp.max(scores, axis=axis, keepdims=True))
    return exponent * (1.0 / jnp.sum(exponent, axis=axis, keepdims=True))


def window_start(block, length):
    start = jnp.clip(block * WINDOW - WINDOW, 0, length - 3 * WINDOW)
    return pl.multiple_of(start, WINDOW)


def attn_forward_kernel(
    ready,
    other_ref,
    columns_ref,
    gain_ref,
    route_query_ref,
    route_key_ref,
    query_index_ref,
    ffn_index_ref,
    own_ref,
    cot_ref,
    hq_ref,
    hk_ref,
    hv_ref,
    ho_ref,
    wq_ref,
    wk_ref,
    wv_ref,
    wo_ref,
    partial_ref,
    input_ref,
    q_ref,
    k_ref,
    v_ref,
    result_ref,
    query_rows_ref,
    key_raw_ref,
    key_rows_ref,
    qh_ref,
    kh_ref,
    vh_ref,
    raw_ref,
    heavy_result_ref,
    token_rows_ref,
    swap_rows_ref,
    ffn_pick_ref,
    pick_ref,
):
    ready(5)
    side = lax.axis_index("tensor")
    half = own_ref.shape[0]
    length = 2 * half
    tile = 256
    for ref, place in ((other_ref, 1 - side), (own_ref, side)):
        if ref is own_ref:
            ready(6)
        for start in range(0, half, tile):
            values = ref[start : start + tile, :].astype(f32)
            normed = values * row_factor(values) * row_of(gain_ref)
            rows = pl.ds(pl.multiple_of(place * half + start, tile), tile)
            input_ref[rows, :] = normed.astype(bf16)
    routed = query_index_ref.shape[1]
    pick_ref[...] = picks(query_index_ref, length)
    ffn_pick_ref[...] = picks(ffn_index_ref, length)
    picker = row_picks(columns_ref, length)
    picked = mm(picker[: 2 * routed], input_ref[...])
    own_pick = ffn_pick_ref[pl.ds(pl.multiple_of(side * half, half), half), :]
    other_pick = ffn_pick_ref[pl.ds(pl.multiple_of((1 - side) * half, half), half), :]
    token_rows = mm(own_pick, own_ref[...], 0, 0) + mm(other_pick, other_ref[...], 0, 0)
    token_rows_ref[...] = token_rows.astype(bf16)
    query_rows = picked[:routed]
    key_raw = picked[routed:]
    query_score = sigmoid(jnp.sum(query_rows * row_of(route_query_ref), axis=-1, keepdims=True))
    key_score = sigmoid(jnp.sum(key_raw * row_of(route_key_ref), axis=-1, keepdims=True))
    query_rows_ref[...] = query_rows.astype(bf16)
    key_raw_ref[...] = key_raw.astype(bf16)
    key_rows_ref[...] = (key_score * key_raw).astype(bf16)
    ready(11)
    swap_rows_ref[routed:, :] = mm(own_pick, cot_ref[...], 0, 0).astype(bf16)
    qh_ref[...] = mm(query_rows_ref[...], hq_ref[...]).astype(bf16)
    kh_ref[...] = mm(key_rows_ref[...], hk_ref[...]).astype(bf16)
    vh_ref[...] = mm(key_rows_ref[...], hv_ref[...]).astype(bf16)
    pair = 2 * HEAD_DIM
    pair_masks = head_masks(pair)
    for start in range(0, qh_ref.shape[1], pair):
        cols = slice(start, start + pair)
        stacked = stack_heads(qh_ref[:, cols] * (HEAD_DIM**-0.5), pair_masks)
        probs = softmax_rows(mm(stacked, kh_ref[:, cols], 1, 1), -1)
        raw_ref[:, cols] = unstack_heads(mm(probs.astype(bf16), vh_ref[:, cols]), pair_masks)
    heavy_result_ref[...] = (query_score * raw_ref[...]).astype(bf16)
    high, low = split_low(mm(heavy_result_ref[...], ho_ref[...]))

    ready(15)
    for start in range(0, length, tile):
        rows = slice(start, start + tile)
        q_ref[rows, :] = mm(input_ref[rows, :], wq_ref[...]).astype(bf16)
        k_ref[rows, :] = mm(input_ref[rows, :], wk_ref[...]).astype(bf16)
        v_ref[rows, :] = mm(input_ref[rows, :], wv_ref[...]).astype(bf16)

    masks = head_masks(q_ref.shape[1])
    heads = len(masks)
    gap = lax.broadcasted_iota(jnp.int32, (WINDOW, 3 * WINDOW), 0) - lax.broadcasted_iota(
        jnp.int32, (WINDOW, 3 * WINDOW), 1
    )

    def one_block(block, carry):
        rows = pl.ds(pl.multiple_of(block * WINDOW, WINDOW), WINDOW)
        start = window_start(block, length)
        keys = pl.ds(start, 3 * WINDOW)
        stacked = stack_heads(q_ref[rows, :] * (HEAD_DIM**-0.5), masks)
        scores = mm(stacked, k_ref[keys, :], 1, 1)
        near = jnp.abs(gap + (block * WINDOW - start)) < WINDOW
        bias = jnp.where(near, 0.0, -1e30)
        probs = softmax_rows(scores + jnp.concatenate([bias] * heads, axis=0), -1)
        out = unstack_heads(mm(probs.astype(bf16), v_ref[keys, :]), masks)
        result_ref[rows, :] = out.astype(bf16)
        return carry

    lax.fori_loop(0, length // WINDOW, one_block, 0, unroll=4)
    spread = jnp.concatenate([high, low], axis=0)
    for start in range(0, length, tile):
        rows = slice(start, start + tile)
        pick = jnp.concatenate([pick_ref[rows, :]] * 2, axis=1)
        partial_ref[rows, :] = (mm(result_ref[rows, :], wo_ref[...]) + mm(pick, spread)).astype(bf16)
    swap_rows_ref[:routed, :] = mm(picker[2 * routed :], partial_ref[...]).astype(bf16)


def gelu_parts(values):
    density = jnp.exp(-0.5 * values * values) * 0.3989422804014327
    below = 0.5 * (1.0 + lax.erf(values * 0.7071067811865476))
    return values * below, below + values * density


def ffn_heavy_kernel(
    ready,
    hg_ref,
    hu_ref,
    hd_ref,
    token_rows_ref,
    mine_ref,
    got_ref,
    gain_ref,
    route_ref,
    send_x_ref,
    send_y_ref,
    send_z_ref,
    rows_back_ref,
    route_grad_ref,
):
    routed, model = token_rows_ref.shape
    rows = slice(0, routed)
    middle = token_rows_ref[...].astype(f32) + (
        mine_ref[rows, :].astype(f32) + got_ref[rows, :].astype(f32)
    )
    cot_rows = mine_ref[routed:, :] + got_ref[routed:, :]
    ready(2)
    rows_low = (middle * row_factor(middle) * row_of(gain_ref)).astype(bf16)
    ffn_rows = rows_low.astype(f32)
    send_x_ref[:, :model] = rows_low
    send_y_ref[:, :model] = rows_low
    send_z_ref[:, :model] = cot_rows
    score = sigmoid(jnp.sum(ffn_rows * row_of(route_ref), axis=-1, keepdims=True))
    chunk = 512
    score_grad = 0.0
    for start in range(0, hg_ref.shape[1], chunk):
        cols = slice(start, start + chunk)
        out_cols = slice(model + start, model + start + chunk)
        gate = mm(rows_low, hg_ref[:, cols])
        up = mm(rows_low, hu_ref[:, cols])
        act_grad = mm(cot_rows, hd_ref[cols, :], 1, 1)
        gelu, slope = gelu_parts(gate)
        mixed = gelu * up
        score_grad = score_grad + jnp.sum(act_grad * mixed, axis=-1, keepdims=True)
        scaled = score * act_grad
        send_x_ref[:, out_cols] = (scaled * up * slope).astype(bf16)
        send_y_ref[:, out_cols] = (scaled * gelu).astype(bf16)
        send_z_ref[:, out_cols] = (score * mixed).astype(bf16)
    logit_grad = score * (1.0 - score) * score_grad
    route_grad_ref[...] = jnp.sum(ffn_rows * logit_grad, axis=0, keepdims=True)
    rows_back_ref[...] = logit_grad * row_of(route_ref)


def ffn_light_kernel(
    ready,
    other_ref,
    mine_ref,
    got_ref,
    cot_other_ref,
    pick_ref,
    rows_back_ref,
    gate_grad_ref,
    up_grad_ref,
    act_heavy_ref,
    hg_ref,
    hu_ref,
    hd_ref,
    wg_ref,
    wu_ref,
    wd_ref,
    gain_ref,
    own_ref,
    cot_own_ref,
    back_ref,
    block_own_ref,
    block_send_ref,
    middle_ref,
    *rest,
):
    lane_refs = rest[:-5]
    light_grad_ref, act_ref, mix_ref, input_ref, cot_ref = rest[-5:]
    side = lax.axis_index("tensor")
    half = block_own_ref.shape[0]
    tile = 256
    ready(1)
    for ref, cot, place in ((other_ref, cot_other_ref, 1 - side), (own_ref, cot_own_ref, side)):
        if ref is own_ref:
            ready(3)
        for start in range(0, half, tile):
            rows = pl.ds(pl.multiple_of(place * half + start, tile), tile)
            branch = mine_ref[rows, :].astype(f32) + got_ref[rows, :].astype(f32)
            middle = ref[start : start + tile, :].astype(f32) + branch
            middle_ref[rows, :] = middle
            input_ref[rows, :] = (middle * row_factor(middle) * row_of(gain_ref)).astype(bf16)
            cot_ref[rows, :] = cot[start : start + tile, :]
    model = input_ref.shape[1]
    down_high, down_low = split_low(mm(act_heavy_ref[:, model:], hd_ref[...]))
    down = jnp.concatenate([down_high, down_low], axis=0)
    rows_back = (
        rows_back_ref[...]
        + mm(gate_grad_ref[:, model:], hg_ref[...], 1, 1)
        + mm(up_grad_ref[:, model:], hu_ref[...], 1, 1)
    )
    rows_back = jnp.concatenate(split_low(rows_back), axis=0)
    width = wg_ref.shape[1]
    for first in range(0, 2):
        place = side if first == 0 else 1 - side
        for start in range(0, half, tile):
            rows = pl.ds(pl.multiple_of(place * half + start, tile), tile)
            piece = slice(start, start + tile)
            gate = mm(input_ref[rows, :], wg_ref[...])
            up = mm(input_ref[rows, :], wu_ref[...])
            act_grad = mm(cot_ref[rows, :], wd_ref[...], 1, 1)
            gelu, slope = gelu_parts(gate)
            act_ref[rows, :] = (gelu * up).astype(bf16)
            mix_ref[rows, :width] = (act_grad * up * slope).astype(bf16)
            mix_ref[rows, width:] = (act_grad * gelu).astype(bf16)
            pick = jnp.concatenate([pick_ref[rows, :]] * 2, axis=1)
            branch = mm(act_ref[rows, :], wd_ref[...]) + mm(pick, down)
            if first == 0:
                block_own_ref[piece, :] = middle_ref[rows, :] + branch
            else:
                block_send_ref[piece, :] = branch.astype(bf16)
            back_ref[rows, :] = (
                mm(mix_ref[rows, :width], wg_ref[...], 1, 1)
                + mm(mix_ref[rows, width:], wu_ref[...], 1, 1)
                + mm(pick, rows_back)
            ).astype(bf16)
    light_grad_ref[:, : 2 * width] = mm(input_ref[...], mix_ref[...], 0, 0).astype(bf16)
    light_grad_ref[:, 2 * width :] = mm(cot_ref[...], act_ref[...], 0, 0).astype(bf16)
    for lane in range(len(lane_refs) // 2):
        lane_split(lane, lane_refs, 0, light_grad_ref, lane * width, (lane + 1) * width)


def lane_split(lane, lane_refs, left, grad_ref, first, last):
    bit = LANES[lane][0]
    mine = my_bit(bit)
    block = grad_ref.shape[0] // PARTS
    keep_ref, send_ref = lane_refs[lane], lane_refs[len(lane_refs) // 2 + lane]
    for p in range(PARTS // 2):
        rows = slice(p * block, (p + 1) * block)
        cols = slice(left, left + last - first)
        for ref, value in ((keep_ref, mine), (send_ref, 1 - mine)):
            ref[rows, cols] = grad_ref[block_rows(insert(p, bit, value), block), first:last]


def attn_backward_kernel(
    ready,
    cot_other_ref,
    middle_ref,
    mine_ref,
    got_ref,
    result_ref,
    query_rows_ref,
    key_raw_ref,
    key_rows_ref,
    qh_ref,
    kh_ref,
    vh_ref,
    raw_ref,
    heavy_result_ref,
    gain_ffn_ref,
    route_query_ref,
    route_key_ref,
    query_index_ref,
    key_index_ref,
    cot_own_ref,
    wo_ref,
    ho_ref,
    hq_ref,
    hk_ref,
    hv_ref,
    own_middle_ref,
    out_ref,
    grad_ref,
    back_high_ref,
    back_low_ref,
    pick_ref,
    small_ref,
    low_ref,
):
    ready(5)
    side = lax.axis_index("tensor")
    half = cot_own_ref.shape[0]
    length = 2 * half
    tile = 256
    scale = HEAD_DIM**-0.5
    heavy = qh_ref.shape[1]
    light = result_ref.shape[1]
    gain_ffn_grad = 0.0
    for cot, place, owned in ((cot_other_ref, 1 - side, False), (cot_own_ref, side, True)):
        if owned:
            ready(6)
        for start in range(0, half, tile):
            rows = pl.ds(pl.multiple_of(place * half + start, tile), tile)
            piece = slice(start, start + tile)
            normed_grad = mine_ref[rows, :].astype(f32) + got_ref[rows, :].astype(f32)
            middle = middle_ref[rows, :]
            factor = row_factor(middle)
            scaled = factor * middle
            gain_ffn_grad = gain_ffn_grad + jnp.sum(scaled * normed_grad, axis=0, keepdims=True)
            gained = row_of(gain_ffn_ref) * normed_grad
            inner = jnp.mean(scaled * gained, axis=-1, keepdims=True)
            grad = cot[piece, :].astype(f32) + factor * (gained - scaled * inner)
            if owned:
                own_middle_ref[piece, :] = grad
            low_ref[rows, :] = grad.astype(bf16)
    ready(11)
    for start in range(0, length, tile):
        rows = slice(start, start + tile)
        out_ref[rows, :] = mm(low_ref[rows, :], wo_ref[...], 1, 1).astype(bf16)
    grad_ref[:, 4 * heavy :] = mm(low_ref[...], result_ref[...], 0, 0).astype(bf16)

    routed = query_index_ref.shape[1]
    pick_ref[:, :routed] = picks(query_index_ref, length)
    pick_ref[:, routed:] = picks(key_index_ref, length)
    query_rows = query_rows_ref[...].astype(f32)
    key_raw = key_raw_ref[...].astype(f32)
    query_score = sigmoid(jnp.sum(query_rows * row_of(route_query_ref), axis=-1, keepdims=True))
    key_score = sigmoid(jnp.sum(key_raw * row_of(route_key_ref), axis=-1, keepdims=True))
    mid_rows = mm(pick_ref[:, :routed], low_ref[...], 0, 0).astype(bf16)
    grad_ref[:, 3 * heavy : 4 * heavy] = mm(mid_rows, heavy_result_ref[...], 0, 0).astype(bf16)
    heavy_out_grad = mm(mid_rows, ho_ref[...], 1, 1).astype(bf16)
    query_score_grad = jnp.sum(
        heavy_out_grad.astype(f32) * raw_ref[...], axis=-1, keepdims=True
    )
    raw_high, raw_low = split_low(query_score * heavy_out_grad.astype(f32))
    pair = 2 * HEAD_DIM
    pair_masks = head_masks(pair)
    stacked_score = jnp.concatenate([query_score] * 2, axis=0)
    q_parts, k_parts, v_parts = [], [], []
    for start in range(0, heavy, pair):
        cols = slice(start, start + pair)
        stacked = stack_heads(qh_ref[:, cols] * scale, pair_masks)
        probs = softmax_rows(mm(stacked, kh_ref[:, cols], 1, 1), -1)
        grad_stacked = stack_heads(heavy_out_grad[:, cols], pair_masks)
        probs_grad = stacked_score * mm(grad_stacked, vh_ref[:, cols], 1, 1)
        inner = jnp.sum(probs * probs_grad, axis=-1, keepdims=True)
        score_grad = (probs * (probs_grad - inner)).astype(bf16)
        probs_low = probs.astype(bf16)
        q_parts.append(unstack_heads(mm(score_grad, kh_ref[:, cols]) * scale, pair_masks))
        k_parts.append(mm(score_grad, stacked, 0, 0))
        v_parts.append(
            mm(probs_low, stack_heads(raw_high[:, cols], pair_masks), 0, 0)
            + mm(probs_low, stack_heads(raw_low[:, cols], pair_masks), 0, 0)
        )
    query_heavy_grad = jnp.concatenate(q_parts, axis=1).astype(bf16)
    key_heavy_grad = jnp.concatenate(k_parts, axis=1).astype(bf16)
    value_heavy_grad = jnp.concatenate(v_parts, axis=1).astype(bf16)
    grad_ref[:, :heavy] = mm(query_rows_ref[...], query_heavy_grad, 0, 0).astype(bf16)
    grad_ref[:, heavy : 2 * heavy] = mm(key_rows_ref[...], key_heavy_grad, 0, 0).astype(bf16)
    grad_ref[:, 2 * heavy : 3 * heavy] = mm(
        key_rows_ref[...], value_heavy_grad, 0, 0
    ).astype(bf16)
    key_rows_grad = mm(key_heavy_grad, hk_ref[...], 1, 1) + mm(
        value_heavy_grad, hv_ref[...], 1, 1
    )
    key_logit_grad = (
        key_score * (1.0 - key_score) * jnp.sum(key_rows_grad * key_raw, axis=-1, keepdims=True)
    )
    query_logit_grad = query_score * (1.0 - query_score) * query_score_grad
    key_raw_grad = key_score * key_rows_grad + key_logit_grad * row_of(route_key_ref)
    query_rows_grad = mm(query_heavy_grad, hq_ref[...], 1, 1)
    query_rows_grad = query_rows_grad + query_logit_grad * row_of(route_query_ref)
    small_ref[...] = jnp.zeros_like(small_ref)
    small_ref[1:2, :] = 0.5 * gain_ffn_grad
    small_ref[2:3, :] = jnp.sum(query_rows * query_logit_grad, axis=0, keepdims=True)
    small_ref[3:4, :] = jnp.sum(key_raw * key_logit_grad, axis=0, keepdims=True)
    high, low = split_low(jnp.concatenate([query_rows_grad, key_raw_grad], axis=0))
    back_high_ref[...] = high
    back_low_ref[...] = low


def lane_cuts(heavy, light):
    return (
        (0, 2 * heavy, 0, light),
        (2 * heavy, 4 * heavy, 0, 0),
        (4 * heavy, 4 * heavy + light, light, 3 * light),
    )


def light_backward_kernel(
    ready,
    other_ref,
    input_ref,
    q_ref,
    k_ref,
    v_ref,
    out_ref,
    heavy_grad_ref,
    back_high_ref,
    back_low_ref,
    pick_ref,
    own_ref,
    wq_ref,
    wk_ref,
    wv_ref,
    own_back_ref,
    send_ref,
    small_ref,
    *rest,
):
    grad_refs = rest[:-6]
    light_grad_ref, kt_ref, qt_grad_ref, k_grad_ref, v_grad_ref, mixed_ref = rest[-6:]
    side = lax.axis_index("tensor")
    half = own_ref.shape[0]
    length = 2 * half
    tile = 256
    scale = HEAD_DIM**-0.5
    kt_ref[...] = k_ref[...].T
    k_grad_ref[...] = jnp.zeros_like(k_grad_ref)
    v_grad_ref[...] = jnp.zeros_like(v_grad_ref)
    masks = head_masks(q_ref.shape[1])
    heads = len(masks)
    gap = lax.broadcasted_iota(jnp.int32, (3 * WINDOW, WINDOW), 1) - lax.broadcasted_iota(
        jnp.int32, (3 * WINDOW, WINDOW), 0
    )

    def one_block(block, carry):
        first = pl.multiple_of(block * WINDOW, WINDOW)
        rows = pl.ds(first, WINDOW)
        start = window_start(block, length)
        keys = pl.ds(start, 3 * WINDOW)
        stacked = stack_heads(q_ref[rows, :] * scale, masks)
        grad_stacked = stack_heads(out_ref[rows, :], masks)
        near = jnp.abs(gap + (block * WINDOW - start)) < WINDOW
        bias = jnp.where(near, 0.0, -1e30)
        scores = mm(k_ref[keys, :], stacked, 1, 1)
        probs = softmax_rows(scores + jnp.concatenate([bias] * heads, axis=1), 0)
        probs_grad = mm(v_ref[keys, :], grad_stacked, 1, 1)
        inner = jnp.sum(probs * probs_grad, axis=0, keepdims=True)
        score_grad = (probs * (probs_grad - inner)).astype(bf16)
        k_grad_ref[keys, :] += mm(score_grad, stacked)
        v_grad_ref[keys, :] += mm(probs.astype(bf16), grad_stacked)
        spread = mm(kt_ref[:, keys], score_grad) * scale
        for head in range(heads):
            lanes = slice(head * HEAD_DIM, (head + 1) * HEAD_DIM)
            qt_grad_ref[lanes, rows] = spread[lanes, head * WINDOW : (head + 1) * WINDOW]
        return carry

    lax.fori_loop(0, length // WINDOW, one_block, 0, unroll=True)
    light = q_ref.shape[1]
    mixed_ref[:, :light] = qt_grad_ref[...].T.astype(bf16)
    mixed_ref[:, light : 2 * light] = k_grad_ref[...].astype(bf16)
    mixed_ref[:, 2 * light :] = v_grad_ref[...].astype(bf16)
    heavy_cols = heavy_grad_ref.shape[1]
    heavy = (heavy_cols - light) // 4
    light_grad = mm(input_ref[...], mixed_ref[...], 0, 0).astype(bf16)
    ready(4)
    gain_attn_grad = 0.0
    for ref, place, owned in ((own_ref, side, True), (other_ref, 1 - side, False)):
        for start in range(0, half, tile):
            rows = pl.ds(pl.multiple_of(place * half + start, tile), tile)
            piece = slice(start, start + tile)
            pick = pick_ref[rows, :]
            back = (
                mm(mixed_ref[rows, :light], wq_ref[...], 1, 1)
                + mm(mixed_ref[rows, light : 2 * light], wk_ref[...], 1, 1)
                + mm(mixed_ref[rows, 2 * light :], wv_ref[...], 1, 1)
                + (mm(pick, back_high_ref[...]) + mm(pick, back_low_ref[...]))
            )
            values = ref[piece, :].astype(f32)
            gain_attn_grad = gain_attn_grad + jnp.sum(
                values * row_factor(values) * back, axis=0, keepdims=True
            )
            if owned:
                own_back_ref[piece, :] = back
            else:
                send_ref[piece, :] = back.astype(bf16)
    small_ref[...] = gain_attn_grad
    if len(grad_refs) == 1:
        grad_refs[0][:, :heavy_cols] = heavy_grad_ref[...]
        grad_refs[0][:, heavy_cols:] = light_grad
        return
    light_grad_ref[...] = light_grad
    for lane, (left, right, first, last) in enumerate(lane_cuts(heavy, light)):
        if right > left:
            lane_split(lane, grad_refs, 0, heavy_grad_ref, left, right)
        if last > first:
            lane_split(lane, grad_refs, right - left, light_grad_ref, first, last)


def join_kernel(lane, send_ref, got_ref, light_ref, next_keep_ref, next_send_ref, full_ref):
    model, heavy = full_ref.shape
    tall = next_send_ref.shape[0]
    light = light_ref.shape[1]
    for wrap in range(light_ref.shape[0] // tall):
        cols = slice(heavy + wrap * light, heavy + (wrap + 1) * light)
        next_send_ref[:, cols] = light_ref[wrap * tall : (wrap + 1) * tall, :]
    left = jnp.concatenate([send_ref[:, :model], got_ref[:, :model]], axis=0)
    right = jnp.concatenate([send_ref[:, model:], got_ref[:, model:]], axis=0)
    full_ref[...] = mm(left, right, 0, 0).astype(bf16)
    first, second = LANES[lane][:2]
    position = second - (1 if first < second else 0)
    mine, next_mine = my_bit(first), my_bit(second)
    block = model // PARTS
    for q in range(PARTS // 4):
        rows = slice(q * block, (q + 1) * block)
        for ref, value in ((next_keep_ref, next_mine), (next_send_ref, 1 - next_mine)):
            p = insert(q, position, value)
            ref[rows, :heavy] = full_ref[block_rows(insert(p, first, mine), block), :]


def pack_small(values, send_ref, left):
    high, low = split_low(values)
    both = jnp.concatenate([high.astype(f32), low.astype(f32)], axis=0).astype(bf16)
    wide = send_ref.shape[1] - left
    for i in range(both.shape[1] // wide):
        send_ref[16 * i : 16 * (i + 1), left:] = both[:, wide * i : wide * (i + 1)]


def unpack_small(got_ref, left, width):
    wide = got_ref.shape[1] - left
    both = jnp.concatenate(
        [got_ref[16 * i : 16 * (i + 1), left:] for i in range(width // wide)], axis=1
    ).astype(f32)
    return both[:8] + both[8:]


def fold_kernel(bit, position, block, pairs, *refs):
    next_keep_ref, next_send_ref = refs[2 * pairs :][-3:-1]
    sum_ref = refs[-1]
    extra = refs[2 * pairs : -3]
    left = 0
    for keep_ref, got_ref in zip(refs[: 2 * pairs : 2], refs[1 : 2 * pairs : 2]):
        rows, width = keep_ref.shape
        tall = min(rows, got_ref.shape[0])
        skip = got_ref.shape[1] - width * (rows // tall) if tall < rows else 0
        for wrap in range(rows // tall):
            piece = slice(wrap * tall, (wrap + 1) * tall)
            got = got_ref[:, skip + wrap * width : skip + (wrap + 1) * width]
            both = keep_ref[piece, :].astype(f32) + got.astype(f32)
            sum_ref[piece, left : left + width] = both.astype(bf16)
        left += width
    mine = my_bit(bit)
    for q in range(next_keep_ref.shape[0] // block):
        rows = slice(q * block, (q + 1) * block)
        next_keep_ref[rows, :] = sum_ref[block_rows(insert(q, position, mine), block), :]
        next_send_ref[rows, :left] = sum_ref[block_rows(insert(q, position, 1 - mine), block), :]
    if extra:
        *parts, small_ref = extra
        small = parts[0][...]
        if len(parts) == 2 and parts[1].dtype == f32:
            small = small + parts[1][...]
        elif len(parts) == 2:
            small = small + unpack_small(parts[1], parts[1].shape[1] - 128, small.shape[1])
        else:
            small = small + unpack_small(refs[1], refs[0].shape[1], small.shape[1])
        small_ref[...] = small
        pack_small(small, next_send_ref, left)


def last_fold_kernel(bit, lanes, *refs):
    extra = refs[2 * lanes : -3]
    keep_ref, send_ref, sum_ref = refs[-3:]
    left = 0
    for lane in range(lanes):
        width = refs[lane].shape[1]
        both = refs[lane][...].astype(f32) + refs[lanes + lane][:, :width].astype(f32)
        sum_ref[:, left : left + width] = both
        left += width
    mine = my_bit(bit)
    block = keep_ref.shape[0]
    keep_ref[...] = sum_ref[block_rows(mine, block), :]
    send_ref[:, :left] = sum_ref[block_rows(1 - mine, block), :].astype(bf16)
    if extra:
        small = extra[0][...]
        small = small + unpack_small(refs[lanes], refs[0].shape[1], small.shape[1])
        extra[1][...] = small
        pack_small(small, send_ref, left)


def final_kernel(widths, keep_ref, got_ref, *refs):
    left = 0
    outs = refs
    if len(refs) > len(widths):
        small_ref, *outs = refs
        total = keep_ref.shape[1]
        small = small_ref[...] + unpack_small(got_ref, total, small_ref.shape[1])
        for i, out_ref in enumerate(outs[len(widths) :]):
            out_ref[...] = small[i]
    for width, out_ref in zip(widths, outs):
        cols = slice(left, left + width)
        out_ref[...] = keep_ref[:, cols] + got_ref[:, cols].astype(f32)
        left += width


def fold(bit, position, block, *pairs, extra=(), micros=2):
    rows = pairs[0].shape[0]
    width = sum(pair.shape[1] for pair in pairs[::2])
    ride = 128 if extra else 0
    return whole(
        functools.partial(fold_ride if extra else fold_kernel, bit, position, block, len(pairs) // 2),
        "fold",
        micros,
        [((rows // 2, width), bf16), ((rows // 2, width + ride), bf16)]
        + [(item.shape, f32) for item in extra[:1]],
        [((rows, width), bf16)],
        *pairs,
        *extra,
    )


def fold_ride(bit, position, block, pairs, *refs):
    keep_ref, send_ref, small_ref, sum_ref = refs[-4:]
    fold_kernel(bit, position, block, pairs, *refs[:-4], small_ref, keep_ref, send_ref, sum_ref)


def last_fold(bit, keeps, gots, extra=()):
    rows = keeps[0].shape[0]
    width = sum(keep.shape[1] for keep in keeps)
    ride = 256 if extra else 0
    return whole(
        functools.partial(last_ride if extra else last_fold_kernel, bit, len(keeps)),
        "last_fold",
        2,
        [((rows // 2, width), f32), ((rows // 2, width + ride), bf16)]
        + [(item.shape, f32) for item in extra[:1]],
        [((rows, width), f32)],
        *keeps,
        *gots,
        *extra,
    )


def last_ride(bit, lanes, *refs):
    keep_ref, send_ref, small_ref, sum_ref = refs[-4:]
    last_fold_kernel(bit, lanes, *refs[:-4], small_ref, keep_ref, send_ref, sum_ref)


def final(widths, keep, got, extra=()):
    return whole(
        functools.partial(final_kernel, widths),
        "final",
        1,
        [((keep.shape[0], width), f32, 0) for width in widths]
        + [((item.shape[1],), f32, 0) for item in extra for _ in range(5)],
        [],
        keep,
        got,
        *extra,
    )


def whole(kernel, name, micros, outs, scratch, *operands, outside=0):
    inside = len(operands) - outside
    spaces = [pltpu.VMEM] * inside + [pltpu.HBM] * outside
    operands = [
        pltpu.with_memory_space_constraint(item, space) for item, space in zip(operands, spaces)
    ]
    shapes = [
        pltpu.VMEM(*out) if len(out) == 2 else jax.ShapeDtypeStruct(*out[:2]) for out in outs
    ]
    stage = [pltpu.VMEM(item.shape, item.dtype) for item in operands[inside:]]
    if outside:
        stage.append(pltpu.SemaphoreType.DMA((outside,)))

    def staged(*refs):
        if not outside:
            return kernel(*refs)
        sources, kept, sems = refs[inside : inside + outside], refs[-1 - outside : -1], refs[-1]
        copies = [
            pltpu.make_async_copy(source, target, sems.at[i])
            for i, (source, target) in enumerate(zip(sources, kept))
        ]
        for copy in copies:
            copy.start()
        waited = [False] * outside

        def ready(count):
            for i in range(count):
                if not waited[i]:
                    copies[i].wait()
                    waited[i] = True

        kernel(ready, *refs[:inside], *kept, *refs[inside + outside : -1 - outside])

    return pl.pallas_call(
        staged,
        name=name,
        out_shape=shapes,
        in_specs=[pl.BlockSpec(memory_space=space) for space in spaces],
        out_specs=[pl.BlockSpec(memory_space=pltpu.VMEM)] * len(outs),
        scratch_shapes=[pltpu.VMEM(shape, dtype) for shape, dtype in scratch] + stage,
        compiler_params=pltpu.CompilerParams(vmem_limit_bytes=VMEM_LIMIT),
        cost_estimate=pl.CostEstimate(
            flops=micros * 10**9, transcendentals=0, bytes_accessed=micros * 10**6
        ),
    )(*operands)


def body(
    tokens,
    cotangent,
    gain_attn,
    gain_ffn,
    route_query,
    route_key,
    route_ffn,
    light_query,
    light_key,
    light_value,
    light_out,
    heavy_query,
    heavy_key,
    heavy_value,
    heavy_out,
    light_gate,
    light_up,
    light_down,
    heavy_gate,
    heavy_up,
    heavy_down,
    query_index,
    key_index,
    ffn_index,
):
    half, width = tokens.shape
    length = 2 * half
    routed = query_index.shape[1]
    light = light_query.shape[1]
    heavy = heavy_query.shape[1]
    light_ff = light_gate.shape[1]
    heavy_ff = heavy_gate.shape[1]
    other_tokens = pair_swap(tokens)
    attn_weights = (
        heavy_query,
        heavy_key,
        heavy_value,
        heavy_out,
        light_query,
        light_key,
        light_value,
        light_out,
    )
    columns = jnp.concatenate([query_index, key_index, ffn_index], axis=1).reshape(-1, 1)
    attn_partial, *saved, token_rows, swap_rows, ffn_pick = whole(
        attn_forward_kernel,
        "attn_forward",
        16,
        [((length, width), bf16)] * 2
        + [((length, light), bf16)] * 4
        + [((routed, width), bf16)] * 3
        + [((routed, heavy), bf16)] * 3
        + [((routed, heavy), f32), ((routed, heavy), bf16)]
        + [((routed, width), bf16), ((2 * routed, width), bf16), ((length, routed), bf16)],
        [((length, routed), bf16)],
        other_tokens,
        columns,
        gain_attn,
        route_query,
        route_key,
        query_index,
        ffn_index,
        tokens,
        cotangent,
        *attn_weights,
        outside=7 + len(attn_weights),
    )
    got_rows = pair_swap(swap_rows)
    other_cotangent = pair_swap(after(got_rows, cotangent))
    partial_got = pair_swap(after(got_rows, attn_partial))
    tuned = lax.axis_size("dp") == PARTS
    *sends, rows_back, route_ffn_grad = whole(
        ffn_heavy_kernel,
        "ffn_heavy",
        12,
        [((routed, width + heavy_ff), bf16)] * 3 + [((routed, width), f32), ((1, width), f32)],
        [],
        heavy_gate,
        heavy_up,
        heavy_down,
        token_rows,
        swap_rows,
        got_rows,
        gain_ffn,
        route_ffn,
        outside=2,
    )
    if tuned:
        gots = [swap_bit(send, order[0]) for send, order in zip(sends, LANES)]
    ffn_back, block_own, block_send, middle, *light_parts = whole(
        ffn_light_kernel,
        "ffn_light",
        12,
        [
            ((length, width), bf16),
            ((half, width), f32),
            ((half, width), bf16),
            ((length, width), f32),
        ]
        + ([((width // 2, light_ff), bf16)] * 6 if tuned else [((width, 3 * light_ff), bf16)]),
        ([((width, 3 * light_ff), bf16)] if tuned else [])
        + [
            ((length, light_ff), bf16),
            ((length, 2 * light_ff), bf16),
            ((length, width), bf16),
            ((length, width), bf16),
        ],
        other_tokens,
        attn_partial,
        partial_got,
        other_cotangent,
        ffn_pick,
        rows_back,
        *sends,
        heavy_gate,
        heavy_up,
        heavy_down,
        light_gate,
        light_up,
        light_down,
        gain_ffn,
        tokens,
        cotangent,
        outside=3,
    )
    if tuned:
        back_got = pair_swap(after(tuple(gots), ffn_back))
        light_keeps = light_parts[:3]
        light_sends = light_parts[3:]
        token = ffn_back
        ffn_keeps, ffn_sends = [], []
        for lane in range(3):
            keep, send = whole(
                functools.partial(join_kernel, lane),
                "join",
                3,
                [((width // 4, heavy_ff), bf16), ((width // 4, heavy_ff + 2 * light_ff), bf16)],
                [((width, heavy_ff), bf16)],
                after(token, sends[lane]),
                gots[lane],
                light_sends[RIDES[lane]],
            )
            token = keep
            ffn_keeps.append(keep)
            ffn_sends.append(send)
        ffn_gots = [swap_bit(send, order[1]) for send, order in zip(ffn_sends, LANES)]
        ffn_back = after(token, ffn_back)
    else:
        back_got = pair_swap(ffn_back)
    attn_input, q_light, k_light, v_light, *routed_saved = saved
    own_middle, out_back, heavy_grad, back_high, back_low, pick, small = whole(
        attn_backward_kernel,
        "attn_backward",
        10,
        [
            ((half, width), f32),
            ((length, light), bf16),
            ((width, 4 * heavy + light), bf16),
            ((2 * routed, width), bf16),
            ((2 * routed, width), bf16),
            ((length, 2 * routed), bf16),
            ((8, width), f32),
        ],
        [((length, width), bf16)],
        other_cotangent,
        middle,
        ffn_back,
        back_got,
        *routed_saved,
        gain_ffn,
        route_query,
        route_key,
        query_index,
        key_index,
        cotangent,
        light_out,
        heavy_out,
        heavy_query,
        heavy_key,
        heavy_value,
        outside=11,
    )
    block = width // lax.axis_size("dp")
    own_back, back_send, gain_attn_grad, *attn_grads = whole(
        light_backward_kernel,
        "light_backward",
        16,
        [((half, width), f32), ((half, width), bf16), ((1, width), f32)]
        + (
            [
                ((width // 2, right - left + last - first), bf16)
                for left, right, first, last in lane_cuts(heavy, light)
            ]
            * 2
            if tuned
            else [((width, 4 * heavy + 4 * light), bf16)]
        ),
        [
            ((width, 3 * light), bf16),
            ((light, length), bf16),
            ((light, length), f32),
            ((length, light), f32),
            ((length, light), f32),
            ((length, 3 * light), bf16),
        ],
        other_tokens,
        attn_input,
        q_light,
        k_light,
        v_light,
        out_back,
        heavy_grad,
        back_high,
        back_low,
        pick,
        tokens,
        light_query,
        light_key,
        light_value,
        outside=4,
    )
    small = small + jnp.pad(route_ffn_grad, ((4, 3), (0, 0)))
    small = small + jnp.pad(gain_attn_grad, ((0, 7), (0, 0)))
    if tuned:
        attn_keeps = attn_grads[:3]

        def middle_stage(orders, stage, token, pairs, extra, rider_lane):
            next_keeps, next_gots = [], []
            for lane, order in enumerate(orders):
                left = sorted(order[stage:])
                keep, send, *small = fold(
                    order[stage],
                    left.index(order[stage]),
                    block,
                    after(token, pairs[lane][0]),
                    *pairs[lane][1:],
                    extra=extra if lane == rider_lane else (),
                    micros=0 if stage == 2 and orders is ATTN_LANES else 2,
                )
                if lane == rider_lane:
                    rider = small
                token = keep
                next_keeps.append(keep)
                next_gots.append(swap_bit(send, order[stage]))
            return token, next_keeps, next_gots, rider

        token, ffn_keeps, ffn_gots_next, rider = middle_stage(
            LANES, 2, gain_attn_grad, list(zip(ffn_keeps, ffn_gots)), (small, pair_swap(small)), 1
        )
        block_got = pair_swap(after(token, block_send))
        block_out = (block_own + block_got.astype(f32)).astype(bf16)
        back_got = pair_swap(after(token, back_send))
        input_grad = input_rule(tokens, gain_attn, own_middle, own_back, back_got)
        attn_gots = [
            swap_bit(after((*ffn_gots_next, block_out, input_grad), send), ATTN_LANES[lane][0])
            for lane, send in enumerate(attn_grads[3:])
        ]
        ffn_keep, ffn_send = last_fold(3, [after(token, ffn_keeps[0]), *ffn_keeps[1:]], ffn_gots_next)
        ffn_got = swap_bit(ffn_send, 3)
        token, attn_keeps, attn_gots, rider = middle_stage(
            ATTN_LANES,
            1,
            ffn_keep,
            [
                (attn_keeps[lane], attn_gots[lane], light_keeps[lane], got)
                for lane, got in enumerate(ffn_gots[RIDES.index(i)] for i in range(3))
            ],
            (*rider, ffn_gots_next[1]),
            0,
        )
        hg, hu, hd = final([heavy_ff] * 3, after(token, ffn_keep), ffn_got)
        token, attn_keeps, attn_gots, rider = middle_stage(
            ATTN_LANES, 2, hg, list(zip(attn_keeps, attn_gots)), tuple(rider), 0
        )
        side_keep, side_send = last_fold(2, [after(token, attn_keeps[1])], attn_gots[1:2])
        side_got = swap_bit(side_send, 2)
        attn_keep, attn_send, rider = last_fold(
            3, [after(side_keep, attn_keeps[0]), attn_keeps[2]], attn_gots[::2], extra=tuple(rider)
        )
        attn_got = swap_bit(attn_send, 3)
        hv, ho, lu = final([heavy, heavy, light_ff], side_keep, side_got)
        widths = [heavy, heavy, light, light_ff, light, light, light, light_ff]
        pieces = final(widths, after(hv, attn_keep), attn_got, extra=(rider,))
        hq, hk, lq, lg, lo, lk, lv, ld, *small_summed = pieces
    else:
        small_summed = butterfly_sum(small)
        block_out = (block_own + pair_swap(block_send).astype(f32)).astype(bf16)
        input_grad = input_rule(tokens, gain_attn, own_middle, own_back, pair_swap(back_send))
    if not tuned:
        order = list(range(lax.axis_size("dp").bit_length() - 1))
        hg, hu, hd = (
            halving_sum(mm(send[:, :width], send[:, width:], 0, 0).astype(bf16), order)
            for send in sends
        )
        lg, lu, ld = jnp.split(halving_sum(light_parts[0], order), 3, axis=1)
        attn_sum = halving_sum(attn_grads[0], order)
        cuts = [heavy, 2 * heavy, 3 * heavy, 4 * heavy, 4 * heavy + light]
        cuts += [4 * heavy + 2 * light, 4 * heavy + 3 * light]
        hq, hk, hv, ho, lo, lq, lk, lv = jnp.split(attn_sum, cuts, axis=1)
    return (
        block_out,
        input_grad,
        small_summed[0],
        small_summed[1],
        small_summed[2],
        small_summed[3],
        small_summed[4],
        lq,
        lk,
        lv,
        lo.T,
        hq,
        hk,
        hv,
        ho.T,
        lg,
        lu,
        ld.T,
        hg,
        hu,
        hd.T,
    )


def solution(mesh):
    in_specs = (
        P(("dp", "tensor"), None),
        P(("dp", "tensor"), None),
        P(),
        P(),
        P(),
        P(),
        P(),
        P(None, "tensor"),
        P(None, "tensor"),
        P(None, "tensor"),
        P("tensor", None),
        P(None, "tensor"),
        P(None, "tensor"),
        P(None, "tensor"),
        P("tensor", None),
        P(None, "tensor"),
        P(None, "tensor"),
        P("tensor", None),
        P(None, "tensor"),
        P(None, "tensor"),
        P("tensor", None),
        P("dp", None),
        P("dp", None),
        P("dp", None),
    )
    out_specs = (
        P(("dp", "tensor"), None),
        P(("dp", "tensor"), None),
        P(),
        P(),
        P(),
        P(),
        P(),
        P("dp", "tensor"),
        P("dp", "tensor"),
        P("dp", "tensor"),
        P("tensor", "dp"),
        P("dp", "tensor"),
        P("dp", "tensor"),
        P("dp", "tensor"),
        P("tensor", "dp"),
        P("dp", "tensor"),
        P("dp", "tensor"),
        P("tensor", "dp"),
        P("dp", "tensor"),
        P("dp", "tensor"),
        P("tensor", "dp"),
    )
    return jax.shard_map(body, mesh=mesh, in_specs=in_specs, out_specs=out_specs, check_vma=False)
```
